32 devices in a mesh: phase: 4 (over y, x), dp: 8 (over z, core).
Axes of the slice: x: 2, y: 2, z: 4, core: 2. Of those that a mesh axis runs over, the one named last changes fastest.
Arguments:
- tap_tokens: bfloat16 [4, 4096, 4096], P('phase', 'dp'), may hold values from -6 to 6
- project_weight: bfloat16 [4, 4096, 256], P('phase'), may hold values from -0.09375 to 0.09375
- expand_four: bfloat16 [256, 4096], replicated, may hold values from -0.375 to 0.375
- expand_two: bfloat16 [256, 1024], replicated, may hold values from -0.375 to 0.375
- shrink_weight: bfloat16 [1024, 256], replicated, may hold values from -0.1875 to 0.1875
- refine_filters: bfloat16 [4, 2, 2304, 256], P(None, None, 'dp'), may hold values from -0.125 to 0.125
- head_matrix: bfloat16 [256, 128], replicated, may hold values from -0.375 to 0.375
- head_vector: float32 [128], replicated, may hold values from -0.5 to 0.5
- tile_slot: int32 [8, 4, 8], replicated, may hold values from 0 to 191, as said below
Outputs:
- scene_depth: float32 [192, 256], P(('phase', 'dp'))
The draws below stay inside these ranges and needn't reach their ends.
Inputs may be any that keep to these rules, and one draw needn't show every extreme that they name: tile_slot[d, s, j] is the slot of tile (d, s, j); it lies among the slots s * 48 to (s + 1) * 48 - 1, and every slot receives at least one tile.
All inputs are finite; a program needn't handle non-finite values.
Results may differ from the reference program's by a relative error of at most 0.015.
Values may be sent and summed in bfloat16 or wider, within the bound.
No kernel may reach another device: no remote copies, remote signals or barrier semaphores. Data moves between devices by JAX's collectives and lax.ppermute only.
A program may use at most 128 MiB of HBM per device.

```python
import jax
import jax.numpy as jnp
from jax import lax

D = 4096
CH = 256
HEAD = 128
G = 32
LEVELS = 4
TILE_ROWS = 8
TILES_DEV = 8
SLOT_DEV = 6
TILE_PIX = 256
CROPS = 4
TOKENS = 4096
SLOTS = 192
N_PHASE = 4
N_DP = 8


def draw_tile_slot(key, part):
    count_tiles = N_DP * TILES_DEV
    count_slots = SLOT_DEV * N_DP
    stacked = []
    for phase_id in range(N_PHASE):
        phase_key = jax.random.fold_in(key, 17 + phase_id)
        order = jax.random.permutation(jax.random.fold_in(phase_key, 1), count_tiles)
        extra = jax.random.randint(jax.random.fold_in(phase_key, 2), (count_tiles,), 0, count_slots)
        slot_ids = jnp.where(order < count_slots, order, extra) + phase_id * count_slots
        stacked.append(slot_ids.reshape(N_DP, TILES_DEV))
    return jnp.stack(stacked, axis=1).astype(jnp.int32)


def shard_levels(rng, shape, cuts, smallest, top_value):
    level = 1.0
    for axis_at, parts in cuts:
        draws = jax.random.uniform(jax.random.fold_in(jax.random.fold_in(rng, 6), axis_at), (parts,), jnp.float32, smallest / len(cuts), top_value / len(cuts))
        level = level * jnp.repeat(jnp.exp(draws), shape[axis_at] // parts).reshape((-1,) + (1,) * (len(shape) - 1 - axis_at))
    return level


def centred(rng, dims, width, reach, pieces=(), held_as=jnp.bfloat16):
    entries = width * jax.random.normal(rng, dims, jnp.float32)
    if pieces:
        entries = entries * shard_levels(rng, dims, pieces, -0.22, 0.18)
    return jnp.clip(entries, -reach, reach).astype(held_as)


def setup_inputs(seed: int = 0) -> dict:
    key_list = jax.random.split(jax.random.key(seed), 10)
    tap_tokens = centred(key_list[0], (LEVELS, TOKENS, D), 1.0, 6.0, ((0, 4), (1, 8)))
    project_weight = centred(key_list[1], (LEVELS, D, CH), D ** -0.5, 0.09375, ((0, 4),))
    expand_four = centred(key_list[2], (CH, 16 * CH), CH ** -0.5, 0.375)
    expand_two = centred(key_list[3], (CH, 4 * CH), CH ** -0.5, 0.375)
    shrink_weight = centred(key_list[4], (4 * CH, CH), (4 * CH) ** -0.5, 0.1875)
    refine_filters = centred(key_list[5], (LEVELS, 2, 9 * CH, CH), (9 * CH) ** -0.5, 0.125, ((2, 8),))
    head_matrix = centred(key_list[6], (CH, HEAD), CH ** -0.5, 0.375)
    head_vector = centred(key_list[7], (HEAD,), HEAD ** -0.5, 0.5, (), jnp.float32)
    tile_slot = draw_tile_slot(jax.random.fold_in(key_list[9], 71), 0)
    return {"tap_tokens": tap_tokens, "project_weight": project_weight, "expand_four": expand_four, "expand_two": expand_two, "shrink_weight": shrink_weight, "refine_filters": refine_filters, "head_matrix": head_matrix, "head_vector": head_vector, "tile_slot": tile_slot}


def expand(feature, matrix, factor):
    height, breadth, channels = feature.shape
    flattened = jnp.dot(feature.reshape(height * breadth, channels), matrix, preferred_element_type=jnp.float32).astype(jnp.bfloat16)
    arranged = flattened.reshape(height, breadth, factor, factor, channels).transpose(0, 2, 1, 3, 4)
    return arranged.reshape(height * factor, breadth * factor, channels)


def shrink(feature, matrix):
    height, breadth, channels = feature.shape
    blocks = feature.reshape(height // 2, 2, breadth // 2, 2, channels).transpose(0, 2, 1, 3, 4)
    blocks = blocks.reshape((height // 2) * (breadth // 2), 4 * channels)
    result = jnp.dot(blocks, matrix, preferred_element_type=jnp.float32).astype(jnp.bfloat16)
    return result.reshape(height // 2, breadth // 2, channels)


def upsample(feature):
    height, breadth, channels = feature.shape
    widened = jnp.broadcast_to(feature[:, None, :, None, :], (height, 2, breadth, 2, channels))
    return widened.reshape(2 * height, 2 * breadth, channels)


def convolve(feature, matrix):
    height, breadth, channels = feature.shape
    padded = jnp.pad(feature, ((1, 1), (1, 1), (0, 0)))
    patches = jnp.concatenate([padded[row_shift:row_shift + height, col_shift:col_shift + breadth] for row_shift in range(3) for col_shift in range(3)], axis=-1)
    result = jnp.dot(patches.reshape(height * breadth, 9 * channels), matrix, preferred_element_type=jnp.float32)
    return result.reshape(height, breadth, channels)


def refine(summed, first_matrix, second_matrix):
    inner_map = convolve(jax.nn.relu(summed).astype(jnp.bfloat16), first_matrix)
    branch = convolve(jax.nn.relu(inner_map).astype(jnp.bfloat16), second_matrix)
    return (summed + branch).astype(jnp.bfloat16)


def reference(tap_tokens, project_weight, expand_four, expand_two, shrink_weight, refine_filters, head_matrix, head_vector, tile_slot):
    def decode_crop(crop_index):
        crop_taps = lax.dynamic_slice_in_dim(tap_tokens, (crop_index * (G * G)).astype(jnp.int32), G * G, 1)
        projected = [jnp.dot(crop_taps[level_id], project_weight[level_id], preferred_element_type=jnp.float32).astype(jnp.bfloat16).reshape(G, G, CH) for level_id in range(LEVELS)]
        inputs = [expand(projected[0], expand_four, 4), expand(projected[1], expand_two, 2), projected[2], shrink(projected[3], shrink_weight)]
        joined_map = refine(inputs[3].astype(jnp.float32), refine_filters[3, 0], refine_filters[3, 1])
        for level_id in (2, 1, 0):
            summed = inputs[level_id].astype(jnp.float32) + upsample(joined_map).astype(jnp.float32)
            joined_map = refine(summed, refine_filters[level_id, 0], refine_filters[level_id, 1])
        hidden = jax.nn.relu(jnp.dot(joined_map.reshape(-1, CH), head_matrix, preferred_element_type=jnp.float32))
        depth_map = jnp.dot(hidden, head_vector, precision=lax.Precision.HIGHEST)
        return depth_map.reshape(4 * G, 4 * G)

    depth_maps = lax.map(decode_crop, jnp.arange(CROPS, dtype=jnp.int32))
    depth_tiles = depth_maps.reshape(CROPS, 2, TILES_DEV, TILE_ROWS, N_PHASE, 4 * G // N_PHASE)
    depth_tiles = depth_tiles.transpose(0, 1, 4, 2, 3, 5).reshape(N_DP * N_PHASE * TILES_DEV, TILE_PIX)
    return jax.ops.segment_sum(depth_tiles, tile_slot.reshape(-1), num_segments=SLOTS)
```

```python
import functools

import jax
import jax.numpy as jnp
from jax import lax
from jax.experimental import pallas as pl
from jax.experimental.pallas import tpu as pltpu
from jax.sharding import PartitionSpec as P

G = 32
TILES_DEV = 8
SLOT_DEV = 6
LEVELS = 4
F32 = jnp.float32
BF16 = jnp.bfloat16
VMEM_LIMIT = 60 * 1024 * 1024


LANES = 128


def take(ref, *at):
    return jnp.concatenate([ref[(i,) + at] for i in range(ref.shape[0])], axis=-1)


def put(ref, value, *at):
    for i in range(ref.shape[0]):
        ref[(i,) + at] = value[..., i * LANES : (i + 1) * LANES]


def dot(lhs, rhs):
    return jnp.dot(lhs, rhs, preferred_element_type=F32)


class Plan:
    def __init__(self, phases, channels):
        self.ch = channels
        self.half = G // 2
        self.block = G // phases
        self.sent = 2 * self.block
        self.rows1 = 3 * G // 4
        self.cols1 = self.block + self.block // 2
        self.cols0 = self.block + 2
        self.conv_cols = 4 * self.block + 4
        self.conv_rows = 4 * self.half + 16

    def sent_start(self, s):
        return jnp.clip(s * self.block - self.block // 2, 0, G - self.sent)

    def start1(self, s):
        return jnp.clip(s * self.block - self.block // 4, 0, G - self.cols1)

    def start0(self, s):
        return jnp.clip(s * self.block - 1, 0, G - self.cols0)


def project_kernel(plan, phases, where, tokens, weight, shrink, *refs):
    outs, acc_lo, acc_hi = refs[:phases], refs[phases], refs[phases + 1]
    step = pl.program_id(0)
    part = dot(tokens[0], weight[0])
    lanes = acc_lo.shape[1]

    @pl.when(step == 0)
    def _():
        acc_lo[...] = part[:, :lanes]
        acc_hi[...] = part[:, lanes:]

    @pl.when(step > 0)
    def _():
        acc_lo[...] += part[:, :lanes]
        acc_hi[...] += part[:, lanes:]

    last = step == pl.num_programs(0) - 1
    phase = where[0]

    def column(start, size, stride):
        where_rows = pl.ds(start, size, stride=stride)
        return jnp.concatenate([acc_lo[where_rows, :], acc_hi[where_rows, :]], axis=1)

    @pl.when(last & (phase < LEVELS - 1))
    def _():
        for k in range(phases):
            start = plan.sent_start(phase ^ k)
            for j in range(plan.sent):
                outs[k][j * plan.half : (j + 1) * plan.half, :] = column(
                    start + j, plan.half, G
                ).astype(BF16)

    @pl.when(last & (phase == LEVELS - 1))
    def _():
        total = jnp.zeros((plan.half * plan.half // 2, plan.ch), F32)
        for a in range(2):
            for b in range(2):
                tall = jnp.concatenate(
                    [column(a * G + 2 * j + b, plan.half // 2, 2 * G) for j in range(G // 2)],
                    axis=0,
                )
                total += dot(
                    tall.astype(BF16), shrink[(2 * a + b) * plan.ch : (2 * a + b + 1) * plan.ch, :]
                )
        for k in range(phases):
            outs[k][: total.shape[0], :] = total.astype(BF16)
            outs[k][total.shape[0] :, :] = jnp.zeros(
                (outs[k].shape[0] - total.shape[0], plan.ch), BF16
            )


def project(plan, phases, where, tokens, weight, shrink):
    rows, depth = tokens.shape[1:]
    block = min(depth, 512)
    pixels = plan.sent * plan.half
    out = jax.ShapeDtypeStruct((pixels, plan.ch), BF16)
    return pl.pallas_call(
        functools.partial(project_kernel, plan, phases),
        grid_spec=pltpu.PrefetchScalarGridSpec(
            num_scalar_prefetch=1,
            grid=(depth // block,),
            in_specs=[
                pl.BlockSpec((1, rows, block), lambda i, w: (0, 0, i)),
                pl.BlockSpec((1, block, plan.ch), lambda i, w: (0, i, 0)),
                pl.BlockSpec(shrink.shape, lambda i, w: (0, 0)),
            ],
            out_specs=[pl.BlockSpec((pixels, plan.ch), lambda i, w: (0, 0))] * phases,
            scratch_shapes=[pltpu.VMEM((rows, plan.ch // 2), F32)] * 2,
        ),
        out_shape=[out] * phases,
        compiler_params=pltpu.CompilerParams(vmem_limit_bytes=VMEM_LIMIT),
        cost_estimate=pl.CostEstimate(
            flops=2 * rows * depth * plan.ch,
            bytes_accessed=2 * depth * (rows + plan.ch),
            transcendentals=0,
        ),
        name="project",
    )(where, tokens, weight, shrink)


def put_shifted(shifted, col, value):
    count, rows, _ = value.shape
    value = jnp.maximum(value, 0.0)
    at = lax.broadcasted_iota(jnp.int32, value.shape, 1)
    above = jnp.where(at == 0, 0.0, pltpu.roll(value, 1, 1))
    below = jnp.where(at == rows - 1, 0.0, pltpu.roll(value, rows - 1, 1))
    for p, moved in enumerate((above, value, below)):
        shifted[p, pl.ds(col + 1, count)] = moved.astype(BF16)


def clear_edges(shifted):
    shape = shifted.shape
    zeros = jnp.zeros((shape[0], 1) + shape[2:], BF16)
    shifted[:, 0:1] = zeros
    shifted[:, shape[1] - 1 : shape[1]] = zeros


def conv_block(shifted, weight, col, count, rows):
    channels = shifted.shape[3]
    start, size = rows
    patches = [
        shifted[p, pl.ds(col + q, count), pl.ds(start, size), :].reshape(count * size, channels)
        for p in range(3)
        for q in range(3)
    ]
    return dot(jnp.concatenate(patches, axis=1), weight[...]).reshape(count, size, -1)


def loop(count, body):
    if count == 1:
        body(0)
    else:
        lax.fori_loop(0, count, lambda i, c: (body(i), c)[1], 0)


def refine(source, weights, first, second, chunk, out_col, out_count, out_chunk, emit):
    cols, rows = first.shape[1] - 2, first.shape[2]
    clear_edges(first)
    clear_edges(second)
    loop(cols // chunk, lambda i: put_shifted(first, i * chunk, source(i * chunk, chunk)))

    def inner(i):
        put_shifted(second, i * chunk, conv_block(first, weights[0], i * chunk, chunk, (0, rows)))

    loop(cols // chunk, inner)

    def outer(i):
        col = out_col + i * out_chunk
        branch = conv_block(second, weights[1], col, out_chunk, (0, rows))
        emit(i * out_chunk, source(col, out_chunk) + branch)

    loop(out_count // out_chunk, outer)


def start_filters(filters, level, weights, sems):
    copies = []
    for m in range(2):
        copy = pltpu.make_async_copy(filters.at[level, m], weights.at[m], sems.at[m])
        copy.start()
        copies.append(copy)
    return copies


def pyramid_kernel(
    plan,
    where,
    mine,
    other,
    expand_four,
    expand_two,
    filters,
    summed0,
    weight3,
    weight2,
    weight1,
    sems,
    out_sem,
    patch,
    map3,
    joined3,
    map2,
    joined2,
    map1,
    joined1,
    map0,
    first3,
    second3,
    first2,
    second2,
    first1,
    second1,
):
    ch = plan.ch
    phase, side = where[0], where[1]
    copies = {}
    for level, weights in ((3, weight3), (2, weight2), (1, weight1)):
        copies[level] = start_filters(filters, level, weights, sems.at[level])

    def load_patches(level):
        k = phase ^ level
        for ref, at in ((mine, side), (other, 1 - side)):
            patch[:, pl.ds(pl.multiple_of(at * plan.half, plan.half), plan.half), :] = (
                ref[k].astype(F32).reshape(plan.sent, plan.half, ch)
            )

    def wait(level):
        for copy in copies[level]:
            copy.wait()

    size3 = G // 2
    quarter = plan.half // 2
    k3 = phase ^ 3
    for ref, at in ((mine, side), (other, 1 - side)):
        map3[:, pl.ds(pl.multiple_of(at * quarter, quarter), quarter), :] = (
            ref[k3, : size3 * quarter, :].astype(F32).reshape(size3, quarter, ch)
        )
    wait(3)

    def keep3(col, value):
        joined3[pl.ds(col, value.shape[0])] = value.astype(BF16).astype(F32)

    refine(
        lambda col, n: map3[pl.ds(col, n)], weight3, first3, second3, size3, 0, size3, size3, keep3
    )

    load_patches(2)
    from3 = plan.sent_start(phase) // 2
    tall = joined3[pl.ds(from3, plan.sent // 2)]
    for b in range(2):
        for a in range(2):
            put(map2, tall, slice(None), b, pl.ds(a, size3, stride=2), slice(None))
    for j in range(plan.sent):
        at = (j // 2, j % 2)
        put(map2, take(map2, *at) + patch[j], *at)
    wait(2)

    def source2(col, n):
        return take(map2, pl.ds(col // 2, n // 2)).reshape(n, G, ch)

    def keep2(col, value):
        joined2[pl.ds(col, value.shape[0])] = value.astype(BF16).astype(F32)

    refine(source2, weight2, first2, second2, plan.block, 0, plan.sent, plan.block, keep2)

    load_patches(1)
    row1 = pl.multiple_of(side * (G - plan.rows1), 8)
    off1 = plan.start1(phase) - plan.sent_start(phase)
    tall = patch[pl.ds(off1, plan.cols1), pl.ds(row1, plan.rows1), :]
    lhs = tall.reshape(plan.cols1 * plan.rows1, ch).astype(BF16)
    below = joined2[pl.ds(off1, plan.cols1), pl.ds(row1, plan.rows1), :]
    for a in range(2):
        for b in range(2):
            n = 2 * a + b
            grown = dot(lhs, expand_two[:, n * ch : (n + 1) * ch])
            put(
                map1,
                grown.reshape(plan.cols1, plan.rows1, ch) + below,
                slice(None),
                b,
                pl.ds(a, plan.rows1, stride=2),
                slice(None),
            )
    wait(1)
    off0 = 2 * (plan.start0(phase) - plan.start1(phase))

    def source1(col, n):
        return take(map1, pl.ds(col // 2, n // 2)).reshape(n, 2 * plan.rows1, ch)

    def keep1(col, value):
        at = pl.ds(col // 2, value.shape[0] // 2)
        value = value.astype(BF16).astype(F32)
        put(joined1, value.reshape(value.shape[0] // 2, 2, 2 * plan.rows1, ch), at)

    refine(
        source1, weight1, first1, second1, plan.block, off0, 2 * plan.cols0, 4, keep1
    )

    load_patches(0)
    off = plan.start0(phase) - plan.sent_start(phase)
    tall = patch[pl.ds(off, plan.cols0), pl.ds(row1, plan.rows1), :]
    lhs = tall.reshape(plan.cols0 * plan.rows1, ch).astype(BF16)
    for a in range(4):
        for b in range(4):
            n = 4 * a + b
            grown = dot(lhs, expand_four[:, n * ch : (n + 1) * ch])
            below = take(
                joined1, slice(None), b // 2, pl.ds(a // 2, plan.rows1, stride=2), slice(None)
            )
            put(
                map0,
                grown.reshape(plan.cols0, plan.rows1, ch) + below,
                slice(None),
                b,
                pl.ds(a, plan.rows1, stride=4),
                slice(None),
            )
    own0 = 4 * (phase * plan.block - plan.start0(phase))
    conv0 = jnp.clip(own0 - 2, 0, 4 * plan.cols0 - plan.conv_cols) // 2
    out = pltpu.make_async_copy(
        map0.reshape(ch // LANES, 2 * plan.cols0, 2, 4 * plan.rows1, LANES).at[
            :,
            pl.ds(conv0, plan.conv_cols // 2),
            :,
            pl.ds(pl.multiple_of(side * 16, 16), plan.conv_rows),
            :,
        ],
        summed0,
        out_sem,
    )
    out.start()
    out.wait()


def pyramid(plan, where, mine, other, expand_four, expand_two, filters):
    ch = plan.ch
    depth = filters.shape[2]
    vmem = pl.BlockSpec(memory_space=pltpu.VMEM)
    any_space = pl.BlockSpec(memory_space=pl.ANY)
    weights = pltpu.VMEM((2, depth, ch), BF16)
    size3 = G // 2
    slabs = ch // LANES

    def maps(cols, rows):
        return [pltpu.VMEM((3, cols + 2, rows, ch), BF16)] * 2

    return pl.pallas_call(
        functools.partial(pyramid_kernel, plan),
        out_shape=jax.ShapeDtypeStruct(
            (ch // LANES, plan.conv_cols // 2, 2, plan.conv_rows, LANES), F32
        ),
        in_specs=[pl.BlockSpec(memory_space=pltpu.SMEM), vmem, vmem, vmem, vmem, any_space],
        out_specs=any_space,
        scratch_shapes=[
            weights,
            weights,
            weights,
            pltpu.SemaphoreType.DMA((LEVELS, 2)),
            pltpu.SemaphoreType.DMA,
            pltpu.VMEM((plan.sent, G, ch), F32),
            pltpu.VMEM((size3, size3, ch), F32),
            pltpu.VMEM((size3, size3, ch), F32),
            pltpu.VMEM((slabs, plan.sent // 2, 2, G, LANES), F32),
            pltpu.VMEM((plan.sent, G, ch), F32),
            pltpu.VMEM((slabs, plan.cols1, 2, 2 * plan.rows1, LANES), F32),
            pltpu.VMEM((slabs, plan.cols0, 2, 2 * plan.rows1, LANES), F32),
            pltpu.VMEM((slabs, plan.cols0, 4, 4 * plan.rows1, LANES), F32),
        ]
        + maps(size3, size3)
        + maps(plan.sent, G)
        + maps(2 * plan.cols1, 2 * plan.rows1),
        compiler_params=pltpu.CompilerParams(vmem_limit_bytes=VMEM_LIMIT),
        cost_estimate=pl.CostEstimate(
            flops=5_000_000_000, bytes_accessed=20_000_000, transcendentals=0
        ),
        name="pyramid",
    )(where, mine, other, expand_four, expand_two, filters)


def finest_kernel(plan, where, summed, head, vector, filters, depth, weights, sems, first, second):
    ch = plan.ch
    phase, side = where[0], where[1]
    copies = start_filters(filters, 0, weights, sems)
    cols, rows = plan.conv_cols, plan.conv_rows
    own_rows = 4 * plan.half
    start0 = 4 * plan.start0(phase)
    own0 = 4 * phase * plan.block - start0
    own = own0 - jnp.clip(own0 - 2, 0, 4 * plan.cols0 - cols)
    row = pl.multiple_of(side * 16, 16)
    clear_edges(first)
    clear_edges(second)
    chunk = 4

    def source(col, n):
        return take(summed, pl.ds(col // 2, n // 2)).reshape(n, rows, ch)

    loop(cols // chunk, lambda i: put_shifted(first, i * chunk, source(i * chunk, chunk)))
    copies[0].wait()

    def inner(i):
        put_shifted(
            second, i * chunk, conv_block(first, weights.at[0], i * chunk, chunk, (0, rows))
        )

    loop(cols // chunk, inner)
    copies[1].wait()

    def outer(i):
        col = own + i * chunk
        branch = conv_block(second, weights.at[1], col, chunk, (row, own_rows))
        at = (pl.ds(col // 2, chunk // 2), slice(None), pl.ds(row, own_rows))
        joined = (take(summed, *at).reshape(branch.shape) + branch).astype(BF16)
        hidden = dot(joined.reshape(chunk * own_rows, ch), head[...])
        hidden = jnp.maximum(hidden, 0.0)
        depth[i] = lax.dot_general(
            vector[...],
            hidden,
            (((1,), (1,)), ((), ())),
            precision=lax.Precision.HIGHEST,
            preferred_element_type=F32,
        )

    loop(4 * plan.block // chunk, outer)


def finest(plan, where, summed, head, vector, filters):
    ch = plan.ch
    vmem = pl.BlockSpec(memory_space=pltpu.VMEM)
    own_cols, own_rows = 4 * plan.block, 4 * plan.half
    chunk = 4
    maps = pltpu.VMEM((3, plan.conv_cols + 2, plan.conv_rows, ch), BF16)
    vector = jnp.broadcast_to(vector[None, :], (8, vector.shape[0]))
    return pl.pallas_call(
        functools.partial(finest_kernel, plan),
        out_shape=jax.ShapeDtypeStruct((own_cols // chunk, 8, chunk * own_rows), F32),
        in_specs=[
            pl.BlockSpec(memory_space=pltpu.SMEM),
            vmem,
            vmem,
            vmem,
            pl.BlockSpec(memory_space=pl.ANY),
        ],
        out_specs=vmem,
        scratch_shapes=[
            pltpu.VMEM((2,) + filters.shape[2:], BF16),
            pltpu.SemaphoreType.DMA((2,)),
            maps,
            maps,
        ],
        compiler_params=pltpu.CompilerParams(vmem_limit_bytes=VMEM_LIMIT),
        cost_estimate=pl.CostEstimate(
            flops=6_000_000_000, bytes_accessed=6_000_000, transcendentals=0
        ),
        name="finest",
    )(where, summed, head, vector, filters)


def per_device(
    phases,
    dp_count,
    tap_tokens,
    project_weight,
    expand_four,
    expand_two,
    shrink_weight,
    refine_filters,
    head_matrix,
    head_vector,
    tile_slot,
):
    plan = Plan(phases, project_weight.shape[2])
    phase_id = lax.axis_index("phase")
    dp_id = lax.axis_index("dp")
    where = jnp.stack([phase_id, dp_id % 2]).astype(jnp.int32)
    filters = lax.all_gather(refine_filters, "dp", axis=2, tiled=True)
    sent = project(plan, phases, where, tap_tokens, project_weight, shrink_weight)
    arrived = [sent[0]] + [
        lax.ppermute(sent[k], "phase", [(s, s ^ k) for s in range(phases)])
        for k in range(1, phases)
    ]
    mine = jnp.stack(arrived)
    other = lax.ppermute(mine, "dp", [(d, d ^ 1) for d in range(dp_count)])
    summed = pyramid(plan, where, mine, other, expand_four, expand_two, filters)
    depth = finest(plan, where, summed, head_matrix, head_vector, filters)
    depth = depth[:, 0].reshape(4 * plan.block, TILES_DEV, -1)
    depth_tiles = depth.transpose(1, 2, 0).reshape(TILES_DEV, -1)
    slots = phase_id * dp_count * SLOT_DEV + jnp.arange(dp_count * SLOT_DEV, dtype=jnp.int32)
    targets = lax.dynamic_slice(tile_slot, (dp_id, phase_id, 0), (1, 1, TILES_DEV)).reshape(-1)
    matches = (slots[:, None] == targets[None, :]).astype(F32)
    partial = jnp.dot(matches, depth_tiles, precision=lax.Precision.HIGHEST)
    partial = partial.reshape(dp_count, SLOT_DEV, -1)
    portions = lax.all_to_all(partial, "dp", split_axis=0, concat_axis=0, tiled=True)
    return portions.sum(axis=0)


def solution(mesh):
    in_specs = (
        P("phase", "dp", None),
        P("phase", None, None),
        P(),
        P(),
        P(),
        P(None, None, "dp", None),
        P(),
        P(),
        P(),
    )
    out_specs = P(("phase", "dp"), None)
    body = functools.partial(per_device, mesh.shape["phase"], mesh.shape["dp"])
    return jax.shard_map(
        body, mesh=mesh, in_specs=in_specs, out_specs=out_specs, check_vma=False
    )
```

```python
import functools

import jax
import jax.numpy as jnp
from jax import lax
from jax.experimental import pallas as pl
from jax.experimental.pallas import tpu as pltpu
from jax.sharding import PartitionSpec as P

G = 32
TILES_DEV = 8
SLOT_DEV = 6
LEVELS = 4
F32 = jnp.float32
BF16 = jnp.bfloat16
VMEM_LIMIT = 60 * 1024 * 1024


LANES = 128


def take(ref, *at):
    return jnp.concatenate([ref[(i,) + at] for i in range(ref.shape[0])], axis=-1)


def put(ref, value, *at):
    for i in range(ref.shape[0]):
        ref[(i,) + at] = value[..., i * LANES : (i + 1) * LANES]


def dot(lhs, rhs):
    return jnp.dot(lhs, rhs, preferred_element_type=F32)


CHIP_ORDER = (2, 1, 3)
GROUPS = ((1, 2, 3), (0,))


class Plan:
    def __init__(self, phases, channels):
        self.ch = channels
        self.half = G // 2
        self.block = G // phases
        self.sent = 2 * self.block
        self.rows1 = 3 * G // 4
        self.cols1 = self.block + self.block // 2
        self.cols0 = self.block + 2
        self.conv_cols = 4 * self.block + 4
        self.conv_rows = 4 * self.half + 16

    def slot_of(self, level):
        return next(g.index(level) for g in GROUPS if level in g)

    def pieces_of(self, level, filters):
        groups = GROUPS[:1] if level else GROUPS[1:]
        n = next(i for i, g in enumerate(groups) if level in g)
        return filters[2 + 8 * n : 10 + 8 * n]

    def sent_start(self, s):
        return jnp.clip(s * self.block - self.block // 2, 0, G - self.sent)

    def start1(self, s):
        return jnp.clip(s * self.block - self.block // 4, 0, G - self.cols1)

    def start0(self, s):
        return jnp.clip(s * self.block - 1, 0, G - self.cols0)


def project_kernel(plan, phases, where, tokens, weight, shrink, *refs):
    outs, acc_lo, acc_hi = refs[:phases], refs[phases], refs[phases + 1]
    step = pl.program_id(0)
    part = dot(tokens[0], weight[0])
    lanes = acc_lo.shape[1]

    @pl.when(step == 0)
    def _():
        acc_lo[...] = part[:, :lanes]
        acc_hi[...] = part[:, lanes:]

    @pl.when(step > 0)
    def _():
        acc_lo[...] += part[:, :lanes]
        acc_hi[...] += part[:, lanes:]

    last = step == pl.num_programs(0) - 1
    phase = where[0]

    def column(start, size, stride):
        where_rows = pl.ds(start, size, stride=stride)
        return jnp.concatenate([acc_lo[where_rows, :], acc_hi[where_rows, :]], axis=1)

    @pl.when(last & (phase < LEVELS - 1))
    def _():
        for k in range(phases):
            start = plan.sent_start(phase ^ k)
            for j in range(plan.sent):
                outs[k][j * plan.half : (j + 1) * plan.half, :] = column(
                    start + j, plan.half, G
                ).astype(BF16)

    @pl.when(last & (phase == LEVELS - 1))
    def _():
        total = jnp.zeros((plan.half * plan.half // 2, plan.ch), F32)
        for a in range(2):
            for b in range(2):
                tall = jnp.concatenate(
                    [column(a * G + 2 * j + b, plan.half // 2, 2 * G) for j in range(G // 2)],
                    axis=0,
                )
                total += dot(
                    tall.astype(BF16), shrink[(2 * a + b) * plan.ch : (2 * a + b + 1) * plan.ch, :]
                )
        for k in range(phases):
            outs[k][: total.shape[0], :] = total.astype(BF16)
            outs[k][total.shape[0] :, :] = jnp.zeros(
                (outs[k].shape[0] - total.shape[0], plan.ch), BF16
            )


def project(plan, phases, where, tokens, weight, shrink):
    rows, depth = tokens.shape[1:]
    block = min(depth, 512)
    pixels = plan.sent * plan.half
    out = jax.ShapeDtypeStruct((pixels, plan.ch), BF16)
    return pl.pallas_call(
        functools.partial(project_kernel, plan, phases),
        grid_spec=pltpu.PrefetchScalarGridSpec(
            num_scalar_prefetch=1,
            grid=(depth // block,),
            in_specs=[
                pl.BlockSpec((1, rows, block), lambda i, w: (0, 0, i)),
                pl.BlockSpec((1, block, plan.ch), lambda i, w: (0, i, 0)),
                pl.BlockSpec(shrink.shape, lambda i, w: (0, 0)),
            ],
            out_specs=[pl.BlockSpec((pixels, plan.ch), lambda i, w: (0, 0))] * phases,
            scratch_shapes=[pltpu.VMEM((rows, plan.ch // 2), F32)] * 2,
        ),
        out_shape=[out] * phases,
        compiler_params=pltpu.CompilerParams(vmem_limit_bytes=VMEM_LIMIT),
        cost_estimate=pl.CostEstimate(
            flops=2 * rows * depth * plan.ch,
            bytes_accessed=2 * depth * (rows + plan.ch),
            transcendentals=0,
        ),
        name="project",
    )(where, tokens, weight, shrink)


def put_shifted(shifted, col, value):
    count, rows, _ = value.shape
    value = jnp.maximum(value, 0.0)
    at = lax.broadcasted_iota(jnp.int32, value.shape, 1)
    above = jnp.where(at == 0, 0.0, pltpu.roll(value, 1, 1))
    below = jnp.where(at == rows - 1, 0.0, pltpu.roll(value, rows - 1, 1))
    for p, moved in enumerate((above, value, below)):
        shifted[p, pl.ds(col + 1, count)] = moved.astype(BF16)


def clear_edges(shifted):
    shape = shifted.shape
    zeros = jnp.zeros((shape[0], 1) + shape[2:], BF16)
    shifted[:, 0:1] = zeros
    shifted[:, shape[1] - 1 : shape[1]] = zeros


def conv_block(shifted, weight, col, count, rows):
    channels = shifted.shape[3]
    start, size = rows
    patches = [
        shifted[p, pl.ds(col + q, count), pl.ds(start, size), :].reshape(count * size, channels)
        for p in range(3)
        for q in range(3)
    ]
    return dot(jnp.concatenate(patches, axis=1), weight[...]).reshape(count, size, -1)


def loop(count, body):
    if count == 1:
        body(0)
    else:
        lax.fori_loop(0, count, lambda i, c: (body(i), c)[1], 0)


def refine(source, weights, first, second, chunk, out_col, out_count, out_chunk, emit):
    cols, rows = first.shape[1] - 2, first.shape[2]
    clear_edges(first)
    clear_edges(second)
    loop(cols // chunk, lambda i: put_shifted(first, i * chunk, source(i * chunk, chunk)))

    def inner(i):
        put_shifted(second, i * chunk, conv_block(first, weights[0], i * chunk, chunk, (0, rows)))

    loop(cols // chunk, inner)

    def outer(i):
        col = out_col + i * out_chunk
        branch = conv_block(second, weights[1], col, out_chunk, (0, rows))
        emit(i * out_chunk, source(col, out_chunk) + branch)

    loop(out_count // out_chunk, outer)


def start_filters(plan, where, filters, level, weights, sem):
    if len(filters) == 1:
        pltpu.make_async_copy(filters[0].at[level], weights, sem).start()
        return
    phase, side, chip = where[0], where[1], where[2]
    own, swapped = filters[:2]
    rows = own.shape[2]
    part = rows // 2
    for ref, core in ((own, side), (swapped, 1 - side)):
        at = pl.ds(pl.multiple_of((2 * chip + core) * rows, 16), rows)
        pltpu.make_async_copy(ref.at[level], weights.at[:, at], sem).start()
    at_level = plan.slot_of(level)
    pieces = plan.pieces_of(level, filters)
    for refs, core in ((pieces[:4], side), (pieces[4:], 1 - side)):
        for ref, moved in zip(refs, (0, 1 + core, 2 - core, 3)):
            quarter = phase ^ moved
            for i, away in enumerate(CHIP_ORDER):
                start = (2 * (chip ^ away) + core) * rows + (quarter % 2) * part
                at = pl.ds(pl.multiple_of(start, 16), part)
                pltpu.make_async_copy(
                    ref.at[i, at_level], weights.at[quarter // 2, at], sem
                ).start()


def wait_filters(weights, sem):
    pltpu.make_async_copy(weights, weights, sem).wait()


def pyramid_kernel(
    plan,
    where,
    mine,
    other,
    expand_four,
    expand_two,
    *refs,
):
    count = len(refs) - PYRAMID_SCRATCH
    filters, refs = refs[:count], refs[count:]
    pyramid_body(plan, where, mine, other, expand_four, expand_two, filters, *refs)


PYRAMID_SCRATCH = 20


def pyramid_body(
    plan,
    where,
    mine,
    other,
    expand_four,
    expand_two,
    filters,
    summed0,
    weight3,
    weight2,
    weight1,
    sems,
    out_sem,
    patch,
    map3,
    joined3,
    map2,
    joined2,
    map1,
    joined1,
    map0,
    first3,
    second3,
    first2,
    second2,
    first1,
    second1,
):
    ch = plan.ch
    phase, side = where[0], where[1]
    weights_of = {3: weight3, 2: weight2, 1: weight1}
    for level, weights in weights_of.items():
        start_filters(plan, where, filters, level, weights, sems.at[level])

    def load_patches(level):
        k = phase ^ level
        for ref, at in ((mine, side), (other, 1 - side)):
            patch[:, pl.ds(pl.multiple_of(at * plan.half, plan.half), plan.half), :] = (
                ref[k].astype(F32).reshape(plan.sent, plan.half, ch)
            )

    def wait(level):
        wait_filters(weights_of[level], sems.at[level])

    size3 = G // 2
    quarter = plan.half // 2
    k3 = phase ^ 3
    for ref, at in ((mine, side), (other, 1 - side)):
        map3[:, pl.ds(pl.multiple_of(at * quarter, quarter), quarter), :] = (
            ref[k3, : size3 * quarter, :].astype(F32).reshape(size3, quarter, ch)
        )
    wait(3)

    def keep3(col, value):
        joined3[pl.ds(col, value.shape[0])] = value.astype(BF16).astype(F32)

    refine(
        lambda col, n: map3[pl.ds(col, n)], weight3, first3, second3, size3, 0, size3, size3, keep3
    )

    load_patches(2)
    from3 = plan.sent_start(phase) // 2
    tall = joined3[pl.ds(from3, plan.sent // 2)]
    for b in range(2):
        for a in range(2):
            put(map2, tall, slice(None), b, pl.ds(a, size3, stride=2), slice(None))
    for j in range(plan.sent):
        at = (j // 2, j % 2)
        put(map2, take(map2, *at) + patch[j], *at)
    wait(2)

    def source2(col, n):
        return take(map2, pl.ds(col // 2, n // 2)).reshape(n, G, ch)

    def keep2(col, value):
        joined2[pl.ds(col, value.shape[0])] = value.astype(BF16).astype(F32)

    refine(source2, weight2, first2, second2, plan.block, 0, plan.sent, plan.block, keep2)

    load_patches(1)
    row1 = pl.multiple_of(side * (G - plan.rows1), 8)
    off1 = plan.start1(phase) - plan.sent_start(phase)
    tall = patch[pl.ds(off1, plan.cols1), pl.ds(row1, plan.rows1), :]
    lhs = tall.reshape(plan.cols1 * plan.rows1, ch).astype(BF16)
    below = joined2[pl.ds(off1, plan.cols1), pl.ds(row1, plan.rows1), :]
    for a in range(2):
        for b in range(2):
            n = 2 * a + b
            grown = dot(lhs, expand_two[:, n * ch : (n + 1) * ch])
            put(
                map1,
                grown.reshape(plan.cols1, plan.rows1, ch) + below,
                slice(None),
                b,
                pl.ds(a, plan.rows1, stride=2),
                slice(None),
            )
    wait(1)
    off0 = 2 * (plan.start0(phase) - plan.start1(phase))

    def source1(col, n):
        return take(map1, pl.ds(col // 2, n // 2)).reshape(n, 2 * plan.rows1, ch)

    def keep1(col, value):
        at = pl.ds(col // 2, value.shape[0] // 2)
        value = value.astype(BF16).astype(F32)
        put(joined1, value.reshape(value.shape[0] // 2, 2, 2 * plan.rows1, ch), at)

    refine(
        source1, weight1, first1, second1, plan.block, off0, 2 * plan.cols0, 4, keep1
    )

    load_patches(0)
    off = plan.start0(phase) - plan.sent_start(phase)
    tall = patch[pl.ds(off, plan.cols0), pl.ds(row1, plan.rows1), :]
    lhs = tall.reshape(plan.cols0 * plan.rows1, ch).astype(BF16)
    for a in range(4):
        for b in range(4):
            n = 4 * a + b
            grown = dot(lhs, expand_four[:, n * ch : (n + 1) * ch])
            below = take(
                joined1, slice(None), b // 2, pl.ds(a // 2, plan.rows1, stride=2), slice(None)
            )
            put(
                map0,
                grown.reshape(plan.cols0, plan.rows1, ch) + below,
                slice(None),
                b,
                pl.ds(a, plan.rows1, stride=4),
                slice(None),
            )
    own0 = 4 * (phase * plan.block - plan.start0(phase))
    conv0 = jnp.clip(own0 - 2, 0, 4 * plan.cols0 - plan.conv_cols) // 2
    out = pltpu.make_async_copy(
        map0.reshape(ch // LANES, 2 * plan.cols0, 2, 4 * plan.rows1, LANES).at[
            :,
            pl.ds(conv0, plan.conv_cols // 2),
            :,
            pl.ds(pl.multiple_of(side * 16, 16), plan.conv_rows),
            :,
        ],
        summed0,
        out_sem,
    )
    out.start()
    out.wait()


def pyramid(plan, where, mine, other, expand_four, expand_two, filters):
    ch = plan.ch
    depth = 9 * ch
    vmem = pl.BlockSpec(memory_space=pltpu.VMEM)
    any_space = pl.BlockSpec(memory_space=pl.ANY)
    weights = pltpu.VMEM((2, depth, ch), BF16)
    size3 = G // 2
    slabs = ch // LANES

    def maps(cols, rows):
        return [pltpu.VMEM((3, cols + 2, rows, ch), BF16)] * 2

    return pl.pallas_call(
        functools.partial(pyramid_kernel, plan),
        out_shape=jax.ShapeDtypeStruct(
            (ch // LANES, plan.conv_cols // 2, 2, plan.conv_rows, LANES), F32
        ),
        in_specs=[pl.BlockSpec(memory_space=pltpu.SMEM), vmem, vmem, vmem, vmem]
        + [any_space] * len(filters),
        out_specs=any_space,
        scratch_shapes=[
            weights,
            weights,
            weights,
            pltpu.SemaphoreType.DMA((LEVELS,)),
            pltpu.SemaphoreType.DMA,
            pltpu.VMEM((plan.sent, G, ch), F32),
            pltpu.VMEM((size3, size3, ch), F32),
            pltpu.VMEM((size3, size3, ch), F32),
            pltpu.VMEM((slabs, plan.sent // 2, 2, G, LANES), F32),
            pltpu.VMEM((plan.sent, G, ch), F32),
            pltpu.VMEM((slabs, plan.cols1, 2, 2 * plan.rows1, LANES), F32),
            pltpu.VMEM((slabs, plan.cols0, 2, 2 * plan.rows1, LANES), F32),
            pltpu.VMEM((slabs, plan.cols0, 4, 4 * plan.rows1, LANES), F32),
        ]
        + maps(size3, size3)
        + maps(plan.sent, G)
        + maps(2 * plan.cols1, 2 * plan.rows1),
        compiler_params=pltpu.CompilerParams(vmem_limit_bytes=VMEM_LIMIT),
        cost_estimate=pl.CostEstimate(
            flops=5_000_000_000, bytes_accessed=20_000_000, transcendentals=0
        ),
        name="pyramid",
    )(where, mine, other, expand_four, expand_two, *filters)


def finest_kernel(plan, where, summed, head, vector, *refs):
    filters, refs = refs[:-5], refs[-5:]
    depth, weights, sem, first, second = refs
    ch = plan.ch
    phase, side = where[0], where[1]
    start_filters(plan, where, filters, 0, weights, sem)
    cols, rows = plan.conv_cols, plan.conv_rows
    own_rows = 4 * plan.half
    start0 = 4 * plan.start0(phase)
    own0 = 4 * phase * plan.block - start0
    own = own0 - jnp.clip(own0 - 2, 0, 4 * plan.cols0 - cols)
    row = pl.multiple_of(side * 16, 16)
    clear_edges(first)
    clear_edges(second)
    chunk = 4

    def source(col, n):
        return take(summed, pl.ds(col // 2, n // 2)).reshape(n, rows, ch)

    loop(cols // chunk, lambda i: put_shifted(first, i * chunk, source(i * chunk, chunk)))
    wait_filters(weights, sem)

    def inner(i):
        put_shifted(
            second, i * chunk, conv_block(first, weights.at[0], i * chunk, chunk, (0, rows))
        )

    loop(cols // chunk, inner)

    def outer(i):
        col = own + i * chunk
        branch = conv_block(second, weights.at[1], col, chunk, (row, own_rows))
        at = (pl.ds(col // 2, chunk // 2), slice(None), pl.ds(row, own_rows))
        joined = (take(summed, *at).reshape(branch.shape) + branch).astype(BF16)
        hidden = dot(joined.reshape(chunk * own_rows, ch), head[...])
        hidden = jnp.maximum(hidden, 0.0)
        depth[i] = lax.dot_general(
            vector[...],
            hidden,
            (((1,), (1,)), ((), ())),
            precision=lax.Precision.HIGHEST,
            preferred_element_type=F32,
        )

    loop(4 * plan.block // chunk, outer)


def finest(plan, where, summed, head, vector, filters):
    ch = plan.ch
    vmem = pl.BlockSpec(memory_space=pltpu.VMEM)
    own_cols, own_rows = 4 * plan.block, 4 * plan.half
    chunk = 4
    maps = pltpu.VMEM((3, plan.conv_cols + 2, plan.conv_rows, ch), BF16)
    vector = jnp.broadcast_to(vector[None, :], (8, vector.shape[0]))
    return pl.pallas_call(
        functools.partial(finest_kernel, plan),
        out_shape=jax.ShapeDtypeStruct((own_cols // chunk, 8, chunk * own_rows), F32),
        in_specs=[
            pl.BlockSpec(memory_space=pltpu.SMEM),
            vmem,
            vmem,
            vmem,
        ]
        + [pl.BlockSpec(memory_space=pl.ANY)] * len(filters),
        out_specs=vmem,
        scratch_shapes=[
            pltpu.VMEM((2, 9 * ch, ch), BF16),
            pltpu.SemaphoreType.DMA,
            maps,
            maps,
        ],
        compiler_params=pltpu.CompilerParams(vmem_limit_bytes=VMEM_LIMIT),
        cost_estimate=pl.CostEstimate(
            flops=6_000_000_000, bytes_accessed=6_000_000, transcendentals=0
        ),
        name="finest",
    )(where, summed, head, vector, *filters)


def gather_filters(filters, phases, dp_count):
    axes = ("phase", "dp")
    phase_id = lax.axis_index("phase")
    chips = dp_count // 2

    def move(value, to):
        route = []
        for p in range(phases):
            for z in range(chips):
                for c in range(2):
                    q, y, d = to(p, z, c)
                    route.append((p * dp_count + 2 * z + c, q * dp_count + 2 * y + d))
        return lax.ppermute(value, axes, route)

    def across(value, bit):
        return move(value, lambda p, z, c: (p, z ^ bit, c))

    def first(value):
        return move(value, lambda p, z, c: (p ^ (1 + c), z, c))

    def second(value):
        return move(value, lambda p, z, c: (p ^ (2 - c), z, c))

    def swap(value):
        return move(value, lambda p, z, c: (p, z, c ^ 1))

    levels, convs, rows, channels = filters.shape
    quarters = filters.reshape(levels, phases, convs * rows // phases, channels)
    swapped = swap(filters)
    gathered = []
    for group in GROUPS:
        part = lax.slice_in_dim(quarters, group[0], group[-1] + 1, axis=0)
        own = lax.dynamic_index_in_dim(part, phase_id, 1, keepdims=False)
        far = across(own, 2)
        column = jnp.stack([far, across(own, 1), across(far, 1)])
        one = first(column)
        pieces = [column, one, second(column), second(one)]
        gathered.append(pieces + [swap(piece) for piece in pieces])
    return [filters, swapped], gathered


def per_device(
    phases,
    dp_count,
    tap_tokens,
    project_weight,
    expand_four,
    expand_two,
    shrink_weight,
    refine_filters,
    head_matrix,
    head_vector,
    tile_slot,
):
    plan = Plan(phases, project_weight.shape[2])
    phase_id = lax.axis_index("phase")
    dp_id = lax.axis_index("dp")
    where = jnp.stack([phase_id, dp_id % 2, dp_id // 2]).astype(jnp.int32)
    if phases == 4 and dp_count == 8 and refine_filters.shape[2] % 32 == 0:
        base, gathered = gather_filters(refine_filters, phases, dp_count)
        upper, finer = base + gathered[0], base + gathered[1]
    else:
        upper = finer = [lax.all_gather(refine_filters, "dp", axis=2, tiled=True)]
    sent = project(plan, phases, where, tap_tokens, project_weight, shrink_weight)
    arrived = [sent[0]] + [
        lax.ppermute(sent[k], "phase", [(s, s ^ k) for s in range(phases)])
        for k in range(1, phases)
    ]
    mine = jnp.stack(arrived)
    other = lax.ppermute(mine, "dp", [(d, d ^ 1) for d in range(dp_count)])
    summed = pyramid(plan, where, mine, other, expand_four, expand_two, upper)
    depth = finest(plan, where, summed, head_matrix, head_vector, finer)
    depth = depth[:, 0].reshape(4 * plan.block, TILES_DEV, -1)
    depth_tiles = depth.transpose(1, 2, 0).reshape(TILES_DEV, -1)
    slots = phase_id * dp_count * SLOT_DEV + jnp.arange(dp_count * SLOT_DEV, dtype=jnp.int32)
    targets = lax.dynamic_slice(tile_slot, (dp_id, phase_id, 0), (1, 1, TILES_DEV)).reshape(-1)
    matches = (slots[:, None] == targets[None, :]).astype(F32)
    partial = jnp.dot(matches, depth_tiles, precision=lax.Precision.HIGHEST)
    partial = partial.reshape(dp_count, SLOT_DEV, -1)
    portions = lax.all_to_all(partial, "dp", split_axis=0, concat_axis=0, tiled=True)
    return portions.sum(axis=0)


def solution(mesh):
    in_specs = (
        P("phase", "dp", None),
        P("phase", None, None),
        P(),
        P(),
        P(),
        P(None, None, "dp", None),
        P(),
        P(),
        P(),
    )
    out_specs = P(("phase", "dp"), None)
    body = functools.partial(per_device, mesh.shape["phase"], mesh.shape["dp"])
    return jax.shard_map(
        body, mesh=mesh, in_specs=in_specs, out_specs=out_specs, check_vma=False
    )
```

```python
import functools

import jax
import jax.numpy as jnp
from jax import lax
from jax.experimental import pallas as pl
from jax.experimental.pallas import tpu as pltpu
from jax.sharding import PartitionSpec as P

G = 32
TILES_DEV = 8
SLOT_DEV = 6
LEVELS = 4
F32 = jnp.float32
BF16 = jnp.bfloat16
PROJECT_VMEM = 16 * 1024 * 1024
COARSE_VMEM = 32 * 1024 * 1024
FINE_VMEM = 48 * 1024 * 1024


LANES = 128


def take(ref, *at):
    return jnp.concatenate([ref[(i,) + at] for i in range(ref.shape[0])], axis=-1)


def put(ref, value, *at):
    for i in range(ref.shape[0]):
        ref[(i,) + at] = value[..., i * LANES : (i + 1) * LANES]


def dot(lhs, rhs):
    return jnp.dot(lhs, rhs, preferred_element_type=F32)


CHIP_ORDER = (2, 1, 3)
GROUPS = ((2, 3), (0, 1))


class Plan:
    def __init__(self, phases, channels):
        self.phases = phases
        self.ch = channels
        self.half = G // 2
        self.block = G // phases
        self.sent = 2 * self.block
        self.rows1 = 3 * G // 4
        self.cols1 = self.block + self.block // 2
        self.cols0 = self.block + 2
        self.conv_cols = 4 * self.block + 4
        self.conv_rows = 4 * self.half + 16

    def slot_of(self, level):
        return next(g.index(level) for g in GROUPS if level in g)

    def sent_start(self, s):
        return jnp.clip(s * self.block - self.block // 2, 0, G - self.sent)

    def start1(self, s):
        return jnp.clip(s * self.block - self.block // 4, 0, G - self.cols1)

    def start0(self, s):
        return jnp.clip(s * self.block - 1, 0, G - self.cols0)


def project_kernel(plan, phases, where, tokens, weight, shrink, *refs):
    outs, acc_lo, acc_hi = refs[:phases], refs[phases], refs[phases + 1]
    step = pl.program_id(0)
    part = dot(tokens[0], weight[0])
    lanes = acc_lo.shape[1]

    @pl.when(step == 0)
    def _():
        acc_lo[...] = part[:, :lanes]
        acc_hi[...] = part[:, lanes:]

    @pl.when(step > 0)
    def _():
        acc_lo[...] += part[:, :lanes]
        acc_hi[...] += part[:, lanes:]

    last = step == pl.num_programs(0) - 1
    phase = where[0]

    def column(start, size, stride):
        where_rows = pl.ds(start, size, stride=stride)
        return jnp.concatenate([acc_lo[where_rows, :], acc_hi[where_rows, :]], axis=1)

    @pl.when(last & (phase < LEVELS - 1))
    def _():
        for k in range(phases):
            start = plan.sent_start(phase ^ k)
            for j in range(plan.sent):
                outs[k][j * plan.half : (j + 1) * plan.half, :] = column(
                    start + j, plan.half, G
                ).astype(BF16)

    @pl.when(last & (phase == LEVELS - 1))
    def _():
        total = jnp.zeros((plan.half * plan.half // 2, plan.ch), F32)
        for a in range(2):
            for b in range(2):
                tall = jnp.concatenate(
                    [column(a * G + 2 * j + b, plan.half // 2, 2 * G) for j in range(G // 2)],
                    axis=0,
                )
                total += dot(
                    tall.astype(BF16), shrink[(2 * a + b) * plan.ch : (2 * a + b + 1) * plan.ch, :]
                )
        for k in range(phases):
            outs[k][: total.shape[0], :] = total.astype(BF16)
            outs[k][total.shape[0] :, :] = jnp.zeros(
                (outs[k].shape[0] - total.shape[0], plan.ch), BF16
            )


def project(plan, phases, where, tokens, weight, shrink):
    rows, depth = tokens.shape[1:]
    block = min(depth, 512)
    pixels = plan.sent * plan.half
    out = jax.ShapeDtypeStruct((pixels, plan.ch), BF16)
    return pl.pallas_call(
        functools.partial(project_kernel, plan, phases),
        grid_spec=pltpu.PrefetchScalarGridSpec(
            num_scalar_prefetch=1,
            grid=(depth // block,),
            in_specs=[
                pl.BlockSpec((1, rows, block), lambda i, w: (0, 0, i)),
                pl.BlockSpec((1, block, plan.ch), lambda i, w: (0, i, 0)),
                pl.BlockSpec(shrink.shape, lambda i, w: (0, 0)),
            ],
            out_specs=[pl.BlockSpec((pixels, plan.ch), lambda i, w: (0, 0))] * phases,
            scratch_shapes=[pltpu.VMEM((rows, plan.ch // 2), F32)] * 2,
        ),
        out_shape=[out] * phases,
        compiler_params=pltpu.CompilerParams(vmem_limit_bytes=PROJECT_VMEM),
        cost_estimate=pl.CostEstimate(
            flops=2 * rows * depth * plan.ch,
            bytes_accessed=2 * depth * (rows + plan.ch),
            transcendentals=0,
        ),
        name="project",
    )(where, tokens, weight, shrink)


def put_shifted(shifted, col, value):
    count, rows, _ = value.shape
    value = jnp.maximum(value, 0.0)
    at = lax.broadcasted_iota(jnp.int32, value.shape, 1)
    above = jnp.where(at == 0, 0.0, pltpu.roll(value, 1, 1))
    below = jnp.where(at == rows - 1, 0.0, pltpu.roll(value, rows - 1, 1))
    for p, moved in enumerate((above, value, below)):
        shifted[p, pl.ds(col + 1, count)] = moved.astype(BF16)


def clear_edges(shifted):
    shape = shifted.shape
    zeros = jnp.zeros((shape[0], 1) + shape[2:], BF16)
    shifted[:, 0:1] = zeros
    shifted[:, shape[1] - 1 : shape[1]] = zeros


def conv_block(shifted, weight, col, count, rows):
    channels = shifted.shape[3]
    start, size = rows
    patches = [
        shifted[p, pl.ds(col + q, count), pl.ds(start, size), :].reshape(count * size, channels)
        for p in range(3)
        for q in range(3)
    ]
    return dot(jnp.concatenate(patches, axis=1), weight[...]).reshape(count, size, -1)


def loop(count, body):
    if count == 1:
        body(0)
    else:
        lax.fori_loop(0, count, lambda i, c: (body(i), c)[1], 0)


def refine(source, weights, sems, first, second, chunk, out_col, out_count, out_chunk, emit):
    cols, rows = first.shape[1] - 2, first.shape[2]
    clear_edges(first)
    clear_edges(second)
    loop(cols // chunk, lambda i: put_shifted(first, i * chunk, source(i * chunk, chunk)))

    wait_filters(weights, sems, 0)

    def inner(i):
        put_shifted(second, i * chunk, conv_block(first, weights.at[0], i * chunk, chunk, (0, rows)))

    loop(cols // chunk, inner)

    wait_filters(weights, sems, 1)

    def outer(i):
        col = out_col + i * out_chunk
        branch = conv_block(second, weights.at[1], col, out_chunk, (0, rows))
        emit(i * out_chunk, source(col, out_chunk) + branch)

    loop(out_count // out_chunk, outer)


def start_filters(plan, where, filters, level, weights, sems):
    if len(filters) == 1:
        for m in range(2):
            pltpu.make_async_copy(filters[0].at[level, m], weights.at[m], sems.at[m]).start()
        return
    phase, side, chip = where[0], where[1], where[2]
    own, swapped = filters[:2]
    rows = own.shape[2]
    part = rows // 2
    slot = plan.slot_of(level)
    for m in range(2):
        for ref, core in ((own, side), (swapped, 1 - side)):
            at = pl.ds(pl.multiple_of((2 * chip + core) * rows, 16), rows)
            pltpu.make_async_copy(ref.at[level, m], weights.at[m, at], sems.at[m]).start()

    def start_pieces(p):
        for m in range(2):
            for half in range(2):
                quarter = 2 * m + half
                for i, away in enumerate(CHIP_ORDER):
                    for refs, core in ((filters[2:6], side), (filters[6:10], 1 - side)):
                        start = (2 * (chip ^ away) + core) * rows + half * part
                        at = pl.ds(pl.multiple_of(start, 16), part)
                        moved = p ^ quarter
                        if moved in (0, 3):
                            pltpu.make_async_copy(
                                refs[moved].at[i, slot], weights.at[m, at], sems.at[m]
                            ).start()
                            continue
                        for c in range(2):
                            k = moved if c == 0 else 3 - moved

                            @pl.when(core == c)
                            def _(ref=refs[k], at=at, i=i, m=m):
                                pltpu.make_async_copy(
                                    ref.at[i, slot], weights.at[m, at], sems.at[m]
                                ).start()

    for p in range(plan.phases):

        @pl.when(phase == p)
        def _(p=p):
            start_pieces(p)


def wait_filters(weights, sems, m):
    pltpu.make_async_copy(weights.at[m], weights.at[m], sems.at[m]).wait()


def load_patches(plan, patch, mine, other, k, side):
    for ref, at in ((mine, side), (other, 1 - side)):
        patch[:, pl.ds(pl.multiple_of(at * plan.half, plan.half), plan.half), :] = (
            ref[k].astype(F32).reshape(plan.sent, plan.half, plan.ch)
        )


def rounded(value):
    return value.astype(BF16).astype(F32)


COARSE_SCRATCH = 14


def coarse_kernel(plan, where, mine, other, expand_two, *refs):
    count = len(refs) - COARSE_SCRATCH
    filters = refs[:count]
    (
        summed1,
        patch0,
        weight3,
        weight2,
        sems,
        patch,
        map3,
        joined3,
        map2,
        joined2,
        first3,
        second3,
        first2,
        second2,
    ) = refs[count:]
    ch = plan.ch
    phase, side = where[0], where[1]
    for level, weights in ((3, weight3), (2, weight2)):
        start_filters(plan, where, filters, level, weights, sems.at[level])

    row1 = pl.multiple_of(side * (G - plan.rows1), 8)
    load_patches(plan, patch, mine, other, phase, side)
    off = plan.start0(phase) - plan.sent_start(phase)
    tall = patch[pl.ds(off, plan.cols0), pl.ds(row1, plan.rows1), :]
    patch0[...] = tall.reshape(patch0.shape).astype(BF16)

    size3 = G // 2
    quarter = plan.half // 2
    k3 = phase ^ 3
    for ref, at in ((mine, side), (other, 1 - side)):
        map3[:, pl.ds(pl.multiple_of(at * quarter, quarter), quarter), :] = (
            ref[k3, : size3 * quarter, :].astype(F32).reshape(size3, quarter, ch)
        )

    def keep3(col, value):
        joined3[pl.ds(col, value.shape[0])] = rounded(value)

    refine(
        lambda col, n: map3[pl.ds(col, n)],
        weight3,
        sems.at[3],
        first3,
        second3,
        size3,
        0,
        size3,
        size3,
        keep3,
    )

    load_patches(plan, patch, mine, other, phase ^ 2, side)
    from3 = plan.sent_start(phase) // 2
    tall = joined3[pl.ds(from3, plan.sent // 2)]
    for b in range(2):
        for a in range(2):
            put(map2, tall, slice(None), b, pl.ds(a, size3, stride=2), slice(None))
    for j in range(plan.sent):
        at = (j // 2, j % 2)
        put(map2, take(map2, *at) + patch[j], *at)

    def source2(col, n):
        return take(map2, pl.ds(col // 2, n // 2)).reshape(n, G, ch)

    def keep2(col, value):
        joined2[pl.ds(col, value.shape[0])] = rounded(value)

    refine(
        source2, weight2, sems.at[2], first2, second2, plan.sent, 0, plan.sent, plan.sent, keep2
    )

    load_patches(plan, patch, mine, other, phase ^ 1, side)
    off1 = plan.start1(phase) - plan.sent_start(phase)
    tall = patch[pl.ds(off1, plan.cols1), pl.ds(row1, plan.rows1), :]
    lhs = tall.reshape(plan.cols1 * plan.rows1, ch).astype(BF16)
    below = joined2[pl.ds(off1, plan.cols1), pl.ds(row1, plan.rows1), :]
    for a in range(2):
        for b in range(2):
            n = 2 * a + b
            grown = dot(lhs, expand_two[:, n * ch : (n + 1) * ch])
            put(
                summed1,
                grown.reshape(plan.cols1, plan.rows1, ch) + below,
                slice(None),
                b,
                pl.ds(a, plan.rows1, stride=2),
                slice(None),
            )


def shifted_maps(cols, rows, ch):
    return [pltpu.VMEM((3, cols + 2, rows, ch), BF16)] * 2


def coarse(plan, where, mine, other, expand_two, filters):
    ch = plan.ch
    vmem = pl.BlockSpec(memory_space=pltpu.VMEM)
    weights = pltpu.VMEM((2, 9 * ch, ch), BF16)
    size3 = G // 2
    slabs = ch // LANES
    return pl.pallas_call(
        functools.partial(coarse_kernel, plan),
        out_shape=[
            jax.ShapeDtypeStruct((slabs, plan.cols1, 2, 2 * plan.rows1, LANES), F32),
            jax.ShapeDtypeStruct((plan.cols0 * plan.rows1, ch), BF16),
        ],
        in_specs=[pl.BlockSpec(memory_space=pltpu.SMEM), vmem, vmem, vmem]
        + [pl.BlockSpec(memory_space=pl.ANY)] * len(filters),
        out_specs=[vmem, vmem],
        scratch_shapes=[
            weights,
            weights,
            pltpu.SemaphoreType.DMA((LEVELS, 2)),
            pltpu.VMEM((plan.sent, G, ch), F32),
            pltpu.VMEM((size3, size3, ch), F32),
            pltpu.VMEM((size3, size3, ch), F32),
            pltpu.VMEM((slabs, plan.sent // 2, 2, G, LANES), F32),
            pltpu.VMEM((plan.sent, G, ch), F32),
        ]
        + shifted_maps(size3, size3, ch)
        + shifted_maps(plan.sent, G, ch),
        compiler_params=pltpu.CompilerParams(vmem_limit_bytes=COARSE_VMEM),
        cost_estimate=pl.CostEstimate(
            flops=2_000_000_000, bytes_accessed=8_000_000, transcendentals=0
        ),
        name="coarse",
    )(where, mine, other, expand_two, *filters)


FINE_SCRATCH = 12


def fine_kernel(plan, where, summed1, patch0, head, vector, expand_four, *refs):
    count = len(refs) - FINE_SCRATCH
    filters = refs[:count]
    (
        depth,
        weight1,
        weight0,
        sems,
        grow,
        grow_sem,
        joined1,
        map0,
        first1,
        second1,
        first,
        second,
    ) = refs[count:]
    ch = plan.ch
    phase, side = where[0], where[1]
    start_filters(plan, where, filters, 1, weight1, sems.at[1])
    grow_copy = pltpu.make_async_copy(expand_four, grow, grow_sem)
    grow_copy.start()
    start_filters(plan, where, filters, 0, weight0, sems.at[0])

    off0 = 2 * (plan.start0(phase) - plan.start1(phase))

    def source1(col, n):
        return take(summed1, pl.ds(col // 2, n // 2)).reshape(n, 2 * plan.rows1, ch)

    def keep1(col, value):
        value = rounded(value)
        put(
            joined1,
            value.reshape(value.shape[0] // 2, 2, 2 * plan.rows1, ch),
            pl.ds(col // 2, value.shape[0] // 2),
        )

    refine(
        source1,
        weight1,
        sems.at[1],
        first1,
        second1,
        plan.cols1,
        off0,
        2 * plan.cols0,
        plan.cols0,
        keep1,
    )

    grow_copy.wait()
    for a in range(4):
        for b in range(4):
            n = 4 * a + b
            grown = dot(patch0[...], grow[:, n * ch : (n + 1) * ch])
            below = take(
                joined1, slice(None), b // 2, pl.ds(a // 2, plan.rows1, stride=2), slice(None)
            )
            put(
                map0,
                grown.reshape(plan.cols0, plan.rows1, ch) + below,
                slice(None),
                b,
                pl.ds(a, plan.rows1, stride=4),
                slice(None),
            )
    cols, rows, own_rows = plan.conv_cols, plan.conv_rows, 4 * plan.half
    own0 = 4 * (phase * plan.block - plan.start0(phase))
    conv0 = jnp.clip(own0 - 2, 0, 4 * plan.cols0 - cols)
    own = own0 - conv0
    row = pl.multiple_of(side * 16, 16)
    pairs = map0.reshape(ch // LANES, 2 * plan.cols0, 2, 4 * plan.rows1, LANES)
    chunk = cols // 2

    def source0(col, n, start, size):
        at = (pl.ds((conv0 + col) // 2, n // 2), slice(None), pl.ds(start, size), slice(None))
        return take(pairs, *at).reshape(n, size, ch)

    clear_edges(first)
    clear_edges(second)
    loop(9, lambda i: put_shifted(first, i * 4, source0(i * 4, 4, row, rows)))
    wait_filters(weight0, sems.at[0], 0)

    def inner(i):
        put_shifted(
            second, i * chunk, conv_block(first, weight0.at[0], i * chunk, chunk, (0, rows))
        )

    loop(cols // chunk, inner)
    wait_filters(weight0, sems.at[0], 1)
    half_cols = 2 * plan.block

    def outer(i):
        col = own + i * half_cols
        branch = conv_block(second, weight0.at[1], col, half_cols, (row, own_rows))
        summed = source0(col, half_cols, pl.multiple_of(2 * row, 16), own_rows)
        joined = (summed + branch).astype(BF16)
        hidden = lax.dot_general(
            head[...],
            joined.reshape(half_cols * own_rows, ch),
            (((1,), (1,)), ((), ())),
            preferred_element_type=F32,
        )
        hidden = jnp.maximum(hidden, 0.0) * vector[...]
        depth[i] = jnp.broadcast_to(hidden.sum(axis=0, keepdims=True), depth.shape[1:])

    loop(2, outer)


def fine(plan, where, summed1, patch0, head, vector, expand_four, filters):
    ch = plan.ch
    vmem = pl.BlockSpec(memory_space=pltpu.VMEM)
    any_space = pl.BlockSpec(memory_space=pl.ANY)
    own_rows = 4 * plan.half
    slabs = ch // LANES
    weights = pltpu.VMEM((2, 9 * ch, ch), BF16)
    return pl.pallas_call(
        functools.partial(fine_kernel, plan),
        out_shape=jax.ShapeDtypeStruct((2, 8, 2 * plan.block * own_rows), F32),
        in_specs=[pl.BlockSpec(memory_space=pltpu.SMEM), vmem, vmem, vmem, vmem, any_space]
        + [any_space] * len(filters),
        out_specs=vmem,
        scratch_shapes=[
            weights,
            weights,
            pltpu.SemaphoreType.DMA((LEVELS, 2)),
            pltpu.VMEM(expand_four.shape, BF16),
            pltpu.SemaphoreType.DMA,
            pltpu.VMEM((slabs, plan.cols0, 2, 2 * plan.rows1, LANES), F32),
            pltpu.VMEM((slabs, plan.cols0, 4, 4 * plan.rows1, LANES), F32),
        ]
        + shifted_maps(2 * plan.cols1, 2 * plan.rows1, ch)
        + shifted_maps(plan.conv_cols, plan.conv_rows, ch),
        compiler_params=pltpu.CompilerParams(vmem_limit_bytes=FINE_VMEM),
        cost_estimate=pl.CostEstimate(
            flops=8_000_000_000, bytes_accessed=10_000_000, transcendentals=0
        ),
        name="fine",
    )(where, summed1, patch0, head.T, vector[:, None], expand_four, *filters)


def gather_filters(filters, phases, dp_count):
    axes = ("phase", "dp")
    phase_id = lax.axis_index("phase")
    chips = dp_count // 2

    def move(value, to):
        route = []
        for p in range(phases):
            for z in range(chips):
                for c in range(2):
                    q, y, d = to(p, z, c)
                    route.append((p * dp_count + 2 * z + c, q * dp_count + 2 * y + d))
        return lax.ppermute(value, axes, route)

    def across(value, bit):
        return move(value, lambda p, z, c: (p, z ^ bit, c))

    def first(value):
        return move(value, lambda p, z, c: (p ^ (1 + c), z, c))

    def second(value):
        return move(value, lambda p, z, c: (p ^ (2 - c), z, c))

    def swap(value):
        return move(value, lambda p, z, c: (p, z, c ^ 1))

    levels, convs, rows, channels = filters.shape
    quarters = filters.reshape(levels, phases, convs * rows // phases, channels)
    swapped = swap(filters)
    gathered = []
    for group in GROUPS:
        part = lax.slice_in_dim(quarters, group[0], group[-1] + 1, axis=0)
        own = lax.dynamic_index_in_dim(part, phase_id, 1, keepdims=False)
        far = across(own, 2)
        column = jnp.stack([far, across(own, 1), across(far, 1)])
        one = first(column)
        pieces = [column, one, second(column), second(one)]
        gathered.append(pieces + [swap(piece) for piece in pieces])
    return [filters, swapped], gathered


def per_device(
    phases,
    dp_count,
    tap_tokens,
    project_weight,
    expand_four,
    expand_two,
    shrink_weight,
    refine_filters,
    head_matrix,
    head_vector,
    tile_slot,
):
    plan = Plan(phases, project_weight.shape[2])
    phase_id = lax.axis_index("phase")
    dp_id = lax.axis_index("dp")
    where = jnp.stack([phase_id, dp_id % 2, dp_id // 2]).astype(jnp.int32)
    if phases == 4 and dp_count == 8 and refine_filters.shape[2] % 32 == 0:
        base, gathered = gather_filters(refine_filters, phases, dp_count)
        upper, finer = base + gathered[0], base + gathered[1]
    else:
        upper = finer = [lax.all_gather(refine_filters, "dp", axis=2, tiled=True)]
    sent = project(plan, phases, where, tap_tokens, project_weight, shrink_weight)
    arrived = [sent[0]] + [
        lax.ppermute(sent[k], "phase", [(s, s ^ k) for s in range(phases)])
        for k in range(1, phases)
    ]
    mine = jnp.stack(arrived)
    other = lax.ppermute(mine, "dp", [(d, d ^ 1) for d in range(dp_count)])
    summed1, patch0 = coarse(plan, where, mine, other, expand_two, upper)
    depth = fine(plan, where, summed1, patch0, head_matrix, head_vector, expand_four, finer)
    depth = depth[:, 0].reshape(4 * plan.block, TILES_DEV, -1)
    depth_tiles = depth.transpose(1, 2, 0).reshape(TILES_DEV, -1)
    slots = phase_id * dp_count * SLOT_DEV + jnp.arange(dp_count * SLOT_DEV, dtype=jnp.int32)
    targets = lax.dynamic_slice(tile_slot, (dp_id, phase_id, 0), (1, 1, TILES_DEV)).reshape(-1)
    matches = (slots[:, None] == targets[None, :]).astype(F32)
    partial = jnp.dot(matches, depth_tiles, precision=lax.Precision.HIGHEST)
    partial = partial.reshape(dp_count, SLOT_DEV, -1)
    portions = lax.all_to_all(partial, "dp", split_axis=0, concat_axis=0, tiled=True)
    return portions.sum(axis=0)


def solution(mesh):
    in_specs = (
        P("phase", "dp", None),
        P("phase", None, None),
        P(),
        P(),
        P(),
        P(None, None, "dp", None),
        P(),
        P(),
        P(),
    )
    out_specs = P(("phase", "dp"), None)
    body = functools.partial(per_device, mesh.shape["phase"], mesh.shape["dp"])
    return jax.shard_map(
        body, mesh=mesh, in_specs=in_specs, out_specs=out_specs, check_vma=False
    )
```

```python
import functools

import jax
import jax.numpy as jnp
from jax import lax
from jax.experimental import pallas as pl
from jax.experimental.pallas import tpu as pltpu
from jax.sharding import PartitionSpec as P

G = 32
TILES_DEV = 8
SLOT_DEV = 6
LEVELS = 4
F32 = jnp.float32
BF16 = jnp.bfloat16
PROJECT_VMEM = 16 * 1024 * 1024
COARSE_VMEM = 16 * 1024 * 1024
FINE_VMEM = 36 * 1024 * 1024


LANES = 128


def take(ref, *at):
    return jnp.concatenate([ref[(i,) + at] for i in range(ref.shape[0])], axis=-1)


def put(ref, value, *at):
    for i in range(ref.shape[0]):
        ref[(i,) + at] = value[..., i * LANES : (i + 1) * LANES]


def dot(lhs, rhs):
    return jnp.dot(lhs, rhs, preferred_element_type=F32)


CHIP_ORDER = (2, 1, 3)
GROUPS = ((2, 3), (0, 1))


class Plan:
    def __init__(self, phases, channels):
        self.phases = phases
        self.ch = channels
        self.half = G // 2
        self.block = G // phases
        self.sent = 2 * self.block
        self.rows1 = 3 * G // 4
        self.cols1 = self.block + self.block // 2
        self.cols0 = self.block + 2
        self.conv_cols = 4 * self.block + 4
        self.conv_rows = 4 * self.half + 16

    def slot_of(self, level):
        return next(g.index(level) for g in GROUPS if level in g)

    def sent_start(self, s):
        return jnp.clip(s * self.block - self.block // 2, 0, G - self.sent)

    def start1(self, s):
        return jnp.clip(s * self.block - self.block // 4, 0, G - self.cols1)

    def start0(self, s):
        return jnp.clip(s * self.block - 1, 0, G - self.cols0)


def project_kernel(plan, phases, where, tokens, weight, shrink, *refs):
    outs, acc_lo, acc_hi = refs[:phases], refs[phases], refs[phases + 1]
    step = pl.program_id(0)
    part = dot(tokens[0], weight[0])
    lanes = acc_lo.shape[1]

    @pl.when(step == 0)
    def _():
        acc_lo[...] = part[:, :lanes]
        acc_hi[...] = part[:, lanes:]

    @pl.when(step > 0)
    def _():
        acc_lo[...] += part[:, :lanes]
        acc_hi[...] += part[:, lanes:]

    last = step == pl.num_programs(0) - 1
    phase = where[0]

    def column(start, size, stride):
        where_rows = pl.ds(start, size, stride=stride)
        return jnp.concatenate([acc_lo[where_rows, :], acc_hi[where_rows, :]], axis=1)

    @pl.when(last & (phase < LEVELS - 1))
    def _():
        for k in range(phases):
            start = plan.sent_start(phase ^ k)
            for j in range(plan.sent):
                outs[k][j * plan.half : (j + 1) * plan.half, :] = column(
                    start + j, plan.half, G
                ).astype(BF16)

    @pl.when(last & (phase == LEVELS - 1))
    def _():
        total = jnp.zeros((plan.half * plan.half // 2, plan.ch), F32)
        for a in range(2):
            for b in range(2):
                tall = jnp.concatenate(
                    [column(a * G + 2 * j + b, plan.half // 2, 2 * G) for j in range(G // 2)],
                    axis=0,
                )
                total += dot(
                    tall.astype(BF16), shrink[(2 * a + b) * plan.ch : (2 * a + b + 1) * plan.ch, :]
                )
        for k in range(phases):
            outs[k][: total.shape[0], :] = total.astype(BF16)
            outs[k][total.shape[0] :, :] = jnp.zeros(
                (outs[k].shape[0] - total.shape[0], plan.ch), BF16
            )


def project(plan, phases, where, tokens, weight, shrink):
    rows, depth = tokens.shape[1:]
    block = min(depth, 512)
    pixels = plan.sent * plan.half
    out = jax.ShapeDtypeStruct((pixels, plan.ch), BF16)
    return pl.pallas_call(
        functools.partial(project_kernel, plan, phases),
        grid_spec=pltpu.PrefetchScalarGridSpec(
            num_scalar_prefetch=1,
            grid=(depth // block,),
            in_specs=[
                pl.BlockSpec((1, rows, block), lambda i, w: (0, 0, i)),
                pl.BlockSpec((1, block, plan.ch), lambda i, w: (0, i, 0)),
                pl.BlockSpec(shrink.shape, lambda i, w: (0, 0)),
            ],
            out_specs=[pl.BlockSpec((pixels, plan.ch), lambda i, w: (0, 0))] * phases,
            scratch_shapes=[pltpu.VMEM((rows, plan.ch // 2), F32)] * 2,
        ),
        out_shape=[out] * phases,
        compiler_params=pltpu.CompilerParams(vmem_limit_bytes=PROJECT_VMEM),
        cost_estimate=pl.CostEstimate(
            flops=2 * rows * depth * plan.ch,
            bytes_accessed=2 * depth * (rows + plan.ch),
            transcendentals=0,
        ),
        name="project",
    )(where, tokens, weight, shrink)


def put_shifted(shifted, col, value):
    count, rows, _ = value.shape
    value = jnp.maximum(value, 0.0)
    at = lax.broadcasted_iota(jnp.int32, value.shape, 1)
    above = jnp.where(at == 0, 0.0, pltpu.roll(value, 1, 1))
    below = jnp.where(at == rows - 1, 0.0, pltpu.roll(value, rows - 1, 1))
    for p, moved in enumerate((above, value, below)):
        shifted[p, pl.ds(col + 1, count)] = moved.astype(BF16)


def clear_edges(shifted):
    shape = shifted.shape
    zeros = jnp.zeros((shape[0], 1) + shape[2:], BF16)
    shifted[:, 0:1] = zeros
    shifted[:, shape[1] - 1 : shape[1]] = zeros


def conv_block(shifted, weight, col, count, rows):
    channels = shifted.shape[3]
    start, size = rows
    patches = [
        shifted[p, pl.ds(col + q, count), pl.ds(start, size), :].reshape(count * size, channels)
        for p in range(3)
        for q in range(3)
    ]
    return dot(jnp.concatenate(patches, axis=1), weight[...]).reshape(count, size, -1)


def loop(count, body):
    if count == 1:
        body(0)
    else:
        lax.fori_loop(0, count, lambda i, c: (body(i), c)[1], 0)


def refine(source, weights, sems, first, second, chunk, out_col, out_count, out_chunk, emit):
    cols, rows = first.shape[1] - 2, first.shape[2]
    clear_edges(first)
    clear_edges(second)
    loop(cols // chunk, lambda i: put_shifted(first, i * chunk, source(i * chunk, chunk)))

    wait_filters(weights, sems, 0)

    def inner(i):
        put_shifted(second, i * chunk, conv_block(first, weights.at[0], i * chunk, chunk, (0, rows)))

    loop(cols // chunk, inner)

    wait_filters(weights, sems, 1)

    def outer(i):
        col = out_col + i * out_chunk
        branch = conv_block(second, weights.at[1], col, out_chunk, (0, rows))
        emit(i * out_chunk, source(col, out_chunk) + branch)

    loop(out_count // out_chunk, outer)


def start_filters(plan, where, filters, level, weights, sems):
    if len(filters) == 1:
        for m in range(2):
            pltpu.make_async_copy(filters[0].at[level, m], weights.at[m], sems.at[m]).start()
        return
    phase, side, chip = where[0], where[1], where[2]
    own, swapped = filters[:2]
    rows = own.shape[2]
    part = rows // 2
    slot = plan.slot_of(level)
    for m in range(2):
        for ref, core in ((own, side), (swapped, 1 - side)):
            at = pl.ds(pl.multiple_of((2 * chip + core) * rows, 16), rows)
            pltpu.make_async_copy(ref.at[level, m], weights.at[m, at], sems.at[m]).start()

    def start_pieces(p):
        for m in range(2):
            for half in range(2):
                quarter = 2 * m + half
                for i, away in enumerate(CHIP_ORDER):
                    for refs, core in ((filters[2:6], side), (filters[6:10], 1 - side)):
                        start = (2 * (chip ^ away) + core) * rows + half * part
                        at = pl.ds(pl.multiple_of(start, 16), part)
                        moved = p ^ quarter
                        if moved in (0, 3):
                            pltpu.make_async_copy(
                                refs[moved].at[i, slot], weights.at[m, at], sems.at[m]
                            ).start()
                            continue
                        for c in range(2):
                            k = moved if c == 0 else 3 - moved

                            @pl.when(core == c)
                            def _(ref=refs[k], at=at, i=i, m=m):
                                pltpu.make_async_copy(
                                    ref.at[i, slot], weights.at[m, at], sems.at[m]
                                ).start()

    for p in range(plan.phases):

        @pl.when(phase == p)
        def _(p=p):
            start_pieces(p)


def wait_filters(weights, sems, m):
    pltpu.make_async_copy(weights.at[m], weights.at[m], sems.at[m]).wait()


def load_patches(plan, patch, mine, other, k, side):
    for ref, at in ((mine, side), (other, 1 - side)):
        patch[:, pl.ds(pl.multiple_of(at * plan.half, plan.half), plan.half), :] = (
            ref[k].astype(F32).reshape(plan.sent, plan.half, plan.ch)
        )


def rounded(value):
    return value.astype(BF16).astype(F32)


COARSE_SCRATCH = 14


def coarse_kernel(plan, where, mine, other, expand_two, *refs):
    count = len(refs) - COARSE_SCRATCH
    filters = refs[:count]
    (
        summed1,
        patch0,
        weight3,
        weight2,
        sems,
        patch,
        map3,
        joined3,
        map2,
        joined2,
        first3,
        second3,
        first2,
        second2,
    ) = refs[count:]
    ch = plan.ch
    phase, side = where[0], where[1]
    for level, weights in ((3, weight3), (2, weight2)):
        start_filters(plan, where, filters, level, weights, sems.at[level])

    row1 = pl.multiple_of(side * (G - plan.rows1), 8)
    load_patches(plan, patch, mine, other, phase, side)
    off = plan.start0(phase) - plan.sent_start(phase)
    tall = patch[pl.ds(off, plan.cols0), pl.ds(row1, plan.rows1), :]
    patch0[...] = tall.reshape(patch0.shape).astype(BF16)

    size3 = G // 2
    quarter = plan.half // 2
    k3 = phase ^ 3
    for ref, at in ((mine, side), (other, 1 - side)):
        map3[:, pl.ds(pl.multiple_of(at * quarter, quarter), quarter), :] = (
            ref[k3, : size3 * quarter, :].astype(F32).reshape(size3, quarter, ch)
        )

    def keep3(col, value):
        joined3[pl.ds(col, value.shape[0])] = rounded(value)

    refine(
        lambda col, n: map3[pl.ds(col, n)],
        weight3,
        sems.at[3],
        first3,
        second3,
        size3,
        0,
        size3,
        size3,
        keep3,
    )

    load_patches(plan, patch, mine, other, phase ^ 2, side)
    from3 = plan.sent_start(phase) // 2
    tall = joined3[pl.ds(from3, plan.sent // 2)]
    for b in range(2):
        for a in range(2):
            put(map2, tall, slice(None), b, pl.ds(a, size3, stride=2), slice(None))
    for j in range(plan.sent):
        at = (j // 2, j % 2)
        put(map2, take(map2, *at) + patch[j], *at)

    def source2(col, n):
        return take(map2, pl.ds(col // 2, n // 2)).reshape(n, G, ch)

    def keep2(col, value):
        joined2[pl.ds(col, value.shape[0])] = rounded(value)

    refine(
        source2, weight2, sems.at[2], first2, second2, plan.sent, 0, plan.sent, plan.sent, keep2
    )

    load_patches(plan, patch, mine, other, phase ^ 1, side)
    off1 = plan.start1(phase) - plan.sent_start(phase)
    tall = patch[pl.ds(off1, plan.cols1), pl.ds(row1, plan.rows1), :]
    lhs = tall.reshape(plan.cols1 * plan.rows1, ch).astype(BF16)
    below = joined2[pl.ds(off1, plan.cols1), pl.ds(row1, plan.rows1), :]
    for a in range(2):
        for b in range(2):
            n = 2 * a + b
            grown = dot(lhs, expand_two[:, n * ch : (n + 1) * ch])
            put(
                summed1,
                grown.reshape(plan.cols1, plan.rows1, ch) + below,
                slice(None),
                b,
                pl.ds(a, plan.rows1, stride=2),
                slice(None),
            )


def shifted_maps(cols, rows, ch):
    return [pltpu.VMEM((3, cols + 2, rows, ch), BF16)] * 2


def coarse(plan, where, mine, other, expand_two, filters):
    ch = plan.ch
    vmem = pl.BlockSpec(memory_space=pltpu.VMEM)
    weights = pltpu.VMEM((2, 9 * ch, ch), BF16)
    size3 = G // 2
    slabs = ch // LANES
    return pl.pallas_call(
        functools.partial(coarse_kernel, plan),
        out_shape=[
            jax.ShapeDtypeStruct((slabs, plan.cols1, 2, 2 * plan.rows1, LANES), F32),
            jax.ShapeDtypeStruct((plan.cols0 * plan.rows1, ch), BF16),
        ],
        in_specs=[pl.BlockSpec(memory_space=pltpu.SMEM), vmem, vmem, vmem]
        + [pl.BlockSpec(memory_space=pl.ANY)] * len(filters),
        out_specs=[vmem, vmem],
        scratch_shapes=[
            weights,
            weights,
            pltpu.SemaphoreType.DMA((LEVELS, 2)),
            pltpu.VMEM((plan.sent, G, ch), F32),
            pltpu.VMEM((size3, size3, ch), F32),
            pltpu.VMEM((size3, size3, ch), F32),
            pltpu.VMEM((slabs, plan.sent // 2, 2, G, LANES), F32),
            pltpu.VMEM((plan.sent, G, ch), F32),
        ]
        + shifted_maps(size3, size3, ch)
        + shifted_maps(plan.sent, G, ch),
        compiler_params=pltpu.CompilerParams(vmem_limit_bytes=COARSE_VMEM),
        cost_estimate=pl.CostEstimate(
            flops=2_000_000_000, bytes_accessed=8_000_000, transcendentals=0
        ),
        name="coarse",
    )(where, mine, other, expand_two, *filters)


FINE_SCRATCH = 12


def fine_kernel(plan, where, summed1, patch0, head, vector, expand_four, *refs):
    count = len(refs) - FINE_SCRATCH
    filters = refs[:count]
    (
        depth,
        weight1,
        weight0,
        sems,
        grow,
        grow_sem,
        joined1,
        map0,
        first1,
        second1,
        first,
        second,
    ) = refs[count:]
    ch = plan.ch
    phase, side = where[0], where[1]
    start_filters(plan, where, filters, 1, weight1, sems.at[1])
    grow_copy = pltpu.make_async_copy(expand_four, grow, grow_sem)
    grow_copy.start()
    start_filters(plan, where, filters, 0, weight0, sems.at[0])

    off0 = 2 * (plan.start0(phase) - plan.start1(phase))

    def source1(col, n):
        return take(summed1, pl.ds(col // 2, n // 2)).reshape(n, 2 * plan.rows1, ch)

    def keep1(col, value):
        value = rounded(value)
        put(
            joined1,
            value.reshape(value.shape[0] // 2, 2, 2 * plan.rows1, ch),
            pl.ds(col // 2, value.shape[0] // 2),
        )

    refine(
        source1,
        weight1,
        sems.at[1],
        first1,
        second1,
        plan.cols1,
        off0,
        2 * plan.cols0,
        plan.cols0,
        keep1,
    )

    grow_copy.wait()
    for a in range(4):
        for b in range(4):
            n = 4 * a + b
            grown = dot(patch0[...], grow[:, n * ch : (n + 1) * ch])
            below = take(
                joined1, slice(None), b // 2, pl.ds(a // 2, plan.rows1, stride=2), slice(None)
            )
            put(
                map0,
                grown.reshape(plan.cols0, plan.rows1, ch) + below,
                slice(None),
                b,
                pl.ds(a, plan.rows1, stride=4),
                slice(None),
            )
    cols, rows, own_rows = plan.conv_cols, plan.conv_rows, 4 * plan.half
    own0 = 4 * (phase * plan.block - plan.start0(phase))
    conv0 = jnp.clip(own0 - 2, 0, 4 * plan.cols0 - cols)
    own = own0 - conv0
    row = pl.multiple_of(side * 16, 16)
    pairs = map0.reshape(ch // LANES, 2 * plan.cols0, 2, 4 * plan.rows1, LANES)
    chunk = cols // 2

    def source0(col, n, start, size):
        at = (pl.ds((conv0 + col) // 2, n // 2), slice(None), pl.ds(start, size), slice(None))
        return take(pairs, *at).reshape(n, size, ch)

    clear_edges(first)
    clear_edges(second)
    loop(9, lambda i: put_shifted(first, i * 4, source0(i * 4, 4, row, rows)))
    wait_filters(weight0, sems.at[0], 0)

    def inner(i):
        put_shifted(
            second, i * chunk, conv_block(first, weight0.at[0], i * chunk, chunk, (0, rows))
        )

    loop(cols // chunk, inner)
    wait_filters(weight0, sems.at[0], 1)
    half_cols = 2 * plan.block

    def outer(i):
        col = own + i * half_cols
        branch = conv_block(second, weight0.at[1], col, half_cols, (row, own_rows))
        summed = source0(col, half_cols, pl.multiple_of(2 * row, 16), own_rows)
        joined = (summed + branch).astype(BF16)
        hidden = lax.dot_general(
            head[...],
            joined.reshape(half_cols * own_rows, ch),
            (((1,), (1,)), ((), ())),
            preferred_element_type=F32,
        )
        hidden = jnp.maximum(hidden, 0.0) * vector[...]
        depth[i] = jnp.broadcast_to(hidden.sum(axis=0, keepdims=True), depth.shape[1:])

    loop(2, outer)


def fine(plan, where, summed1, patch0, head, vector, expand_four, filters):
    ch = plan.ch
    vmem = pl.BlockSpec(memory_space=pltpu.VMEM)
    any_space = pl.BlockSpec(memory_space=pl.ANY)
    own_rows = 4 * plan.half
    slabs = ch // LANES
    weights = pltpu.VMEM((2, 9 * ch, ch), BF16)
    return pl.pallas_call(
        functools.partial(fine_kernel, plan),
        out_shape=jax.ShapeDtypeStruct((2, 8, 2 * plan.block * own_rows), F32),
        in_specs=[pl.BlockSpec(memory_space=pltpu.SMEM), vmem, vmem, vmem, vmem, any_space]
        + [any_space] * len(filters),
        out_specs=vmem,
        scratch_shapes=[
            weights,
            weights,
            pltpu.SemaphoreType.DMA((LEVELS, 2)),
            pltpu.VMEM(expand_four.shape, BF16),
            pltpu.SemaphoreType.DMA,
            pltpu.VMEM((slabs, plan.cols0, 2, 2 * plan.rows1, LANES), F32),
            pltpu.VMEM((slabs, plan.cols0, 4, 4 * plan.rows1, LANES), F32),
        ]
        + shifted_maps(2 * plan.cols1, 2 * plan.rows1, ch)
        + shifted_maps(plan.conv_cols, plan.conv_rows, ch),
        compiler_params=pltpu.CompilerParams(vmem_limit_bytes=FINE_VMEM),
        cost_estimate=pl.CostEstimate(
            flops=8_000_000_000, bytes_accessed=10_000_000, transcendentals=0
        ),
        name="fine",
    )(where, summed1, patch0, head.T, vector[:, None], expand_four, *filters)


def gather_filters(filters, phases, dp_count):
    axes = ("phase", "dp")
    phase_id = lax.axis_index("phase")
    chips = dp_count // 2

    def move(value, to):
        route = []
        for p in range(phases):
            for z in range(chips):
                for c in range(2):
                    q, y, d = to(p, z, c)
                    route.append((p * dp_count + 2 * z + c, q * dp_count + 2 * y + d))
        return lax.ppermute(value, axes, route)

    def across(value, bit):
        return move(value, lambda p, z, c: (p, z ^ bit, c))

    def first(value):
        return move(value, lambda p, z, c: (p ^ (1 + c), z, c))

    def second(value):
        return move(value, lambda p, z, c: (p ^ (2 - c), z, c))

    def swap(value):
        return move(value, lambda p, z, c: (p, z, c ^ 1))

    levels, convs, rows, channels = filters.shape
    part = convs * rows // phases
    quarters = filters.reshape(levels, phases, part, channels)
    swapped = swap(filters)
    gathered = []
    for group in GROUPS:
        own = lax.dynamic_slice(
            quarters, (group[0], phase_id, 0, 0), (len(group), 1, part, channels)
        )[:, 0]
        far = across(own, 2)
        near = across(own, 1)
        column = jnp.stack([far, near, across(far, 1)])
        one = first(column)
        pieces = [column, one, second(column), second(one)]
        gathered.append(pieces + [swap(v) for v in pieces])
    return [filters, swapped], gathered


def by_permutes(phases, dp_count):
    return phases == 4 and dp_count == 8


def per_device(
    phases,
    dp_count,
    tap_tokens,
    project_weight,
    expand_four,
    expand_two,
    shrink_weight,
    refine_filters,
    head_matrix,
    head_vector,
    tile_slot,
):
    plan = Plan(phases, project_weight.shape[2])
    phase_id = lax.axis_index("phase")
    dp_id = lax.axis_index("dp")
    where = jnp.stack([phase_id, dp_id % 2, dp_id // 2]).astype(jnp.int32)
    if by_permutes(phases, dp_count):
        base, gathered = gather_filters(refine_filters, phases, dp_count)
        upper, finer = base + gathered[0], base + gathered[1]
    else:
        upper = finer = [lax.all_gather(refine_filters, "dp", axis=2, tiled=True)]
    sent = project(plan, phases, where, tap_tokens, project_weight, shrink_weight)
    arrived = [sent[0]]
    for k in range(1, phases):
        arrived.append(lax.ppermute(sent[k], "phase", [(s, s ^ k) for s in range(phases)]))
    mine = jnp.stack(arrived)
    other = lax.ppermute(mine, "dp", [(d, d ^ 1) for d in range(dp_count)])
    summed1, patch0 = coarse(plan, where, mine, other, expand_two, upper)
    depth = fine(plan, where, summed1, patch0, head_matrix, head_vector, expand_four, finer)
    depth = depth[:, 0].reshape(4 * plan.block, TILES_DEV, -1)
    depth_tiles = depth.transpose(1, 2, 0).reshape(TILES_DEV, -1)
    slots = phase_id * dp_count * SLOT_DEV + jnp.arange(dp_count * SLOT_DEV, dtype=jnp.int32)
    targets = lax.dynamic_slice(tile_slot, (dp_id, phase_id, 0), (1, 1, TILES_DEV)).reshape(-1)
    matches = (slots[:, None] == targets[None, :]).astype(F32)
    partial = jnp.dot(matches, depth_tiles, precision=lax.Precision.HIGHEST)
    partial = partial.reshape(dp_count, SLOT_DEV, -1)
    portions = lax.all_to_all(partial, "dp", split_axis=0, concat_axis=0, tiled=True)
    return portions.sum(axis=0)


def solution(mesh):
    in_specs = (
        P("phase", "dp", None),
        P("phase", None, None),
        P(),
        P(),
        P(),
        P(None, None, "dp", None),
        P(),
        P(),
        P(),
    )
    out_specs = P(("phase", "dp"), None)
    phases, dp_count = mesh.shape["phase"], mesh.shape["dp"]

    def body(*args):
        return per_device(phases, dp_count, *args)

    return jax.shard_map(
        body, mesh=mesh, in_specs=in_specs, out_specs=out_specs, check_vma=False
    )
```

```python
import functools

import jax
import jax.numpy as jnp
from jax import lax
from jax.experimental import pallas as pl
from jax.experimental.pallas import tpu as pltpu
from jax.sharding import PartitionSpec as P

G = 32
TILES_DEV = 8
SLOT_DEV = 6
LEVELS = 4
F32 = jnp.float32
BF16 = jnp.bfloat16
STACK_VMEM = 4 * 1024 * 1024
PROJECT_VMEM = 12 * 1024 * 1024
COARSE_VMEM = 12 * 1024 * 1024
FINE_VMEM = 32 * 1024 * 1024


LANES = 128


def take(ref, *at):
    return jnp.concatenate([ref[(i,) + at] for i in range(ref.shape[0])], axis=-1)


def put(ref, value, *at):
    for i in range(ref.shape[0]):
        ref[(i,) + at] = value[..., i * LANES : (i + 1) * LANES]


def dot(lhs, rhs):
    return jnp.dot(lhs, rhs, preferred_element_type=F32)


CHIP_ORDER = (2, 1, 3)
GROUPS = ((2, 3), (0, 1))


class Plan:
    def __init__(self, phases, channels):
        self.ch = channels
        self.half = G // 2
        self.block = G // phases
        self.sent = 2 * self.block
        self.rows1 = 3 * G // 4
        self.cols1 = self.block + self.block // 2
        self.cols0 = self.block + 2
        self.conv_cols = 4 * self.block + 4
        self.conv_rows = 4 * self.half + 16

    def slot_of(self, level):
        return next(g.index(level) for g in GROUPS if level in g)

    def sent_start(self, s):
        return jnp.clip(s * self.block - self.block // 2, 0, G - self.sent)

    def start1(self, s):
        return jnp.clip(s * self.block - self.block // 4, 0, G - self.cols1)

    def start0(self, s):
        return jnp.clip(s * self.block - 1, 0, G - self.cols0)


def project_kernel(plan, phases, where, tokens, weight, shrink, *refs):
    outs, acc_lo, acc_hi = refs[:phases], refs[phases], refs[phases + 1]
    lanes = acc_lo.shape[1]
    rows = tokens.shape[1] // 2
    for i in range(2):
        at = pl.ds(i * rows, rows)
        value = dot(tokens[0, at, :], weight[0])
        acc_lo[at, :] = value[:, :lanes]
        acc_hi[at, :] = value[:, lanes:]
    phase = where[0]

    def column(start, size, stride):
        where_rows = pl.ds(start, size, stride=stride)
        return jnp.concatenate([acc_lo[where_rows, :], acc_hi[where_rows, :]], axis=1)

    @pl.when(phase < LEVELS - 1)
    def _():
        for k in range(phases):
            start = plan.sent_start(phase ^ k)
            for j in range(plan.sent):
                outs[k][j * plan.half : (j + 1) * plan.half, :] = column(
                    start + j, plan.half, G
                ).astype(BF16)

    @pl.when(phase == LEVELS - 1)
    def _():
        total = jnp.zeros((plan.half * plan.half // 2, plan.ch), F32)
        for a in range(2):
            for b in range(2):
                tall = jnp.concatenate(
                    [column(a * G + 2 * j + b, plan.half // 2, 2 * G) for j in range(G // 2)],
                    axis=0,
                )
                total += dot(
                    tall.astype(BF16), shrink[(2 * a + b) * plan.ch : (2 * a + b + 1) * plan.ch, :]
                )
        for k in range(phases):
            outs[k][: total.shape[0], :] = total.astype(BF16)
            outs[k][total.shape[0] :, :] = jnp.zeros(
                (outs[k].shape[0] - total.shape[0], plan.ch), BF16
            )


def project(plan, phases, where, tokens, weight, shrink):
    rows, depth = tokens.shape[1:]
    pixels = plan.sent * plan.half
    out = jax.ShapeDtypeStruct((pixels, plan.ch), BF16)
    vmem = pl.BlockSpec(memory_space=pltpu.VMEM)
    return pl.pallas_call(
        functools.partial(project_kernel, plan, phases),
        in_specs=[pl.BlockSpec(memory_space=pltpu.SMEM), vmem, vmem, vmem],
        out_specs=[vmem] * phases,
        scratch_shapes=[pltpu.VMEM((rows, plan.ch // 2), F32)] * 2,
        out_shape=[out] * phases,
        compiler_params=pltpu.CompilerParams(vmem_limit_bytes=PROJECT_VMEM),
        cost_estimate=pl.CostEstimate(
            flops=2 * rows * depth * plan.ch,
            bytes_accessed=2 * depth * (rows + plan.ch),
            transcendentals=0,
        ),
        name="project",
    )(where, tokens, weight, shrink)


def stack_kernel(*refs):
    for i, ref in enumerate(refs[:-1]):
        refs[-1][i] = ref[...]


def stack(values):
    vmem = pl.BlockSpec(memory_space=pltpu.VMEM)
    size = len(values) * values[0].size * values[0].dtype.itemsize
    return pl.pallas_call(
        stack_kernel,
        out_shape=jax.ShapeDtypeStruct((len(values),) + values[0].shape, values[0].dtype),
        in_specs=[vmem] * len(values),
        out_specs=vmem,
        compiler_params=pltpu.CompilerParams(vmem_limit_bytes=STACK_VMEM),
        cost_estimate=pl.CostEstimate(flops=0, bytes_accessed=2 * size, transcendentals=0),
        name="stack",
    )(*values)


def put_shifted(shifted, col, value):
    count, rows, _ = value.shape
    value = jnp.maximum(value, 0.0)
    at = lax.broadcasted_iota(jnp.int32, value.shape, 1)
    above = jnp.where(at == 0, 0.0, pltpu.roll(value, 1, 1))
    below = jnp.where(at == rows - 1, 0.0, pltpu.roll(value, rows - 1, 1))
    for p, moved in enumerate((above, value, below)):
        shifted[p, pl.ds(col + 1, count)] = moved.astype(BF16)


def clear_edges(shifted):
    shape = shifted.shape
    zeros = jnp.zeros((shape[0], 1) + shape[2:], BF16)
    shifted[:, 0:1] = zeros
    shifted[:, shape[1] - 1 : shape[1]] = zeros


def conv_block(shifted, weight, col, count, rows):
    channels = shifted.shape[3]
    start, size = rows
    patches = [
        shifted[p, pl.ds(col + q, count), pl.ds(start, size), :].reshape(count * size, channels)
        for p in range(3)
        for q in range(3)
    ]
    return dot(jnp.concatenate(patches, axis=1), weight[...]).reshape(count, size, -1)


def loop(count, body):
    if count == 1:
        body(0)
    else:
        lax.fori_loop(0, count, lambda i, c: (body(i), c)[1], 0)


def refine(source, wait, weights, first, second, chunk, out_col, out_count, out_chunk, emit):
    cols, rows = first.shape[1] - 2, first.shape[2]
    clear_edges(first)
    clear_edges(second)
    loop(cols // chunk, lambda i: put_shifted(first, i * chunk, source(i * chunk, chunk)))

    wait(0)

    def inner(i):
        put_shifted(second, i * chunk, conv_block(first, weights.at[0], i * chunk, chunk, (0, rows)))

    loop(cols // chunk, inner)

    wait(1)

    def outer(i):
        col = out_col + i * out_chunk
        branch = conv_block(second, weights.at[1], col, out_chunk, (0, rows))
        emit(i * out_chunk, source(col, out_chunk) + branch)

    loop(out_count // out_chunk, outer)


def start_filters(filters, level, weights, sems):
    if len(filters) == 1:
        for m in range(2):
            pltpu.make_async_copy(filters[0].at[level, m], weights.at[m], sems.at[m]).start()


def wait_filters(filters, weights, sems, m):
    if len(filters) == 1:
        pltpu.make_async_copy(filters[0].at[0, m], weights.at[m], sems.at[m]).wait()


def lay_filters(plan, where, filters, level, weights):
    if len(filters) == 1:
        return
    phase, side, chip = where[0], where[1], where[2]
    own, swapped = filters[:2]
    rows = own.shape[2]
    part = rows // 2
    slot = plan.slot_of(level)
    for ref, core in ((own, side), (swapped, 1 - side)):
        at = pl.ds(pl.multiple_of((2 * chip + core) * rows, 16), rows)
        for m in range(2):
            weights[m, at, :] = ref[level, m]
    for refs, core in ((filters[2:6], side), (filters[6:10], 1 - side)):
        for ref, moved in zip(refs, (0, 1 + core, 2 - core, 3)):
            quarter = phase ^ moved
            for i, away in enumerate(CHIP_ORDER):
                start = (2 * (chip ^ away) + core) * rows + (quarter % 2) * part
                at = pl.ds(pl.multiple_of(start, 16), part)
                weights[quarter // 2, at, :] = ref[i, slot]


def filter_specs(filters):
    space = pl.ANY if len(filters) == 1 else pltpu.VMEM
    return [pl.BlockSpec(memory_space=space)] * len(filters)


def load_patches(plan, patch, mine, other, k, side):
    for ref, at in ((mine, side), (other, 1 - side)):
        patch[:, pl.ds(pl.multiple_of(at * plan.half, plan.half), plan.half), :] = (
            ref[k].astype(F32).reshape(plan.sent, plan.half, plan.ch)
        )


def rounded(value):
    return value.astype(BF16).astype(F32)


COARSE_SCRATCH = 14


def coarse_kernel(plan, where, mine, other, expand_two, *refs):
    count = len(refs) - COARSE_SCRATCH
    filters = refs[:count]
    (
        summed1,
        patch0,
        weight3,
        weight2,
        sems,
        patch,
        map3,
        joined3,
        map2,
        joined2,
        first3,
        second3,
        first2,
        second2,
    ) = refs[count:]
    ch = plan.ch
    phase, side = where[0], where[1]
    for level, weights in ((3, weight3), (2, weight2)):
        start_filters(filters, level, weights, sems.at[level])
        lay_filters(plan, where, filters, level, weights)

    row1 = pl.multiple_of(side * (G - plan.rows1), 8)
    load_patches(plan, patch, mine, other, phase, side)
    off = plan.start0(phase) - plan.sent_start(phase)
    tall = patch[pl.ds(off, plan.cols0), pl.ds(row1, plan.rows1), :]
    patch0[...] = tall.reshape(patch0.shape).astype(BF16)

    size3 = G // 2
    quarter = plan.half // 2
    k3 = phase ^ 3
    for ref, at in ((mine, side), (other, 1 - side)):
        map3[:, pl.ds(pl.multiple_of(at * quarter, quarter), quarter), :] = (
            ref[k3, : size3 * quarter, :].astype(F32).reshape(size3, quarter, ch)
        )

    def keep3(col, value):
        joined3[pl.ds(col, value.shape[0])] = rounded(value)

    refine(
        lambda col, n: map3[pl.ds(col, n)],
        lambda m: wait_filters(filters, weight3, sems.at[3], m),
        weight3,
        first3,
        second3,
        size3,
        0,
        size3,
        size3,
        keep3,
    )

    load_patches(plan, patch, mine, other, phase ^ 2, side)
    from3 = plan.sent_start(phase) // 2
    tall = joined3[pl.ds(from3, plan.sent // 2)]
    for b in range(2):
        for a in range(2):
            put(map2, tall, slice(None), b, pl.ds(a, size3, stride=2), slice(None))
    for j in range(plan.sent):
        at = (j // 2, j % 2)
        put(map2, take(map2, *at) + patch[j], *at)

    def source2(col, n):
        return take(map2, pl.ds(col // 2, n // 2)).reshape(n, G, ch)

    def keep2(col, value):
        joined2[pl.ds(col, value.shape[0])] = rounded(value)

    refine(
        source2,
        lambda m: wait_filters(filters, weight2, sems.at[2], m),
        weight2,
        first2,
        second2,
        plan.sent,
        0,
        plan.sent,
        plan.sent,
        keep2,
    )

    load_patches(plan, patch, mine, other, phase ^ 1, side)
    off1 = plan.start1(phase) - plan.sent_start(phase)
    tall = patch[pl.ds(off1, plan.cols1), pl.ds(row1, plan.rows1), :]
    lhs = tall.reshape(plan.cols1 * plan.rows1, ch).astype(BF16)
    below = joined2[pl.ds(off1, plan.cols1), pl.ds(row1, plan.rows1), :]
    for a in range(2):
        for b in range(2):
            n = 2 * a + b
            grown = dot(lhs, expand_two[:, n * ch : (n + 1) * ch])
            put(
                summed1,
                grown.reshape(plan.cols1, plan.rows1, ch) + below,
                slice(None),
                b,
                pl.ds(a, plan.rows1, stride=2),
                slice(None),
            )


def shifted_maps(cols, rows, ch):
    return [pltpu.VMEM((3, cols + 2, rows, ch), BF16)] * 2


def coarse(plan, where, mine, other, expand_two, filters):
    ch = plan.ch
    vmem = pl.BlockSpec(memory_space=pltpu.VMEM)
    weights = pltpu.VMEM((2, 9 * ch, ch), BF16)
    size3 = G // 2
    slabs = ch // LANES
    return pl.pallas_call(
        functools.partial(coarse_kernel, plan),
        out_shape=[
            jax.ShapeDtypeStruct((slabs, plan.cols1, 2, 2 * plan.rows1, LANES), F32),
            jax.ShapeDtypeStruct((plan.cols0 * plan.rows1, ch), BF16),
        ],
        in_specs=[pl.BlockSpec(memory_space=pltpu.SMEM), vmem, vmem, vmem]
        + filter_specs(filters),
        out_specs=[vmem, vmem],
        scratch_shapes=[
            weights,
            weights,
            pltpu.SemaphoreType.DMA((LEVELS, 2)),
            pltpu.VMEM((plan.sent, G, ch), F32),
            pltpu.VMEM((size3, size3, ch), F32),
            pltpu.VMEM((size3, size3, ch), F32),
            pltpu.VMEM((slabs, plan.sent // 2, 2, G, LANES), F32),
            pltpu.VMEM((plan.sent, G, ch), F32),
        ]
        + shifted_maps(size3, size3, ch)
        + shifted_maps(plan.sent, G, ch),
        compiler_params=pltpu.CompilerParams(vmem_limit_bytes=COARSE_VMEM),
        cost_estimate=pl.CostEstimate(
            flops=2_000_000_000, bytes_accessed=8_000_000, transcendentals=0
        ),
        name="coarse",
    )(where, mine, other, expand_two, *filters)


FINE_SCRATCH = 12


def fine_kernel(plan, where, summed1, patch0, head, vector, expand_four, matches, *refs):
    count = len(refs) - FINE_SCRATCH
    filters = refs[:count]
    (
        portions,
        weight1,
        weight0,
        sems,
        joined1,
        map0,
        first1,
        second1,
        first,
        second,
        by_col,
        by_row,
    ) = refs[count:]
    ch = plan.ch
    phase, side = where[0], where[1]
    for level, weights in ((1, weight1), (0, weight0)):
        start_filters(filters, level, weights, sems.at[level])
        lay_filters(plan, where, filters, level, weights)

    off0 = 2 * (plan.start0(phase) - plan.start1(phase))

    def source1(col, n):
        return take(summed1, pl.ds(col // 2, n // 2)).reshape(n, 2 * plan.rows1, ch)

    def keep1(col, value):
        value = rounded(value)
        put(
            joined1,
            value.reshape(value.shape[0] // 2, 2, 2 * plan.rows1, ch),
            pl.ds(col // 2, value.shape[0] // 2),
        )

    refine(
        source1,
        lambda m: wait_filters(filters, weight1, sems.at[1], m),
        weight1,
        first1,
        second1,
        plan.cols1,
        off0,
        2 * plan.cols0,
        plan.cols0,
        keep1,
    )

    for a in range(4):
        for b in range(4):
            n = 4 * a + b
            grown = dot(patch0[...], expand_four[:, n * ch : (n + 1) * ch])
            below = take(
                joined1, slice(None), b // 2, pl.ds(a // 2, plan.rows1, stride=2), slice(None)
            )
            put(
                map0,
                grown.reshape(plan.cols0, plan.rows1, ch) + below,
                slice(None),
                b,
                pl.ds(a, plan.rows1, stride=4),
                slice(None),
            )
    cols, rows, own_rows = plan.conv_cols, plan.conv_rows, 4 * plan.half
    own0 = 4 * (phase * plan.block - plan.start0(phase))
    conv0 = jnp.clip(own0 - 2, 0, 4 * plan.cols0 - cols)
    own = own0 - conv0
    row = pl.multiple_of(side * 16, 16)
    pairs = map0.reshape(ch // LANES, 2 * plan.cols0, 2, 4 * plan.rows1, LANES)
    chunk = cols // 2

    def source0(col, n, start, size):
        at = (pl.ds((conv0 + col) // 2, n // 2), slice(None), pl.ds(start, size), slice(None))
        return take(pairs, *at).reshape(n, size, ch)

    clear_edges(first)
    clear_edges(second)
    loop(9, lambda i: put_shifted(first, i * 4, source0(i * 4, 4, row, rows)))
    wait_filters(filters, weight0, sems.at[0], 0)

    def inner(i):
        put_shifted(
            second, i * chunk, conv_block(first, weight0.at[0], i * chunk, chunk, (0, rows))
        )

    loop(cols // chunk, inner)
    wait_filters(filters, weight0, sems.at[0], 1)
    half_cols = 2 * plan.block
    hidden_size = head.shape[1]
    scale = jnp.broadcast_to(vector[...], (hidden_size, hidden_size)).T[:, :1]

    def outer(i):
        col = own + i * half_cols
        branch = conv_block(second, weight0.at[1], col, half_cols, (row, own_rows))
        summed = source0(col, half_cols, pl.multiple_of(2 * row, 16), own_rows)
        joined = (summed + branch).astype(BF16)
        hidden = lax.dot_general(
            head[...],
            joined.reshape(half_cols * own_rows, ch),
            (((0,), (1,)), ((), ())),
            preferred_element_type=F32,
        )
        depth = (jnp.maximum(hidden, 0.0) * scale).sum(axis=0, keepdims=True)
        for j in range(half_cols):
            by_col[pl.ds(i * half_cols + j, 1), :own_rows] = depth[
                :, j * own_rows : (j + 1) * own_rows
            ]

    loop(2, outer)

    by_row[...] = by_col[...].T
    tile_rows = own_rows // TILES_DEV
    tiles = jnp.concatenate(
        [
            by_row[pl.ds(i, TILES_DEV, stride=tile_rows), :][:, : 2 * half_cols]
            for i in range(tile_rows)
        ],
        axis=1,
    )

    def add_tiles(d):
        chosen = matches[d]
        total = chosen[:, 0:1] * tiles[0:1]
        for j in range(1, TILES_DEV):
            total += chosen[:, j : j + 1] * tiles[j : j + 1]
        portions[d] = total

    for d in range(portions.shape[0]):
        add_tiles(d)


def fine(plan, where, summed1, patch0, head, vector, expand_four, matches, filters):
    ch = plan.ch
    vmem = pl.BlockSpec(memory_space=pltpu.VMEM)
    slabs = ch // LANES
    pixels = 16 * plan.block * plan.half // TILES_DEV
    weights = pltpu.VMEM((2, 9 * ch, ch), BF16)
    return pl.pallas_call(
        functools.partial(fine_kernel, plan),
        out_shape=jax.ShapeDtypeStruct(matches.shape[:2] + (pixels,), F32),
        in_specs=[pl.BlockSpec(memory_space=pltpu.SMEM)] + [vmem] * 6 + filter_specs(filters),
        out_specs=vmem,
        scratch_shapes=[
            weights,
            weights,
            pltpu.SemaphoreType.DMA((LEVELS, 2)),
            pltpu.VMEM((slabs, plan.cols0, 2, 2 * plan.rows1, LANES), F32),
            pltpu.VMEM((slabs, plan.cols0, 4, 4 * plan.rows1, LANES), F32),
        ]
        + shifted_maps(2 * plan.cols1, 2 * plan.rows1, ch)
        + shifted_maps(plan.conv_cols, plan.conv_rows, ch)
        + [pltpu.VMEM((LANES, LANES), F32)] * 2,
        compiler_params=pltpu.CompilerParams(vmem_limit_bytes=FINE_VMEM),
        cost_estimate=pl.CostEstimate(
            flops=8_000_000_000, bytes_accessed=10_000_000, transcendentals=0
        ),
        name="fine",
    )(where, summed1, patch0, head, vector[None, :], expand_four, matches, *filters)


def gather_filters(filters, phase_id, phases, dp_count):
    axes = ("phase", "dp")
    chips = dp_count // 2

    def move(value, to):
        route = []
        for p in range(phases):
            for z in range(chips):
                for c in range(2):
                    q, y, d = to(p, z, c)
                    route.append((p * dp_count + 2 * z + c, q * dp_count + 2 * y + d))
        return lax.ppermute(value, axes, route)

    def across(value, bit):
        return move(value, lambda p, z, c: (p, z ^ bit, c))

    def first(value):
        return move(value, lambda p, z, c: (p ^ (1 + c), z, c))

    def second(value):
        return move(value, lambda p, z, c: (p ^ (2 - c), z, c))

    def swap(value):
        return move(value, lambda p, z, c: (p, z, c ^ 1))

    levels, convs, rows, channels = filters.shape
    part = convs * rows // phases
    quarters = filters.reshape(levels, phases, part, channels)
    swapped = swap(filters)
    gathered = []
    for group in GROUPS:
        own = lax.dynamic_slice(
            quarters, (group[0], phase_id, 0, 0), (len(group), 1, part, channels)
        )[:, 0]
        far = across(own, 2)
        near = across(own, 1)
        column = stack([far, near, across(far, 1)])
        one = first(column)
        pieces = [column, one, second(column), second(one)]
        gathered.append(pieces + [swap(v) for v in pieces])
    return [filters, swapped], gathered


def by_permutes(phases, dp_count):
    return phases == 4 and dp_count == 8


def per_device(
    phases,
    dp_count,
    tap_tokens,
    project_weight,
    expand_four,
    expand_two,
    shrink_weight,
    refine_filters,
    head_matrix,
    head_vector,
    tile_slot,
):
    plan = Plan(phases, project_weight.shape[2])
    phase_id = lax.axis_index("phase")
    dp_id = lax.axis_index("dp")
    where = jnp.stack([phase_id, dp_id % 2, dp_id // 2]).astype(jnp.int32)
    slots = phase_id * dp_count * SLOT_DEV + jnp.arange(dp_count * SLOT_DEV, dtype=jnp.int32)
    targets = lax.dynamic_slice(tile_slot, (dp_id, phase_id, 0), (1, 1, TILES_DEV))
    matches = (slots.reshape(dp_count, SLOT_DEV, 1) == targets).astype(F32)
    where, matches = lax.optimization_barrier((where, matches))
    phase_id = where[0]
    if by_permutes(phases, dp_count):
        base, gathered = gather_filters(refine_filters, phase_id, phases, dp_count)
        upper, finer = base + gathered[0], base + gathered[1]
    else:
        upper = finer = [lax.all_gather(refine_filters, "dp", axis=2, tiled=True)]
    sent = project(plan, phases, where, tap_tokens, project_weight, shrink_weight)
    arrived = [sent[0]]
    for k in range(1, phases):
        arrived.append(lax.ppermute(sent[k], "phase", [(s, s ^ k) for s in range(phases)]))
    mine = stack(arrived)
    other = lax.ppermute(mine, "dp", [(d, d ^ 1) for d in range(dp_count)])
    summed1, patch0 = coarse(plan, where, mine, other, expand_two, upper)
    partial = fine(
        plan, where, summed1, patch0, head_matrix, head_vector, expand_four, matches, finer
    )
    portions = lax.all_to_all(partial, "dp", split_axis=0, concat_axis=0, tiled=True)
    return portions.sum(axis=0)


def solution(mesh):
    in_specs = (
        P("phase", "dp", None),
        P("phase", None, None),
        P(),
        P(),
        P(),
        P(None, None, "dp", None),
        P(),
        P(),
        P(),
    )
    out_specs = P(("phase", "dp"), None)
    phases, dp_count = mesh.shape["phase"], mesh.shape["dp"]

    def body(*args):
        return per_device(phases, dp_count, *args)

    return jax.shard_map(
        body, mesh=mesh, in_specs=in_specs, out_specs=out_specs, check_vma=False
    )
```

```python
import functools

import jax
import jax.numpy as jnp
from jax import lax
from jax.experimental import pallas as pl
from jax.experimental.pallas import tpu as pltpu
from jax.sharding import PartitionSpec as P

G = 32
TILES_DEV = 8
SLOT_DEV = 6
LEVELS = 4
F32 = jnp.float32
BF16 = jnp.bfloat16
STACK_VMEM = 4 * 1024 * 1024
PROJECT_VMEM = 60 * 1024 * 1024
PROJECT_STEPS = 8
COARSE_VMEM = 12 * 1024 * 1024
FINE_VMEM = 32 * 1024 * 1024


LANES = 128


def take(ref, *at):
    return jnp.concatenate([ref[(i,) + at] for i in range(ref.shape[0])], axis=-1)


def put(ref, value, *at):
    for i in range(ref.shape[0]):
        ref[(i,) + at] = value[..., i * LANES : (i + 1) * LANES]


def dot(lhs, rhs):
    return jnp.dot(lhs, rhs, preferred_element_type=F32)


CHIP_ORDER = (2, 1, 3)
GROUPS = ((2, 3), (0, 1))


class Plan:
    def __init__(self, phases, channels):
        self.ch = channels
        self.half = G // 2
        self.block = G // phases
        self.sent = 2 * self.block
        self.rows1 = 3 * G // 4
        self.cols1 = self.block + self.block // 2
        self.cols0 = self.block + 2
        self.conv_cols = 4 * self.block + 4
        self.conv_rows = 4 * self.half + 16

    def slot_of(self, level):
        return next(g.index(level) for g in GROUPS if level in g)

    def sent_start(self, s):
        return jnp.clip(s * self.block - self.block // 2, 0, G - self.sent)

    def start1(self, s):
        return jnp.clip(s * self.block - self.block // 4, 0, G - self.cols1)

    def start0(self, s):
        return jnp.clip(s * self.block - 1, 0, G - self.cols0)


def project_kernel(plan, phases, where, tokens_hbm, weight_hbm, shrink_hbm, *refs):
    outs = refs[:phases]
    acc_lo, acc_hi, tokens, weight, shrink, sems, shrink_sem = refs[phases:]
    lanes = acc_lo.shape[1]
    depth = tokens.shape[1]
    size = depth // PROJECT_STEPS
    copies = []
    for i in range(PROJECT_STEPS):
        at = pl.ds(i * size, size)
        pair = (
            pltpu.make_async_copy(weight_hbm.at[0, at], weight.at[at], sems.at[0, i]),
            pltpu.make_async_copy(tokens_hbm.at[0, :, at], tokens.at[:, at], sems.at[1, i]),
        )
        for copy in pair:
            copy.start()
        copies.append(pair)
    shrink_copy = pltpu.make_async_copy(shrink_hbm, shrink, shrink_sem)
    shrink_copy.start()
    for i, pair in enumerate(copies):
        for copy in pair:
            copy.wait()
        at = slice(i * size, (i + 1) * size)
        part = dot(tokens[:, at], weight[at, :])
        if i == 0:
            acc_lo[...] = part[:, :lanes]
            acc_hi[...] = part[:, lanes:]
        else:
            acc_lo[...] += part[:, :lanes]
            acc_hi[...] += part[:, lanes:]
    shrink_copy.wait()
    phase = where[0]

    def column(start, size, stride):
        where_rows = pl.ds(start, size, stride=stride)
        return jnp.concatenate([acc_lo[where_rows, :], acc_hi[where_rows, :]], axis=1)

    @pl.when(phase < LEVELS - 1)
    def _():
        for k in range(phases):
            start = plan.sent_start(phase ^ k)
            for j in range(plan.sent):
                outs[k][j * plan.half : (j + 1) * plan.half, :] = column(
                    start + j, plan.half, G
                ).astype(BF16)

    @pl.when(phase == LEVELS - 1)
    def _():
        total = jnp.zeros((plan.half * plan.half // 2, plan.ch), F32)
        for a in range(2):
            for b in range(2):
                tall = jnp.concatenate(
                    [column(a * G + 2 * j + b, plan.half // 2, 2 * G) for j in range(G // 2)],
                    axis=0,
                )
                total += dot(
                    tall.astype(BF16), shrink[(2 * a + b) * plan.ch : (2 * a + b + 1) * plan.ch, :]
                )
        for k in range(phases):
            outs[k][: total.shape[0], :] = total.astype(BF16)
            outs[k][total.shape[0] :, :] = jnp.zeros(
                (outs[k].shape[0] - total.shape[0], plan.ch), BF16
            )


def project(plan, phases, where, tokens, weight, shrink):
    rows, depth = tokens.shape[1:]
    pixels = plan.sent * plan.half
    hbm = pl.BlockSpec(memory_space=pltpu.HBM)
    out = jax.ShapeDtypeStruct((pixels, plan.ch), BF16)
    vmem = pl.BlockSpec(memory_space=pltpu.VMEM)
    return pl.pallas_call(
        functools.partial(project_kernel, plan, phases),
        in_specs=[pl.BlockSpec(memory_space=pltpu.SMEM), hbm, hbm, hbm],
        out_specs=[vmem] * phases,
        scratch_shapes=[pltpu.VMEM((rows, plan.ch // 2), F32)] * 2
        + [
            pltpu.VMEM((rows, depth), BF16),
            pltpu.VMEM((depth, plan.ch), BF16),
            pltpu.VMEM(shrink.shape, BF16),
            pltpu.SemaphoreType.DMA((2, PROJECT_STEPS)),
            pltpu.SemaphoreType.DMA,
        ],
        out_shape=[out] * phases,
        compiler_params=pltpu.CompilerParams(vmem_limit_bytes=PROJECT_VMEM),
        cost_estimate=pl.CostEstimate(
            flops=2 * rows * depth * plan.ch,
            bytes_accessed=2 * depth * (rows + plan.ch),
            transcendentals=0,
        ),
        name="project",
    )(where, tokens, weight, shrink)


def stack_kernel(*refs):
    for i, ref in enumerate(refs[:-1]):
        refs[-1][i] = ref[...]


def stack(values):
    vmem = pl.BlockSpec(memory_space=pltpu.VMEM)
    size = len(values) * values[0].size * values[0].dtype.itemsize
    return pl.pallas_call(
        stack_kernel,
        out_shape=jax.ShapeDtypeStruct((len(values),) + values[0].shape, values[0].dtype),
        in_specs=[vmem] * len(values),
        out_specs=vmem,
        compiler_params=pltpu.CompilerParams(vmem_limit_bytes=STACK_VMEM),
        cost_estimate=pl.CostEstimate(flops=0, bytes_accessed=2 * size, transcendentals=0),
        name="stack",
    )(*values)


def put_shifted(shifted, col, value):
    count, rows, _ = value.shape
    value = jnp.maximum(value, 0.0)
    at = lax.broadcasted_iota(jnp.int32, value.shape, 1)
    above = jnp.where(at == 0, 0.0, pltpu.roll(value, 1, 1))
    below = jnp.where(at == rows - 1, 0.0, pltpu.roll(value, rows - 1, 1))
    for p, moved in enumerate((above, value, below)):
        shifted[p, pl.ds(col + 1, count)] = moved.astype(BF16)


def clear_edges(shifted):
    shape = shifted.shape
    zeros = jnp.zeros((shape[0], 1) + shape[2:], BF16)
    shifted[:, 0:1] = zeros
    shifted[:, shape[1] - 1 : shape[1]] = zeros


def conv_block(shifted, weight, col, count, rows):
    channels = shifted.shape[3]
    start, size = rows
    patches = [
        shifted[p, pl.ds(col + q, count), pl.ds(start, size), :].reshape(count * size, channels)
        for p in range(3)
        for q in range(3)
    ]
    return dot(jnp.concatenate(patches, axis=1), weight[...]).reshape(count, size, -1)


def loop(count, body):
    if count == 1:
        body(0)
    else:
        lax.fori_loop(0, count, lambda i, c: (body(i), c)[1], 0)


def refine(source, wait, weights, first, second, chunk, out_col, out_count, out_chunk, emit):
    cols, rows = first.shape[1] - 2, first.shape[2]
    clear_edges(first)
    clear_edges(second)
    loop(cols // chunk, lambda i: put_shifted(first, i * chunk, source(i * chunk, chunk)))

    wait(0)

    def inner(i):
        put_shifted(second, i * chunk, conv_block(first, weights.at[0], i * chunk, chunk, (0, rows)))

    loop(cols // chunk, inner)

    wait(1)

    def outer(i):
        col = out_col + i * out_chunk
        branch = conv_block(second, weights.at[1], col, out_chunk, (0, rows))
        emit(i * out_chunk, source(col, out_chunk) + branch)

    loop(out_count // out_chunk, outer)


def start_filters(filters, level, weights, sems):
    if len(filters) == 1:
        for m in range(2):
            pltpu.make_async_copy(filters[0].at[level, m], weights.at[m], sems.at[m]).start()


def wait_filters(filters, weights, sems, m):
    if len(filters) == 1:
        pltpu.make_async_copy(filters[0].at[0, m], weights.at[m], sems.at[m]).wait()


def lay_filters(plan, where, filters, level, weights):
    if len(filters) == 1:
        return
    phase, side, chip = where[0], where[1], where[2]
    own, swapped = filters[:2]
    rows = own.shape[2]
    part = rows // 2
    slot = plan.slot_of(level)
    for ref, core in ((own, side), (swapped, 1 - side)):
        at = pl.ds(pl.multiple_of((2 * chip + core) * rows, 16), rows)
        for m in range(2):
            weights[m, at, :] = ref[level, m]
    if len(filters) == 6:
        for refs, core in ((filters[2:4], side), (filters[4:6], 1 - side)):
            held = (phase >> core) % 2
            for ref, m in zip(refs, (held, 1 - held)):
                for i, away in enumerate(CHIP_ORDER):
                    start = (2 * (chip ^ away) + core) * rows
                    weights[m, pl.ds(pl.multiple_of(start, 16), rows), :] = ref[i, slot]
        return
    for refs, core in ((filters[2:6], side), (filters[6:10], 1 - side)):
        for ref, moved in zip(refs, (0, 1 + core, 2 - core, 3)):
            quarter = phase ^ moved
            for i, away in enumerate(CHIP_ORDER):
                start = (2 * (chip ^ away) + core) * rows + (quarter % 2) * part
                at = pl.ds(pl.multiple_of(start, 16), part)
                weights[quarter // 2, at, :] = ref[i, slot]


def filter_specs(filters):
    space = pl.ANY if len(filters) == 1 else pltpu.VMEM
    return [pl.BlockSpec(memory_space=space)] * len(filters)


def load_patches(plan, patch, mine, other, k, side):
    for ref, at in ((mine, side), (other, 1 - side)):
        patch[:, pl.ds(pl.multiple_of(at * plan.half, plan.half), plan.half), :] = (
            ref[k].astype(F32).reshape(plan.sent, plan.half, plan.ch)
        )


def rounded(value):
    return value.astype(BF16).astype(F32)


COARSE_SCRATCH = 14


def coarse_kernel(plan, where, mine, other, expand_two, *refs):
    count = len(refs) - COARSE_SCRATCH
    filters = refs[:count]
    (
        summed1,
        patch0,
        weight3,
        weight2,
        sems,
        patch,
        map3,
        joined3,
        map2,
        joined2,
        first3,
        second3,
        first2,
        second2,
    ) = refs[count:]
    ch = plan.ch
    phase, side = where[0], where[1]
    for level, weights in ((3, weight3), (2, weight2)):
        start_filters(filters, level, weights, sems.at[level])
        lay_filters(plan, where, filters, level, weights)

    row1 = pl.multiple_of(side * (G - plan.rows1), 8)
    load_patches(plan, patch, mine, other, phase, side)
    off = plan.start0(phase) - plan.sent_start(phase)
    tall = patch[pl.ds(off, plan.cols0), pl.ds(row1, plan.rows1), :]
    patch0[...] = tall.reshape(patch0.shape).astype(BF16)

    size3 = G // 2
    quarter = plan.half // 2
    k3 = phase ^ 3
    for ref, at in ((mine, side), (other, 1 - side)):
        map3[:, pl.ds(pl.multiple_of(at * quarter, quarter), quarter), :] = (
            ref[k3, : size3 * quarter, :].astype(F32).reshape(size3, quarter, ch)
        )

    def keep3(col, value):
        joined3[pl.ds(col, value.shape[0])] = rounded(value)

    refine(
        lambda col, n: map3[pl.ds(col, n)],
        lambda m: wait_filters(filters, weight3, sems.at[3], m),
        weight3,
        first3,
        second3,
        size3,
        0,
        size3,
        size3,
        keep3,
    )

    load_patches(plan, patch, mine, other, phase ^ 2, side)
    from3 = plan.sent_start(phase) // 2
    tall = joined3[pl.ds(from3, plan.sent // 2)]
    for b in range(2):
        for a in range(2):
            put(map2, tall, slice(None), b, pl.ds(a, size3, stride=2), slice(None))
    for j in range(plan.sent):
        at = (j // 2, j % 2)
        put(map2, take(map2, *at) + patch[j], *at)

    def source2(col, n):
        return take(map2, pl.ds(col // 2, n // 2)).reshape(n, G, ch)

    def keep2(col, value):
        joined2[pl.ds(col, value.shape[0])] = rounded(value)

    refine(
        source2,
        lambda m: wait_filters(filters, weight2, sems.at[2], m),
        weight2,
        first2,
        second2,
        plan.sent,
        0,
        plan.sent,
        plan.sent,
        keep2,
    )

    load_patches(plan, patch, mine, other, phase ^ 1, side)
    off1 = plan.start1(phase) - plan.sent_start(phase)
    tall = patch[pl.ds(off1, plan.cols1), pl.ds(row1, plan.rows1), :]
    lhs = tall.reshape(plan.cols1 * plan.rows1, ch).astype(BF16)
    below = joined2[pl.ds(off1, plan.cols1), pl.ds(row1, plan.rows1), :]
    for a in range(2):
        for b in range(2):
            n = 2 * a + b
            grown = dot(lhs, expand_two[:, n * ch : (n + 1) * ch])
            put(
                summed1,
                grown.reshape(plan.cols1, plan.rows1, ch) + below,
                slice(None),
                b,
                pl.ds(a, plan.rows1, stride=2),
                slice(None),
            )


def shifted_maps(cols, rows, ch):
    return [pltpu.VMEM((3, cols + 2, rows, ch), BF16)] * 2


def coarse(plan, where, mine, other, expand_two, filters):
    ch = plan.ch
    vmem = pl.BlockSpec(memory_space=pltpu.VMEM)
    weights = pltpu.VMEM((2, 9 * ch, ch), BF16)
    size3 = G // 2
    slabs = ch // LANES
    return pl.pallas_call(
        functools.partial(coarse_kernel, plan),
        out_shape=[
            jax.ShapeDtypeStruct((slabs, plan.cols1, 2, 2 * plan.rows1, LANES), F32),
            jax.ShapeDtypeStruct((plan.cols0 * plan.rows1, ch), BF16),
        ],
        in_specs=[pl.BlockSpec(memory_space=pltpu.SMEM), vmem, vmem, vmem]
        + filter_specs(filters),
        out_specs=[vmem, vmem],
        scratch_shapes=[
            weights,
            weights,
            pltpu.SemaphoreType.DMA((LEVELS, 2)),
            pltpu.VMEM((plan.sent, G, ch), F32),
            pltpu.VMEM((size3, size3, ch), F32),
            pltpu.VMEM((size3, size3, ch), F32),
            pltpu.VMEM((slabs, plan.sent // 2, 2, G, LANES), F32),
            pltpu.VMEM((plan.sent, G, ch), F32),
        ]
        + shifted_maps(size3, size3, ch)
        + shifted_maps(plan.sent, G, ch),
        compiler_params=pltpu.CompilerParams(vmem_limit_bytes=COARSE_VMEM),
        cost_estimate=pl.CostEstimate(
            flops=2_000_000_000, bytes_accessed=8_000_000, transcendentals=0
        ),
        name="coarse",
    )(where, mine, other, expand_two, *filters)


FINE_SCRATCH = 12


def fine_kernel(plan, where, summed1, patch0, head, vector, expand_four, matches, *refs):
    count = len(refs) - FINE_SCRATCH
    filters = refs[:count]
    (
        portions,
        weight1,
        weight0,
        sems,
        joined1,
        map0,
        first1,
        second1,
        first,
        second,
        by_col,
        by_row,
    ) = refs[count:]
    ch = plan.ch
    phase, side = where[0], where[1]
    for level, weights in ((1, weight1), (0, weight0)):
        start_filters(filters, level, weights, sems.at[level])
        lay_filters(plan, where, filters, level, weights)

    off0 = 2 * (plan.start0(phase) - plan.start1(phase))

    def source1(col, n):
        return take(summed1, pl.ds(col // 2, n // 2)).reshape(n, 2 * plan.rows1, ch)

    def keep1(col, value):
        value = rounded(value)
        put(
            joined1,
            value.reshape(value.shape[0] // 2, 2, 2 * plan.rows1, ch),
            pl.ds(col // 2, value.shape[0] // 2),
        )

    refine(
        source1,
        lambda m: wait_filters(filters, weight1, sems.at[1], m),
        weight1,
        first1,
        second1,
        plan.cols1,
        off0,
        2 * plan.cols0,
        plan.cols0,
        keep1,
    )

    for a in range(4):
        for b in range(4):
            n = 4 * a + b
            grown = dot(patch0[...], expand_four[:, n * ch : (n + 1) * ch])
            below = take(
                joined1, slice(None), b // 2, pl.ds(a // 2, plan.rows1, stride=2), slice(None)
            )
            put(
                map0,
                grown.reshape(plan.cols0, plan.rows1, ch) + below,
                slice(None),
                b,
                pl.ds(a, plan.rows1, stride=4),
                slice(None),
            )
    cols, rows, own_rows = plan.conv_cols, plan.conv_rows, 4 * plan.half
    own0 = 4 * (phase * plan.block - plan.start0(phase))
    conv0 = jnp.clip(own0 - 2, 0, 4 * plan.cols0 - cols)
    own = own0 - conv0
    row = pl.multiple_of(side * 16, 16)
    pairs = map0.reshape(ch // LANES, 2 * plan.cols0, 2, 4 * plan.rows1, LANES)
    chunk = cols // 2

    def source0(col, n, start, size):
        at = (pl.ds((conv0 + col) // 2, n // 2), slice(None), pl.ds(start, size), slice(None))
        return take(pairs, *at).reshape(n, size, ch)

    clear_edges(first)
    clear_edges(second)
    loop(9, lambda i: put_shifted(first, i * 4, source0(i * 4, 4, row, rows)))
    wait_filters(filters, weight0, sems.at[0], 0)

    def inner(i):
        put_shifted(
            second, i * chunk, conv_block(first, weight0.at[0], i * chunk, chunk, (0, rows))
        )

    loop(cols // chunk, inner)
    wait_filters(filters, weight0, sems.at[0], 1)
    half_cols = 2 * plan.block
    hidden_size = head.shape[1]
    scale = jnp.broadcast_to(vector[...], (hidden_size, hidden_size)).T[:, :1]

    def outer(i):
        col = own + i * half_cols
        branch = conv_block(second, weight0.at[1], col, half_cols, (row, own_rows))
        summed = source0(col, half_cols, pl.multiple_of(2 * row, 16), own_rows)
        joined = (summed + branch).astype(BF16)
        hidden = lax.dot_general(
            head[...],
            joined.reshape(half_cols * own_rows, ch),
            (((0,), (1,)), ((), ())),
            preferred_element_type=F32,
        )
        depth = (jnp.maximum(hidden, 0.0) * scale).sum(axis=0, keepdims=True)
        for j in range(half_cols):
            by_col[pl.ds(i * half_cols + j, 1), :own_rows] = depth[
                :, j * own_rows : (j + 1) * own_rows
            ]

    loop(2, outer)

    by_row[...] = by_col[...].T
    tile_rows = own_rows // TILES_DEV
    tiles = jnp.concatenate(
        [
            by_row[pl.ds(i, TILES_DEV, stride=tile_rows), :][:, : 2 * half_cols]
            for i in range(tile_rows)
        ],
        axis=1,
    )

    def add_tiles(d):
        chosen = matches[d]
        total = chosen[:, 0:1] * tiles[0:1]
        for j in range(1, TILES_DEV):
            total += chosen[:, j : j + 1] * tiles[j : j + 1]
        portions[d] = total

    for d in range(portions.shape[0]):
        add_tiles(d)


def fine(plan, where, summed1, patch0, head, vector, expand_four, matches, filters):
    ch = plan.ch
    vmem = pl.BlockSpec(memory_space=pltpu.VMEM)
    slabs = ch // LANES
    pixels = 16 * plan.block * plan.half // TILES_DEV
    weights = pltpu.VMEM((2, 9 * ch, ch), BF16)
    return pl.pallas_call(
        functools.partial(fine_kernel, plan),
        out_shape=jax.ShapeDtypeStruct(matches.shape[:2] + (pixels,), F32),
        in_specs=[pl.BlockSpec(memory_space=pltpu.SMEM)] + [vmem] * 6 + filter_specs(filters),
        out_specs=vmem,
        scratch_shapes=[
            weights,
            weights,
            pltpu.SemaphoreType.DMA((LEVELS, 2)),
            pltpu.VMEM((slabs, plan.cols0, 2, 2 * plan.rows1, LANES), F32),
            pltpu.VMEM((slabs, plan.cols0, 4, 4 * plan.rows1, LANES), F32),
        ]
        + shifted_maps(2 * plan.cols1, 2 * plan.rows1, ch)
        + shifted_maps(plan.conv_cols, plan.conv_rows, ch)
        + [pltpu.VMEM((LANES, LANES), F32)] * 2,
        compiler_params=pltpu.CompilerParams(vmem_limit_bytes=FINE_VMEM),
        cost_estimate=pl.CostEstimate(
            flops=8_000_000_000, bytes_accessed=10_000_000, transcendentals=0
        ),
        name="fine",
    )(where, summed1, patch0, head, vector[None, :], expand_four, matches, *filters)


def gather_filters(filters, phase_id, held, phases, dp_count):
    axes = ("phase", "dp")
    chips = dp_count // 2

    def move(value, to):
        route = []
        for p in range(phases):
            for z in range(chips):
                for c in range(2):
                    q, y, d = to(p, z, c)
                    route.append((p * dp_count + 2 * z + c, q * dp_count + 2 * y + d))
        return lax.ppermute(value, axes, route)

    def across(value, bit):
        return move(value, lambda p, z, c: (p, z ^ bit, c))

    def first(value):
        return move(value, lambda p, z, c: (p ^ (1 + c), z, c))

    def second(value):
        return move(value, lambda p, z, c: (p ^ (2 - c), z, c))

    def swap(value):
        return move(value, lambda p, z, c: (p, z, c ^ 1))

    levels, convs, rows, channels = filters.shape
    part = convs * rows // phases
    quarters = filters.reshape(levels, phases, part, channels)
    swapped = swap(filters)
    gathered = []
    for n, group in enumerate(GROUPS):
        if n == 0:
            source, chosen = quarters, phase_id
        else:
            source, chosen = filters, held
        own = lax.dynamic_slice(
            source, (group[0], chosen, 0, 0), (len(group), 1) + source.shape[2:]
        )[:, 0]
        far = across(own, 2)
        near = across(own, 1)
        column = stack([far, near, across(far, 1)])
        one = first(column)
        pieces = [column, one]
        if n == 0:
            pieces += [second(column), second(one)]
        gathered.append(pieces + [swap(v) for v in pieces])
    return [filters, swapped], gathered


def by_permutes(phases, dp_count):
    return phases == 4 and dp_count == 8


def per_device(
    phases,
    dp_count,
    tap_tokens,
    project_weight,
    expand_four,
    expand_two,
    shrink_weight,
    refine_filters,
    head_matrix,
    head_vector,
    tile_slot,
):
    plan = Plan(phases, project_weight.shape[2])
    phase_id = lax.axis_index("phase")
    dp_id = lax.axis_index("dp")
    held = (phase_id >> (dp_id & 1)) & 1
    where = jnp.stack([phase_id, dp_id & 1, dp_id >> 1]).astype(jnp.int32)
    slots = phase_id * dp_count * SLOT_DEV + jnp.arange(dp_count * SLOT_DEV, dtype=jnp.int32)
    targets = lax.dynamic_slice(tile_slot, (dp_id, phase_id, 0), (1, 1, TILES_DEV))
    matches = (slots.reshape(dp_count, SLOT_DEV, 1) == targets).astype(F32)
    where, matches, phase_id, held = lax.optimization_barrier((where, matches, phase_id, held))
    if by_permutes(phases, dp_count):
        base, gathered = gather_filters(refine_filters, phase_id, held, phases, dp_count)
        upper, finer = base + gathered[0], base + gathered[1]
    else:
        upper = finer = [lax.all_gather(refine_filters, "dp", axis=2, tiled=True)]
    sent = project(plan, phases, where, tap_tokens, project_weight, shrink_weight)
    arrived = [sent[0]]
    for k in range(1, phases):
        arrived.append(lax.ppermute(sent[k], "phase", [(s, s ^ k) for s in range(phases)]))
    mine = stack(arrived)
    other = lax.ppermute(mine, "dp", [(d, d ^ 1) for d in range(dp_count)])
    summed1, patch0 = coarse(plan, where, mine, other, expand_two, upper)
    partial = fine(
        plan, where, summed1, patch0, head_matrix, head_vector, expand_four, matches, finer
    )
    portions = lax.all_to_all(partial, "dp", split_axis=0, concat_axis=0, tiled=True)
    return portions.sum(axis=0)


def solution(mesh):
    in_specs = (
        P("phase", "dp", None),
        P("phase", None, None),
        P(),
        P(),
        P(),
        P(None, None, "dp", None),
        P(),
        P(),
        P(),
    )
    out_specs = P(("phase", "dp"), None)
    phases, dp_count = mesh.shape["phase"], mesh.shape["dp"]

    def body(*args):
        return per_device(phases, dp_count, *args)

    return jax.shard_map(
        body, mesh=mesh, in_specs=in_specs, out_specs=out_specs, check_vma=False
    )
```

```python
import functools

import jax
import jax.numpy as jnp
from jax import lax
from jax.experimental import pallas as pl
from jax.experimental.pallas import tpu as pltpu
from jax.sharding import PartitionSpec as P

G = 32
TILES_DEV = 8
SLOT_DEV = 6
LEVELS = 4
F32 = jnp.float32
BF16 = jnp.bfloat16
STACK_VMEM = 4 * 1024 * 1024
PROJECT_VMEM = 60 * 1024 * 1024
PROJECT_STEPS = 8
COARSE_VMEM = 12 * 1024 * 1024
MIDDLE_VMEM = 20 * 1024 * 1024
FINE_VMEM = 24 * 1024 * 1024


LANES = 128


def take(ref, *at):
    return jnp.concatenate([ref[(i,) + at] for i in range(ref.shape[0])], axis=-1)


def put(ref, value, *at):
    for i in range(ref.shape[0]):
        ref[(i,) + at] = value[..., i * LANES : (i + 1) * LANES]


def dot(lhs, rhs):
    return jnp.dot(lhs, rhs, preferred_element_type=F32)


CHIP_ORDER = (2, 1, 3)
GROUPS = ((2, 3), (1,), (0,))


class Plan:
    def __init__(self, phases, channels):
        self.ch = channels
        self.half = G // 2
        self.block = G // phases
        self.sent = 2 * self.block
        self.rows1 = 3 * G // 4
        self.cols1 = self.block + self.block // 2
        self.cols0 = self.block + 2
        self.conv_cols = 4 * self.block + 4
        self.conv_rows = 4 * self.half + 16

    def slot_of(self, level):
        return next(g.index(level) for g in GROUPS if level in g)

    def sent_start(self, s):
        return jnp.clip(s * self.block - self.block // 2, 0, G - self.sent)

    def start1(self, s):
        return jnp.clip(s * self.block - self.block // 4, 0, G - self.cols1)

    def start0(self, s):
        return jnp.clip(s * self.block - 1, 0, G - self.cols0)


def project_kernel(plan, phases, where, tokens_hbm, weight_hbm, shrink_hbm, *refs):
    outs = refs[:phases]
    acc_lo, acc_hi, tokens, weight, shrink, sems, shrink_sem = refs[phases:]
    lanes = acc_lo.shape[1]
    depth = tokens.shape[1]
    size = depth // PROJECT_STEPS
    copies = []
    for i in range(PROJECT_STEPS):
        at = pl.ds(i * size, size)
        pair = (
            pltpu.make_async_copy(weight_hbm.at[0, at], weight.at[at], sems.at[0, i]),
            pltpu.make_async_copy(tokens_hbm.at[0, :, at], tokens.at[:, at], sems.at[1, i]),
        )
        for copy in pair:
            copy.start()
        copies.append(pair)
    shrink_copy = pltpu.make_async_copy(shrink_hbm, shrink, shrink_sem)
    shrink_copy.start()
    for i, pair in enumerate(copies):
        for copy in pair:
            copy.wait()
        at = slice(i * size, (i + 1) * size)
        part = dot(tokens[:, at], weight[at, :])
        if i == 0:
            acc_lo[...] = part[:, :lanes]
            acc_hi[...] = part[:, lanes:]
        else:
            acc_lo[...] += part[:, :lanes]
            acc_hi[...] += part[:, lanes:]
    shrink_copy.wait()
    phase = where[0]

    def column(start, size, stride):
        where_rows = pl.ds(start, size, stride=stride)
        return jnp.concatenate([acc_lo[where_rows, :], acc_hi[where_rows, :]], axis=1)

    @pl.when(phase < LEVELS - 1)
    def _():
        for k in range(phases):
            start = plan.sent_start(phase ^ k)
            for j in range(plan.sent):
                outs[k][j * plan.half : (j + 1) * plan.half, :] = column(
                    start + j, plan.half, G
                ).astype(BF16)

    @pl.when(phase == LEVELS - 1)
    def _():
        total = jnp.zeros((plan.half * plan.half // 2, plan.ch), F32)
        for a in range(2):
            for b in range(2):
                tall = jnp.concatenate(
                    [column(a * G + 2 * j + b, plan.half // 2, 2 * G) for j in range(G // 2)],
                    axis=0,
                )
                total += dot(
                    tall.astype(BF16), shrink[(2 * a + b) * plan.ch : (2 * a + b + 1) * plan.ch, :]
                )
        for k in range(phases):
            outs[k][: total.shape[0], :] = total.astype(BF16)
            outs[k][total.shape[0] :, :] = jnp.zeros(
                (outs[k].shape[0] - total.shape[0], plan.ch), BF16
            )


def project(plan, phases, where, tokens, weight, shrink):
    rows, depth = tokens.shape[1:]
    pixels = plan.sent * plan.half
    hbm = pl.BlockSpec(memory_space=pltpu.HBM)
    out = jax.ShapeDtypeStruct((pixels, plan.ch), BF16)
    vmem = pl.BlockSpec(memory_space=pltpu.VMEM)
    return pl.pallas_call(
        functools.partial(project_kernel, plan, phases),
        in_specs=[pl.BlockSpec(memory_space=pltpu.SMEM), hbm, hbm, hbm],
        out_specs=[vmem] * phases,
        scratch_shapes=[pltpu.VMEM((rows, plan.ch // 2), F32)] * 2
        + [
            pltpu.VMEM((rows, depth), BF16),
            pltpu.VMEM((depth, plan.ch), BF16),
            pltpu.VMEM(shrink.shape, BF16),
            pltpu.SemaphoreType.DMA((2, PROJECT_STEPS)),
            pltpu.SemaphoreType.DMA,
        ],
        out_shape=[out] * phases,
        compiler_params=pltpu.CompilerParams(vmem_limit_bytes=PROJECT_VMEM),
        cost_estimate=pl.CostEstimate(
            flops=2 * rows * depth * plan.ch,
            bytes_accessed=2 * depth * (rows + plan.ch),
            transcendentals=0,
        ),
        name="project",
    )(where, tokens, weight, shrink)


def stack_kernel(*refs):
    for i, ref in enumerate(refs[:-1]):
        refs[-1][i] = ref[...]


def stack(values):
    vmem = pl.BlockSpec(memory_space=pltpu.VMEM)
    size = len(values) * values[0].size * values[0].dtype.itemsize
    return pl.pallas_call(
        stack_kernel,
        out_shape=jax.ShapeDtypeStruct((len(values),) + values[0].shape, values[0].dtype),
        in_specs=[vmem] * len(values),
        out_specs=vmem,
        compiler_params=pltpu.CompilerParams(vmem_limit_bytes=STACK_VMEM),
        cost_estimate=pl.CostEstimate(flops=0, bytes_accessed=2 * size, transcendentals=0),
        name="stack",
    )(*values)


def put_shifted(shifted, col, value):
    count, rows, _ = value.shape
    value = jnp.maximum(value, 0.0)
    at = lax.broadcasted_iota(jnp.int32, value.shape, 1)
    above = jnp.where(at == 0, 0.0, pltpu.roll(value, 1, 1))
    below = jnp.where(at == rows - 1, 0.0, pltpu.roll(value, rows - 1, 1))
    for p, moved in enumerate((above, value, below)):
        shifted[p, pl.ds(col + 1, count)] = moved.astype(BF16)


def clear_edges(shifted):
    shape = shifted.shape
    zeros = jnp.zeros((shape[0], 1) + shape[2:], BF16)
    shifted[:, 0:1] = zeros
    shifted[:, shape[1] - 1 : shape[1]] = zeros


def conv_block(shifted, weight, col, count, rows):
    channels = shifted.shape[3]
    start, size = rows
    patches = [
        shifted[p, pl.ds(col + q, count), pl.ds(start, size), :].reshape(count * size, channels)
        for p in range(3)
        for q in range(3)
    ]
    return dot(jnp.concatenate(patches, axis=1), weight[...]).reshape(count, size, -1)


def loop(count, body):
    if count == 1:
        body(0)
    else:
        lax.fori_loop(0, count, lambda i, c: (body(i), c)[1], 0)


def refine(source, wait, weights, first, second, chunk, out_col, out_count, out_chunk, emit):
    cols, rows = first.shape[1] - 2, first.shape[2]
    clear_edges(first)
    clear_edges(second)
    loop(cols // chunk, lambda i: put_shifted(first, i * chunk, source(i * chunk, chunk)))

    wait(0)

    def inner(i):
        put_shifted(second, i * chunk, conv_block(first, weights.at[0], i * chunk, chunk, (0, rows)))

    loop(cols // chunk, inner)

    wait(1)

    def outer(i):
        col = out_col + i * out_chunk
        branch = conv_block(second, weights.at[1], col, out_chunk, (0, rows))
        emit(i * out_chunk, source(col, out_chunk) + branch)

    loop(out_count // out_chunk, outer)


def start_filters(filters, level, weights, sems):
    if len(filters) == 1:
        for m in range(2):
            pltpu.make_async_copy(filters[0].at[level, m], weights.at[m], sems.at[m]).start()


def wait_filters(filters, weights, sems, m):
    if len(filters) == 1:
        pltpu.make_async_copy(filters[0].at[0, m], weights.at[m], sems.at[m]).wait()


def lay_filters(plan, where, filters, level, weights):
    if len(filters) == 1:
        return
    phase, side, chip = where[0], where[1], where[2]
    own, swapped = filters[:2]
    rows = own.shape[2]
    part = rows // 2
    slot = plan.slot_of(level)
    for ref, core in ((own, side), (swapped, 1 - side)):
        at = pl.ds(pl.multiple_of((2 * chip + core) * rows, 16), rows)
        for m in range(2):
            weights[m, at, :] = ref[level, m]
    if len(filters) == 6:
        for refs, core in ((filters[2:4], side), (filters[4:6], 1 - side)):
            held = (phase >> core) % 2
            for ref, m in zip(refs, (held, 1 - held)):
                for i, away in enumerate(CHIP_ORDER):
                    start = (2 * (chip ^ away) + core) * rows
                    weights[m, pl.ds(pl.multiple_of(start, 16), rows), :] = ref[i, slot]
        return
    for refs, core in ((filters[2:6], side), (filters[6:10], 1 - side)):
        for ref, moved in zip(refs, (0, 1 + core, 2 - core, 3)):
            quarter = phase ^ moved
            for i, away in enumerate(CHIP_ORDER):
                start = (2 * (chip ^ away) + core) * rows + (quarter % 2) * part
                at = pl.ds(pl.multiple_of(start, 16), part)
                weights[quarter // 2, at, :] = ref[i, slot]


def filter_specs(filters):
    space = pl.ANY if len(filters) == 1 else pltpu.VMEM
    return [pl.BlockSpec(memory_space=space)] * len(filters)


def load_patches(plan, patch, mine, other, k, side):
    for ref, at in ((mine, side), (other, 1 - side)):
        patch[:, pl.ds(pl.multiple_of(at * plan.half, plan.half), plan.half), :] = (
            ref[k].astype(F32).reshape(plan.sent, plan.half, plan.ch)
        )


def rounded(value):
    return value.astype(BF16).astype(F32)


COARSE_SCRATCH = 14


def coarse_kernel(plan, where, mine, other, expand_two, *refs):
    count = len(refs) - COARSE_SCRATCH
    filters = refs[:count]
    (
        summed1,
        patch0,
        weight3,
        weight2,
        sems,
        patch,
        map3,
        joined3,
        map2,
        joined2,
        first3,
        second3,
        first2,
        second2,
    ) = refs[count:]
    ch = plan.ch
    phase, side = where[0], where[1]
    for level, weights in ((3, weight3), (2, weight2)):
        start_filters(filters, level, weights, sems.at[level])
        lay_filters(plan, where, filters, level, weights)

    row1 = pl.multiple_of(side * (G - plan.rows1), 8)
    load_patches(plan, patch, mine, other, phase, side)
    off = plan.start0(phase) - plan.sent_start(phase)
    tall = patch[pl.ds(off, plan.cols0), pl.ds(row1, plan.rows1), :]
    patch0[...] = tall.reshape(patch0.shape).astype(BF16)

    size3 = G // 2
    quarter = plan.half // 2
    k3 = phase ^ 3
    for ref, at in ((mine, side), (other, 1 - side)):
        map3[:, pl.ds(pl.multiple_of(at * quarter, quarter), quarter), :] = (
            ref[k3, : size3 * quarter, :].astype(F32).reshape(size3, quarter, ch)
        )

    def keep3(col, value):
        joined3[pl.ds(col, value.shape[0])] = rounded(value)

    refine(
        lambda col, n: map3[pl.ds(col, n)],
        lambda m: wait_filters(filters, weight3, sems.at[3], m),
        weight3,
        first3,
        second3,
        size3,
        0,
        size3,
        size3,
        keep3,
    )

    load_patches(plan, patch, mine, other, phase ^ 2, side)
    from3 = plan.sent_start(phase) // 2
    tall = joined3[pl.ds(from3, plan.sent // 2)]
    for b in range(2):
        for a in range(2):
            put(map2, tall, slice(None), b, pl.ds(a, size3, stride=2), slice(None))
    for j in range(plan.sent):
        at = (j // 2, j % 2)
        put(map2, take(map2, *at) + patch[j], *at)

    def source2(col, n):
        return take(map2, pl.ds(col // 2, n // 2)).reshape(n, G, ch)

    def keep2(col, value):
        joined2[pl.ds(col, value.shape[0])] = rounded(value)

    refine(
        source2,
        lambda m: wait_filters(filters, weight2, sems.at[2], m),
        weight2,
        first2,
        second2,
        plan.sent,
        0,
        plan.sent,
        plan.sent,
        keep2,
    )

    load_patches(plan, patch, mine, other, phase ^ 1, side)
    off1 = plan.start1(phase) - plan.sent_start(phase)
    tall = patch[pl.ds(off1, plan.cols1), pl.ds(row1, plan.rows1), :]
    lhs = tall.reshape(plan.cols1 * plan.rows1, ch).astype(BF16)
    below = joined2[pl.ds(off1, plan.cols1), pl.ds(row1, plan.rows1), :]
    for a in range(2):
        for b in range(2):
            n = 2 * a + b
            grown = dot(lhs, expand_two[:, n * ch : (n + 1) * ch])
            put(
                summed1,
                grown.reshape(plan.cols1, plan.rows1, ch) + below,
                slice(None),
                b,
                pl.ds(a, plan.rows1, stride=2),
                slice(None),
            )


def shifted_maps(cols, rows, ch):
    return [pltpu.VMEM((3, cols + 2, rows, ch), BF16)] * 2


def coarse(plan, where, mine, other, expand_two, filters):
    ch = plan.ch
    vmem = pl.BlockSpec(memory_space=pltpu.VMEM)
    weights = pltpu.VMEM((2, 9 * ch, ch), BF16)
    size3 = G // 2
    slabs = ch // LANES
    return pl.pallas_call(
        functools.partial(coarse_kernel, plan),
        out_shape=[
            jax.ShapeDtypeStruct((slabs, plan.cols1, 2, 2 * plan.rows1, LANES), F32),
            jax.ShapeDtypeStruct((plan.cols0 * plan.rows1, ch), BF16),
        ],
        in_specs=[pl.BlockSpec(memory_space=pltpu.SMEM), vmem, vmem, vmem]
        + filter_specs(filters),
        out_specs=[vmem, vmem],
        scratch_shapes=[
            weights,
            weights,
            pltpu.SemaphoreType.DMA((LEVELS, 2)),
            pltpu.VMEM((plan.sent, G, ch), F32),
            pltpu.VMEM((size3, size3, ch), F32),
            pltpu.VMEM((size3, size3, ch), F32),
            pltpu.VMEM((slabs, plan.sent // 2, 2, G, LANES), F32),
            pltpu.VMEM((plan.sent, G, ch), F32),
        ]
        + shifted_maps(size3, size3, ch)
        + shifted_maps(plan.sent, G, ch),
        compiler_params=pltpu.CompilerParams(vmem_limit_bytes=COARSE_VMEM),
        cost_estimate=pl.CostEstimate(
            flops=2_000_000_000, bytes_accessed=8_000_000, transcendentals=0
        ),
        name="coarse",
    )(where, mine, other, expand_two, *filters)


MIDDLE_SCRATCH = 6


def middle_kernel(plan, where, summed1, patch0, expand_four, *refs):
    count = len(refs) - MIDDLE_SCRATCH
    filters = refs[:count]
    summed0, weight1, sems, joined1, first1, second1 = refs[count:]
    ch = plan.ch
    phase = where[0]
    start_filters(filters, 1, weight1, sems)
    lay_filters(plan, where, filters, 1, weight1)

    off0 = 2 * (plan.start0(phase) - plan.start1(phase))

    def source1(col, n):
        return take(summed1, pl.ds(col // 2, n // 2)).reshape(n, 2 * plan.rows1, ch)

    def keep1(col, value):
        value = rounded(value)
        put(
            joined1,
            value.reshape(value.shape[0] // 2, 2, 2 * plan.rows1, ch),
            pl.ds(col // 2, value.shape[0] // 2),
        )

    refine(
        source1,
        lambda m: wait_filters(filters, weight1, sems, m),
        weight1,
        first1,
        second1,
        plan.cols1,
        off0,
        2 * plan.cols0,
        plan.cols0,
        keep1,
    )

    for a in range(4):
        for b in range(4):
            n = 4 * a + b
            grown = dot(patch0[...], expand_four[:, n * ch : (n + 1) * ch])
            below = take(
                joined1, slice(None), b // 2, pl.ds(a // 2, plan.rows1, stride=2), slice(None)
            )
            put(
                summed0,
                grown.reshape(plan.cols0, plan.rows1, ch) + below,
                slice(None),
                b,
                pl.ds(a, plan.rows1, stride=4),
                slice(None),
            )


def middle(plan, where, summed1, patch0, expand_four, filters):
    ch = plan.ch
    vmem = pl.BlockSpec(memory_space=pltpu.VMEM)
    slabs = ch // LANES
    return pl.pallas_call(
        functools.partial(middle_kernel, plan),
        out_shape=jax.ShapeDtypeStruct((slabs, plan.cols0, 4, 4 * plan.rows1, LANES), F32),
        in_specs=[pl.BlockSpec(memory_space=pltpu.SMEM)] + [vmem] * 3 + filter_specs(filters),
        out_specs=vmem,
        scratch_shapes=[
            pltpu.VMEM((2, 9 * ch, ch), BF16),
            pltpu.SemaphoreType.DMA((2,)),
            pltpu.VMEM((slabs, plan.cols0, 2, 2 * plan.rows1, LANES), F32),
        ]
        + shifted_maps(2 * plan.cols1, 2 * plan.rows1, ch),
        compiler_params=pltpu.CompilerParams(vmem_limit_bytes=MIDDLE_VMEM),
        cost_estimate=pl.CostEstimate(
            flops=3_000_000_000, bytes_accessed=6_000_000, transcendentals=0
        ),
        name="middle",
    )(where, summed1, patch0, expand_four, *filters)


FINE_SCRATCH = 7


def fine_kernel(plan, where, map0, head, vector, matches, *refs):
    count = len(refs) - FINE_SCRATCH
    filters = refs[:count]
    portions, weight0, sems, first, second, by_col, by_row = refs[count:]
    ch = plan.ch
    phase, side = where[0], where[1]
    start_filters(filters, 0, weight0, sems)
    lay_filters(plan, where, filters, 0, weight0)
    cols, rows, own_rows = plan.conv_cols, plan.conv_rows, 4 * plan.half
    own0 = 4 * (phase * plan.block - plan.start0(phase))
    conv0 = jnp.clip(own0 - 2, 0, 4 * plan.cols0 - cols)
    own = own0 - conv0
    row = pl.multiple_of(side * 16, 16)
    pairs = map0.reshape(ch // LANES, 2 * plan.cols0, 2, 4 * plan.rows1, LANES)
    chunk = cols // 2

    def source0(col, n, start, size):
        at = (pl.ds((conv0 + col) // 2, n // 2), slice(None), pl.ds(start, size), slice(None))
        return take(pairs, *at).reshape(n, size, ch)

    clear_edges(first)
    clear_edges(second)
    loop(9, lambda i: put_shifted(first, i * 4, source0(i * 4, 4, row, rows)))
    wait_filters(filters, weight0, sems, 0)

    def inner(i):
        put_shifted(
            second, i * chunk, conv_block(first, weight0.at[0], i * chunk, chunk, (0, rows))
        )

    loop(cols // chunk, inner)
    wait_filters(filters, weight0, sems, 1)
    half_cols = 2 * plan.block
    hidden_size = head.shape[1]
    scale = jnp.broadcast_to(vector[...], (hidden_size, hidden_size)).T[:, :1]

    def outer(i):
        col = own + i * half_cols
        branch = conv_block(second, weight0.at[1], col, half_cols, (row, own_rows))
        summed = source0(col, half_cols, pl.multiple_of(2 * row, 16), own_rows)
        joined = (summed + branch).astype(BF16)
        hidden = lax.dot_general(
            head[...],
            joined.reshape(half_cols * own_rows, ch),
            (((0,), (1,)), ((), ())),
            preferred_element_type=F32,
        )
        depth = (jnp.maximum(hidden, 0.0) * scale).sum(axis=0, keepdims=True)
        for j in range(half_cols):
            by_col[pl.ds(i * half_cols + j, 1), :own_rows] = depth[
                :, j * own_rows : (j + 1) * own_rows
            ]

    loop(2, outer)

    by_row[...] = by_col[...].T
    tile_rows = own_rows // TILES_DEV
    tiles = jnp.concatenate(
        [
            by_row[pl.ds(i, TILES_DEV, stride=tile_rows), :][:, : 2 * half_cols]
            for i in range(tile_rows)
        ],
        axis=1,
    )

    def add_tiles(d):
        chosen = matches[d]
        total = chosen[:, 0:1] * tiles[0:1]
        for j in range(1, TILES_DEV):
            total += chosen[:, j : j + 1] * tiles[j : j + 1]
        portions[d] = total

    for d in range(portions.shape[0]):
        add_tiles(d)


def fine(plan, where, summed0, head, vector, matches, filters):
    ch = plan.ch
    vmem = pl.BlockSpec(memory_space=pltpu.VMEM)
    pixels = 16 * plan.block * plan.half // TILES_DEV
    return pl.pallas_call(
        functools.partial(fine_kernel, plan),
        out_shape=jax.ShapeDtypeStruct(matches.shape[:2] + (pixels,), F32),
        in_specs=[pl.BlockSpec(memory_space=pltpu.SMEM)] + [vmem] * 4 + filter_specs(filters),
        out_specs=vmem,
        scratch_shapes=[pltpu.VMEM((2, 9 * ch, ch), BF16), pltpu.SemaphoreType.DMA((2,))]
        + shifted_maps(plan.conv_cols, plan.conv_rows, ch)
        + [pltpu.VMEM((LANES, LANES), F32)] * 2,
        compiler_params=pltpu.CompilerParams(vmem_limit_bytes=FINE_VMEM),
        cost_estimate=pl.CostEstimate(
            flops=6_000_000_000, bytes_accessed=8_000_000, transcendentals=0
        ),
        name="fine",
    )(where, summed0, head, vector[None, :], matches, *filters)


def gather_filters(filters, phase_id, held, phases, dp_count):
    axes = ("phase", "dp")
    chips = dp_count // 2

    def move(value, to):
        route = []
        for p in range(phases):
            for z in range(chips):
                for c in range(2):
                    q, y, d = to(p, z, c)
                    route.append((p * dp_count + 2 * z + c, q * dp_count + 2 * y + d))
        return lax.ppermute(value, axes, route)

    def across(value, bit):
        return move(value, lambda p, z, c: (p, z ^ bit, c))

    def first(value):
        return move(value, lambda p, z, c: (p ^ (1 + c), z, c))

    def second(value):
        return move(value, lambda p, z, c: (p ^ (2 - c), z, c))

    def swap(value):
        return move(value, lambda p, z, c: (p, z, c ^ 1))

    levels, convs, rows, channels = filters.shape
    part = convs * rows // phases
    quarters = filters.reshape(levels, phases, part, channels)
    swapped = swap(filters)
    gathered = []
    for n, group in enumerate(GROUPS):
        if n == 0:
            source, chosen = quarters, phase_id
        else:
            source, chosen = filters, held
        own = lax.dynamic_slice(
            source, (group[0], chosen, 0, 0), (len(group), 1) + source.shape[2:]
        )[:, 0]
        far = across(own, 2)
        near = across(own, 1)
        column = stack([far, near, across(far, 1)])
        one = first(column)
        pieces = [column, one]
        if n == 0:
            pieces += [second(column), second(one)]
        gathered.append(pieces + [swap(v) for v in pieces])
    return [filters, swapped], gathered


def by_permutes(phases, dp_count):
    return phases == 4 and dp_count == 8


def per_device(
    phases,
    dp_count,
    tap_tokens,
    project_weight,
    expand_four,
    expand_two,
    shrink_weight,
    refine_filters,
    head_matrix,
    head_vector,
    tile_slot,
):
    plan = Plan(phases, project_weight.shape[2])
    phase_id = lax.axis_index("phase")
    dp_id = lax.axis_index("dp")
    held = (phase_id >> (dp_id & 1)) & 1
    where = jnp.stack([phase_id, dp_id & 1, dp_id >> 1]).astype(jnp.int32)
    slots = phase_id * dp_count * SLOT_DEV + jnp.arange(dp_count * SLOT_DEV, dtype=jnp.int32)
    targets = lax.dynamic_slice(tile_slot, (dp_id, phase_id, 0), (1, 1, TILES_DEV))
    matches = (slots.reshape(dp_count, SLOT_DEV, 1) == targets).astype(F32)
    if by_permutes(phases, dp_count):
        base, gathered = gather_filters(refine_filters, phase_id, held, phases, dp_count)
        upper, medium, finer = (base + pieces for pieces in gathered)
    else:
        upper = medium = finer = [lax.all_gather(refine_filters, "dp", axis=2, tiled=True)]
    sent = project(plan, phases, where, tap_tokens, project_weight, shrink_weight)
    arrived = [sent[0]]
    for k in range(1, phases):
        arrived.append(lax.ppermute(sent[k], "phase", [(s, s ^ k) for s in range(phases)]))
    mine = stack(arrived)
    other = lax.ppermute(mine, "dp", [(d, d ^ 1) for d in range(dp_count)])
    summed1, patch0 = coarse(plan, where, mine, other, expand_two, upper)
    summed0 = middle(plan, where, summed1, patch0, expand_four, medium)
    partial = fine(plan, where, summed0, head_matrix, head_vector, matches, finer)
    portions = lax.all_to_all(partial, "dp", split_axis=0, concat_axis=0, tiled=True)
    return portions.sum(axis=0)


def solution(mesh):
    in_specs = (
        P("phase", "dp", None),
        P("phase", None, None),
        P(),
        P(),
        P(),
        P(None, None, "dp", None),
        P(),
        P(),
        P(),
    )
    out_specs = P(("phase", "dp"), None)
    phases, dp_count = mesh.shape["phase"], mesh.shape["dp"]

    def body(*args):
        return per_device(phases, dp_count, *args)

    return jax.shard_map(
        body, mesh=mesh, in_specs=in_specs, out_specs=out_specs, check_vma=False
    )
```

```python
import functools

import jax
import jax.numpy as jnp
from jax import lax
from jax.experimental import pallas as pl
from jax.experimental.pallas import tpu as pltpu
from jax.sharding import PartitionSpec as P

G = 32
TILES_DEV = 8
SLOT_DEV = 6
LEVELS = 4
F32 = jnp.float32
BF16 = jnp.bfloat16
STACK_VMEM = 4 * 1024 * 1024
PROJECT_VMEM = 60 * 1024 * 1024
PROJECT_STEPS = 8
COARSE_VMEM = 12 * 1024 * 1024
MIDDLE_VMEM = 20 * 1024 * 1024
FINE_VMEM = 24 * 1024 * 1024


LANES = 128


def take(ref, *at):
    return jnp.concatenate([ref[(i,) + at] for i in range(ref.shape[0])], axis=-1)


def put(ref, value, *at):
    for i in range(ref.shape[0]):
        ref[(i,) + at] = value[..., i * LANES : (i + 1) * LANES]


def dot(lhs, rhs):
    return jnp.dot(lhs, rhs, preferred_element_type=F32)


CHIP_ORDER = (2, 1, 3)
GROUPS = ((2, 3), (1,), (0,))


class Plan:
    def __init__(self, phases, channels):
        self.ch = channels
        self.half = G // 2
        self.block = G // phases
        self.sent = 2 * self.block
        self.rows1 = 3 * G // 4
        self.cols1 = self.block + self.block // 2
        self.cols0 = self.block + 2
        self.conv_cols = 4 * self.block + 4
        self.conv_rows = 4 * self.half + 16

    def slot_of(self, level):
        return next(g.index(level) for g in GROUPS if level in g)

    def sent_start(self, s):
        return jnp.clip(s * self.block - self.block // 2, 0, G - self.sent)

    def start1(self, s):
        return jnp.clip(s * self.block - self.block // 4, 0, G - self.cols1)

    def start0(self, s):
        return jnp.clip(s * self.block - 1, 0, G - self.cols0)


def project_kernel(plan, phases, where, tokens_hbm, weight_hbm, shrink_hbm, *refs):
    outs = refs[:phases]
    acc_lo, acc_hi, tokens, weight, shrink, sems, shrink_sem = refs[phases:]
    lanes = acc_lo.shape[1]
    depth = tokens.shape[1]
    size = depth // PROJECT_STEPS
    copies = []
    for i in range(PROJECT_STEPS):
        at = pl.ds(i * size, size)
        pair = (
            pltpu.make_async_copy(weight_hbm.at[0, at], weight.at[at], sems.at[0, i]),
            pltpu.make_async_copy(tokens_hbm.at[0, :, at], tokens.at[:, at], sems.at[1, i]),
        )
        for copy in pair:
            copy.start()
        copies.append(pair)
    shrink_copy = pltpu.make_async_copy(shrink_hbm, shrink, shrink_sem)
    shrink_copy.start()
    for i, pair in enumerate(copies):
        for copy in pair:
            copy.wait()
        at = slice(i * size, (i + 1) * size)
        part = dot(tokens[:, at], weight[at, :])
        if i == 0:
            acc_lo[...] = part[:, :lanes]
            acc_hi[...] = part[:, lanes:]
        else:
            acc_lo[...] += part[:, :lanes]
            acc_hi[...] += part[:, lanes:]
    shrink_copy.wait()
    phase = where[0]

    def column(start, size, stride):
        where_rows = pl.ds(start, size, stride=stride)
        return jnp.concatenate([acc_lo[where_rows, :], acc_hi[where_rows, :]], axis=1)

    @pl.when(phase < LEVELS - 1)
    def _():
        for k in range(phases):
            start = plan.sent_start(phase ^ k)
            for j in range(plan.sent):
                outs[k][j * plan.half : (j + 1) * plan.half, :] = column(
                    start + j, plan.half, G
                ).astype(BF16)

    @pl.when(phase == LEVELS - 1)
    def _():
        total = jnp.zeros((plan.half * plan.half // 2, plan.ch), F32)
        for a in range(2):
            for b in range(2):
                tall = jnp.concatenate(
                    [column(a * G + 2 * j + b, plan.half // 2, 2 * G) for j in range(G // 2)],
                    axis=0,
                )
                total += dot(
                    tall.astype(BF16), shrink[(2 * a + b) * plan.ch : (2 * a + b + 1) * plan.ch, :]
                )
        for k in range(phases):
            outs[k][: total.shape[0], :] = total.astype(BF16)
            outs[k][total.shape[0] :, :] = jnp.zeros(
                (outs[k].shape[0] - total.shape[0], plan.ch), BF16
            )


def project(plan, phases, where, tokens, weight, shrink):
    rows, depth = tokens.shape[1:]
    pixels = plan.sent * plan.half
    hbm = pl.BlockSpec(memory_space=pltpu.HBM)
    out = jax.ShapeDtypeStruct((pixels, plan.ch), BF16)
    vmem = pl.BlockSpec(memory_space=pltpu.VMEM)
    return pl.pallas_call(
        functools.partial(project_kernel, plan, phases),
        in_specs=[pl.BlockSpec(memory_space=pltpu.SMEM), hbm, hbm, hbm],
        out_specs=[vmem] * phases,
        scratch_shapes=[pltpu.VMEM((rows, plan.ch // 2), F32)] * 2
        + [
            pltpu.VMEM((rows, depth), BF16),
            pltpu.VMEM((depth, plan.ch), BF16),
            pltpu.VMEM(shrink.shape, BF16),
            pltpu.SemaphoreType.DMA((2, PROJECT_STEPS)),
            pltpu.SemaphoreType.DMA,
        ],
        out_shape=[out] * phases,
        compiler_params=pltpu.CompilerParams(vmem_limit_bytes=PROJECT_VMEM),
        cost_estimate=pl.CostEstimate(
            flops=2 * rows * depth * plan.ch,
            bytes_accessed=2 * depth * (rows + plan.ch),
            transcendentals=0,
        ),
        name="project",
    )(where, tokens, weight, shrink)


def stack_kernel(*refs):
    for i, ref in enumerate(refs[:-1]):
        refs[-1][i] = ref[...]


def stack(values):
    vmem = pl.BlockSpec(memory_space=pltpu.VMEM)
    size = len(values) * values[0].size * values[0].dtype.itemsize
    return pl.pallas_call(
        stack_kernel,
        out_shape=jax.ShapeDtypeStruct((len(values),) + values[0].shape, values[0].dtype),
        in_specs=[vmem] * len(values),
        out_specs=vmem,
        compiler_params=pltpu.CompilerParams(vmem_limit_bytes=STACK_VMEM),
        cost_estimate=pl.CostEstimate(flops=0, bytes_accessed=2 * size, transcendentals=0),
        name="stack",
    )(*values)


def put_shifted(shifted, col, value):
    count, rows, _ = value.shape
    value = jnp.maximum(value, 0.0)
    at = lax.broadcasted_iota(jnp.int32, value.shape, 1)
    above = jnp.where(at == 0, 0.0, pltpu.roll(value, 1, 1))
    below = jnp.where(at == rows - 1, 0.0, pltpu.roll(value, rows - 1, 1))
    for p, moved in enumerate((above, value, below)):
        shifted[p, pl.ds(col + 1, count)] = moved.astype(BF16)


def clear_edges(shifted):
    shape = shifted.shape
    zeros = jnp.zeros((shape[0], 1) + shape[2:], BF16)
    shifted[:, 0:1] = zeros
    shifted[:, shape[1] - 1 : shape[1]] = zeros


def conv_block(shifted, weight, col, count, rows):
    channels = shifted.shape[3]
    start, size = rows
    patches = [
        shifted[p, pl.ds(col + q, count), pl.ds(start, size), :].reshape(count * size, channels)
        for p in range(3)
        for q in range(3)
    ]
    return dot(jnp.concatenate(patches, axis=1), weight[...]).reshape(count, size, -1)


def loop(count, body):
    lax.fori_loop(0, count, lambda i, c: (body(i), c)[1], 0)


def steps(count, body):
    for i in range(count):
        body(i)


def refine(source, wait, weights, first, second, chunk, out_col, out_count, out_chunk, emit):
    cols, rows = first.shape[1] - 2, first.shape[2]
    clear_edges(first)
    clear_edges(second)
    steps(cols // chunk, lambda i: put_shifted(first, i * chunk, source(i * chunk, chunk)))

    wait(0)

    def inner(i):
        put_shifted(second, i * chunk, conv_block(first, weights.at[0], i * chunk, chunk, (0, rows)))

    steps(cols // chunk, inner)

    wait(1)

    def outer(i):
        col = out_col + i * out_chunk
        branch = conv_block(second, weights.at[1], col, out_chunk, (0, rows))
        emit(i * out_chunk, source(col, out_chunk) + branch)

    steps(out_count // out_chunk, outer)


def start_filters(filters, level, weights, sems):
    if len(filters) == 1:
        for m in range(2):
            pltpu.make_async_copy(filters[0].at[level, m], weights.at[m], sems.at[m]).start()


def wait_filters(filters, weights, sems, m):
    if len(filters) == 1:
        pltpu.make_async_copy(filters[0].at[0, m], weights.at[m], sems.at[m]).wait()


def lay_filters(plan, where, filters, level, weights):
    if len(filters) == 1:
        return
    phase, side, chip = where[0], where[1], where[2]
    own, swapped = filters[:2]
    rows = own.shape[2]
    part = rows // 2
    slot = plan.slot_of(level)
    for ref, core in ((own, side), (swapped, 1 - side)):
        at = pl.ds(pl.multiple_of((2 * chip + core) * rows, 16), rows)
        for m in range(2):
            weights[m, at, :] = ref[level, m]
    if len(filters) == 6:
        for refs, core in ((filters[2:4], side), (filters[4:6], 1 - side)):
            held = (phase >> core) % 2
            for ref, m in zip(refs, (held, 1 - held)):
                for i, away in enumerate(CHIP_ORDER):
                    start = (2 * (chip ^ away) + core) * rows
                    weights[m, pl.ds(pl.multiple_of(start, 16), rows), :] = ref[i, slot]
        return
    for refs, core in ((filters[2:6], side), (filters[6:10], 1 - side)):
        for ref, moved in zip(refs, (0, 1 + core, 2 - core, 3)):
            quarter = phase ^ moved
            for i, away in enumerate(CHIP_ORDER):
                start = (2 * (chip ^ away) + core) * rows + (quarter % 2) * part
                at = pl.ds(pl.multiple_of(start, 16), part)
                weights[quarter // 2, at, :] = ref[i, slot]


def filter_specs(filters):
    space = pl.ANY if len(filters) == 1 else pltpu.VMEM
    return [pl.BlockSpec(memory_space=space)] * len(filters)


def load_patches(plan, patch, mine, other, k, side):
    for ref, at in ((mine, side), (other, 1 - side)):
        patch[:, pl.ds(pl.multiple_of(at * plan.half, plan.half), plan.half), :] = (
            ref[k].astype(F32).reshape(plan.sent, plan.half, plan.ch)
        )


def rounded(value):
    return value.astype(BF16).astype(F32)


COARSE_SCRATCH = 14


def coarse_kernel(plan, where, mine, other, expand_two, *refs):
    count = len(refs) - COARSE_SCRATCH
    filters = refs[:count]
    (
        summed1,
        patch0,
        weight3,
        weight2,
        sems,
        patch,
        map3,
        joined3,
        map2,
        joined2,
        first3,
        second3,
        first2,
        second2,
    ) = refs[count:]
    ch = plan.ch
    phase, side = where[0], where[1]
    for level, weights in ((3, weight3), (2, weight2)):
        start_filters(filters, level, weights, sems.at[level])
        lay_filters(plan, where, filters, level, weights)

    row1 = pl.multiple_of(side * (G - plan.rows1), 8)
    load_patches(plan, patch, mine, other, phase, side)
    off = plan.start0(phase) - plan.sent_start(phase)
    tall = patch[pl.ds(off, plan.cols0), pl.ds(row1, plan.rows1), :]
    patch0[...] = tall.reshape(patch0.shape).astype(BF16)

    size3 = G // 2
    quarter = plan.half // 2
    k3 = phase ^ 3
    for ref, at in ((mine, side), (other, 1 - side)):
        map3[:, pl.ds(pl.multiple_of(at * quarter, quarter), quarter), :] = (
            ref[k3, : size3 * quarter, :].astype(F32).reshape(size3, quarter, ch)
        )

    def keep3(col, value):
        joined3[pl.ds(col, value.shape[0])] = rounded(value)

    refine(
        lambda col, n: map3[pl.ds(col, n)],
        lambda m: wait_filters(filters, weight3, sems.at[3], m),
        weight3,
        first3,
        second3,
        size3,
        0,
        size3,
        size3,
        keep3,
    )

    load_patches(plan, patch, mine, other, phase ^ 2, side)
    from3 = plan.sent_start(phase) // 2
    tall = joined3[pl.ds(from3, plan.sent // 2)]
    for b in range(2):
        for a in range(2):
            put(map2, tall, slice(None), b, pl.ds(a, size3, stride=2), slice(None))
    for j in range(plan.sent):
        at = (j // 2, j % 2)
        put(map2, take(map2, *at) + patch[j], *at)

    def source2(col, n):
        return take(map2, pl.ds(col // 2, n // 2)).reshape(n, G, ch)

    def keep2(col, value):
        joined2[pl.ds(col, value.shape[0])] = rounded(value)

    refine(
        source2,
        lambda m: wait_filters(filters, weight2, sems.at[2], m),
        weight2,
        first2,
        second2,
        plan.sent,
        0,
        plan.sent,
        plan.sent,
        keep2,
    )

    load_patches(plan, patch, mine, other, phase ^ 1, side)
    off1 = plan.start1(phase) - plan.sent_start(phase)
    tall = patch[pl.ds(off1, plan.cols1), pl.ds(row1, plan.rows1), :]
    lhs = tall.reshape(plan.cols1 * plan.rows1, ch).astype(BF16)
    below = joined2[pl.ds(off1, plan.cols1), pl.ds(row1, plan.rows1), :]
    for a in range(2):
        for b in range(2):
            n = 2 * a + b
            grown = dot(lhs, expand_two[:, n * ch : (n + 1) * ch])
            put(
                summed1,
                grown.reshape(plan.cols1, plan.rows1, ch) + below,
                slice(None),
                b,
                pl.ds(a, plan.rows1, stride=2),
                slice(None),
            )


def shifted_maps(cols, rows, ch):
    return [pltpu.VMEM((3, cols + 2, rows, ch), BF16)] * 2


def coarse(plan, where, mine, other, expand_two, filters):
    ch = plan.ch
    vmem = pl.BlockSpec(memory_space=pltpu.VMEM)
    weights = pltpu.VMEM((2, 9 * ch, ch), BF16)
    size3 = G // 2
    slabs = ch // LANES
    return pl.pallas_call(
        functools.partial(coarse_kernel, plan),
        out_shape=[
            jax.ShapeDtypeStruct((slabs, plan.cols1, 2, 2 * plan.rows1, LANES), F32),
            jax.ShapeDtypeStruct((plan.cols0 * plan.rows1, ch), BF16),
        ],
        in_specs=[pl.BlockSpec(memory_space=pltpu.SMEM), vmem, vmem, vmem]
        + filter_specs(filters),
        out_specs=[vmem, vmem],
        scratch_shapes=[
            weights,
            weights,
            pltpu.SemaphoreType.DMA((LEVELS, 2)),
            pltpu.VMEM((plan.sent, G, ch), F32),
            pltpu.VMEM((size3, size3, ch), F32),
            pltpu.VMEM((size3, size3, ch), F32),
            pltpu.VMEM((slabs, plan.sent // 2, 2, G, LANES), F32),
            pltpu.VMEM((plan.sent, G, ch), F32),
        ]
        + shifted_maps(size3, size3, ch)
        + shifted_maps(plan.sent, G, ch),
        compiler_params=pltpu.CompilerParams(vmem_limit_bytes=COARSE_VMEM),
        cost_estimate=pl.CostEstimate(
            flops=2_000_000_000, bytes_accessed=8_000_000, transcendentals=0
        ),
        name="coarse",
    )(where, mine, other, expand_two, *filters)


MIDDLE_SCRATCH = 6


def middle_kernel(plan, where, summed1, patch0, expand_four, *refs):
    count = len(refs) - MIDDLE_SCRATCH
    filters = refs[:count]
    summed0, weight1, sems, joined1, first1, second1 = refs[count:]
    ch = plan.ch
    phase = where[0]
    start_filters(filters, 1, weight1, sems)
    lay_filters(plan, where, filters, 1, weight1)

    off0 = 2 * (plan.start0(phase) - plan.start1(phase))

    def source1(col, n):
        return take(summed1, pl.ds(col // 2, n // 2)).reshape(n, 2 * plan.rows1, ch)

    def keep1(col, value):
        value = rounded(value)
        put(
            joined1,
            value.reshape(value.shape[0] // 2, 2, 2 * plan.rows1, ch),
            pl.ds(col // 2, value.shape[0] // 2),
        )

    refine(
        source1,
        lambda m: wait_filters(filters, weight1, sems, m),
        weight1,
        first1,
        second1,
        plan.cols1,
        off0,
        2 * plan.cols0,
        plan.cols0,
        keep1,
    )

    for a in range(4):
        for b in range(4):
            n = 4 * a + b
            grown = dot(patch0[...], expand_four[:, n * ch : (n + 1) * ch])
            below = take(
                joined1, slice(None), b // 2, pl.ds(a // 2, plan.rows1, stride=2), slice(None)
            )
            put(
                summed0,
                grown.reshape(plan.cols0, plan.rows1, ch) + below,
                slice(None),
                b,
                pl.ds(a, plan.rows1, stride=4),
                slice(None),
            )


def middle(plan, where, summed1, patch0, expand_four, filters):
    ch = plan.ch
    vmem = pl.BlockSpec(memory_space=pltpu.VMEM)
    slabs = ch // LANES
    return pl.pallas_call(
        functools.partial(middle_kernel, plan),
        out_shape=jax.ShapeDtypeStruct((slabs, plan.cols0, 4, 4 * plan.rows1, LANES), F32),
        in_specs=[pl.BlockSpec(memory_space=pltpu.SMEM)] + [vmem] * 3 + filter_specs(filters),
        out_specs=vmem,
        scratch_shapes=[
            pltpu.VMEM((2, 9 * ch, ch), BF16),
            pltpu.SemaphoreType.DMA((2,)),
            pltpu.VMEM((slabs, plan.cols0, 2, 2 * plan.rows1, LANES), F32),
        ]
        + shifted_maps(2 * plan.cols1, 2 * plan.rows1, ch),
        compiler_params=pltpu.CompilerParams(vmem_limit_bytes=MIDDLE_VMEM),
        cost_estimate=pl.CostEstimate(
            flops=3_000_000_000, bytes_accessed=6_000_000, transcendentals=0
        ),
        name="middle",
    )(where, summed1, patch0, expand_four, *filters)


FINE_SCRATCH = 7


def fine_kernel(plan, where, map0, head, vector, tile_slot, *refs):
    count = len(refs) - FINE_SCRATCH
    filters = refs[:count]
    portions, weight0, sems, first, second, by_col, by_row = refs[count:]
    ch = plan.ch
    phase, side = where[0], where[1]
    start_filters(filters, 0, weight0, sems)
    lay_filters(plan, where, filters, 0, weight0)
    cols, rows, own_rows = plan.conv_cols, plan.conv_rows, 4 * plan.half
    own0 = 4 * (phase * plan.block - plan.start0(phase))
    conv0 = jnp.clip(own0 - 2, 0, 4 * plan.cols0 - cols)
    own = own0 - conv0
    row = pl.multiple_of(side * 16, 16)
    pairs = map0.reshape(ch // LANES, 2 * plan.cols0, 2, 4 * plan.rows1, LANES)
    chunk = cols // 2

    def source0(col, n, start, size):
        at = (pl.ds((conv0 + col) // 2, n // 2), slice(None), pl.ds(start, size), slice(None))
        return take(pairs, *at).reshape(n, size, ch)

    clear_edges(first)
    clear_edges(second)
    loop(9, lambda i: put_shifted(first, i * 4, source0(i * 4, 4, row, rows)))
    wait_filters(filters, weight0, sems, 0)

    def inner(i):
        put_shifted(
            second, i * chunk, conv_block(first, weight0.at[0], i * chunk, chunk, (0, rows))
        )

    loop(cols // chunk, inner)
    wait_filters(filters, weight0, sems, 1)
    half_cols = 2 * plan.block
    hidden_size = head.shape[1]
    scale = jnp.broadcast_to(vector[...], (hidden_size, hidden_size)).T[:, :1]

    def outer(i):
        col = own + i * half_cols
        branch = conv_block(second, weight0.at[1], col, half_cols, (row, own_rows))
        summed = source0(col, half_cols, pl.multiple_of(2 * row, 16), own_rows)
        joined = (summed + branch).astype(BF16)
        hidden = lax.dot_general(
            head[...],
            joined.reshape(half_cols * own_rows, ch),
            (((0,), (1,)), ((), ())),
            preferred_element_type=F32,
        )
        depth = (jnp.maximum(hidden, 0.0) * scale).sum(axis=0, keepdims=True)
        for j in range(half_cols):
            by_col[pl.ds(i * half_cols + j, 1), :own_rows] = depth[
                :, j * own_rows : (j + 1) * own_rows
            ]

    loop(2, outer)

    by_row[...] = by_col[...].T
    tile_rows = own_rows // TILES_DEV
    tiles = jnp.concatenate(
        [
            by_row[pl.ds(i, TILES_DEV, stride=tile_rows), :][:, : 2 * half_cols]
            for i in range(tile_rows)
        ],
        axis=1,
    )

    count = portions.shape[0]
    targets = tile_slot[2 * where[2] + side, pl.ds(phase, 1), :]
    slot = lax.broadcasted_iota(jnp.int32, (SLOT_DEV, TILES_DEV), 0) + phase * count * SLOT_DEV
    for d in range(count):
        chosen = (slot + d * SLOT_DEV == targets).astype(F32)
        total = chosen[:, 0:1] * tiles[0:1]
        for j in range(1, TILES_DEV):
            total += chosen[:, j : j + 1] * tiles[j : j + 1]
        portions[d] = total


def fine(plan, dp_count, where, summed0, head, vector, tile_slot, filters):
    ch = plan.ch
    vmem = pl.BlockSpec(memory_space=pltpu.VMEM)
    pixels = 16 * plan.block * plan.half // TILES_DEV
    return pl.pallas_call(
        functools.partial(fine_kernel, plan),
        out_shape=jax.ShapeDtypeStruct((dp_count, SLOT_DEV, pixels), F32),
        in_specs=[pl.BlockSpec(memory_space=pltpu.SMEM)] + [vmem] * 4 + filter_specs(filters),
        out_specs=vmem,
        scratch_shapes=[pltpu.VMEM((2, 9 * ch, ch), BF16), pltpu.SemaphoreType.DMA((2,))]
        + shifted_maps(plan.conv_cols, plan.conv_rows, ch)
        + [pltpu.VMEM((LANES, LANES), F32)] * 2,
        compiler_params=pltpu.CompilerParams(vmem_limit_bytes=FINE_VMEM),
        cost_estimate=pl.CostEstimate(
            flops=6_000_000_000, bytes_accessed=8_000_000, transcendentals=0
        ),
        name="fine",
    )(where, summed0, head, vector[None, :], tile_slot, *filters)


def gather_filters(filters, phase_id, held, phases, dp_count):
    axes = ("phase", "dp")
    chips = dp_count // 2

    def move(value, to):
        route = []
        for p in range(phases):
            for z in range(chips):
                for c in range(2):
                    q, y, d = to(p, z, c)
                    route.append((p * dp_count + 2 * z + c, q * dp_count + 2 * y + d))
        return lax.ppermute(value, axes, route)

    def across(value, bit):
        return move(value, lambda p, z, c: (p, z ^ bit, c))

    def first(value):
        return move(value, lambda p, z, c: (p ^ (1 + c), z, c))

    def second(value):
        return move(value, lambda p, z, c: (p ^ (2 - c), z, c))

    def swap(value):
        return move(value, lambda p, z, c: (p, z, c ^ 1))

    levels, convs, rows, channels = filters.shape
    part = convs * rows // phases
    quarters = filters.reshape(levels, phases, part, channels)
    swapped = swap(filters)
    gathered = []
    for n, group in enumerate(GROUPS):
        if n == 0:
            source, chosen = quarters, phase_id
        else:
            source, chosen = filters, held
        own = lax.dynamic_slice(
            source, (group[0], chosen, 0, 0), (len(group), 1) + source.shape[2:]
        )[:, 0]
        far = across(own, 2)
        near = across(own, 1)
        column = stack([far, near, across(far, 1)])
        one = first(column)
        pieces = [column, one]
        if n == 0:
            pieces += [second(column), second(one)]
        gathered.append(pieces + [swap(v) for v in pieces])
    return [filters, swapped], gathered


def by_permutes(phases, dp_count):
    return phases == 4 and dp_count == 8


def per_device(
    phases,
    dp_count,
    tap_tokens,
    project_weight,
    expand_four,
    expand_two,
    shrink_weight,
    refine_filters,
    head_matrix,
    head_vector,
    tile_slot,
):
    plan = Plan(phases, project_weight.shape[2])
    phase_id = lax.axis_index("phase")
    dp_id = lax.axis_index("dp")
    held = (phase_id >> (dp_id & 1)) & 1
    where = jnp.stack([phase_id, dp_id & 1, dp_id >> 1]).astype(jnp.int32)
    if by_permutes(phases, dp_count):
        base, gathered = gather_filters(refine_filters, phase_id, held, phases, dp_count)
        upper, medium, finer = (base + pieces for pieces in gathered)
    else:
        upper = medium = finer = [lax.all_gather(refine_filters, "dp", axis=2, tiled=True)]
    sent = project(plan, phases, where, tap_tokens, project_weight, shrink_weight)
    arrived = [sent[0]]
    for k in range(1, phases):
        arrived.append(lax.ppermute(sent[k], "phase", [(s, s ^ k) for s in range(phases)]))
    mine = stack(arrived)
    other = lax.ppermute(mine, "dp", [(d, d ^ 1) for d in range(dp_count)])
    summed1, patch0 = coarse(plan, where, mine, other, expand_two, upper)
    summed0 = middle(plan, where, summed1, patch0, expand_four, medium)
    partial = fine(plan, dp_count, where, summed0, head_matrix, head_vector, tile_slot, finer)
    portions = lax.all_to_all(partial, "dp", split_axis=0, concat_axis=0, tiled=True)
    return portions.sum(axis=0)


def solution(mesh):
    in_specs = (
        P("phase", "dp", None),
        P("phase", None, None),
        P(),
        P(),
        P(),
        P(None, None, "dp", None),
        P(),
        P(),
        P(),
    )
    out_specs = P(("phase", "dp"), None)
    phases, dp_count = mesh.shape["phase"], mesh.shape["dp"]

    def body(*args):
        return per_device(phases, dp_count, *args)

    return jax.shard_map(
        body, mesh=mesh, in_specs=in_specs, out_specs=out_specs, check_vma=False
    )
```

```python
import functools

import jax
import jax.numpy as jnp
from jax import lax
from jax.experimental import pallas as pl
from jax.experimental.pallas import tpu as pltpu
from jax.sharding import PartitionSpec as P

G = 32
TILES_DEV = 8
SLOT_DEV = 6
LEVELS = 4
F32 = jnp.float32
BF16 = jnp.bfloat16
STACK_VMEM = 4 * 1024 * 1024
PROJECT_VMEM = 60 * 1024 * 1024
PROJECT_STEPS = 8
COARSE_VMEM = 12 * 1024 * 1024
MIDDLE_VMEM = 20 * 1024 * 1024
FINE_VMEM = 24 * 1024 * 1024


LANES = 128


def take(ref, *at):
    return jnp.concatenate([ref[(i,) + at] for i in range(ref.shape[0])], axis=-1)


def put(ref, value, *at):
    for i in range(ref.shape[0]):
        ref[(i,) + at] = value[..., i * LANES : (i + 1) * LANES]


def dot(lhs, rhs):
    return jnp.dot(lhs, rhs, preferred_element_type=F32)


CHIP_ORDER = (2, 1, 3)
GROUPS = ((2, 3), (1,), (0,))


class Plan:
    def __init__(self, phases, channels):
        self.ch = channels
        self.half = G // 2
        self.block = G // phases
        self.sent = 2 * self.block
        self.rows1 = 3 * G // 4
        self.cols1 = self.block + self.block // 2
        self.cols0 = self.block + 2
        self.conv_cols = 4 * self.block + 4
        self.conv_rows = 4 * self.half + 16

    def slot_of(self, level):
        return next(g.index(level) for g in GROUPS if level in g)

    def sent_start(self, s):
        return jnp.clip(s * self.block - self.block // 2, 0, G - self.sent)

    def start1(self, s):
        return jnp.clip(s * self.block - self.block // 4, 0, G - self.cols1)

    def start0(self, s):
        return jnp.clip(s * self.block - 1, 0, G - self.cols0)


def project_kernel(plan, phases, where, tokens_hbm, weight_hbm, shrink_hbm, *refs):
    outs = refs[:phases]
    acc_lo, acc_hi, tokens, weight, shrink, sems, shrink_sem = refs[phases:]
    lanes = acc_lo.shape[1]
    depth = tokens.shape[1]
    size = depth // PROJECT_STEPS
    copies = []
    for i in range(PROJECT_STEPS):
        at = pl.ds(i * size, size)
        pair = (
            pltpu.make_async_copy(weight_hbm.at[0, at], weight.at[at], sems.at[0, i]),
            pltpu.make_async_copy(tokens_hbm.at[0, :, at], tokens.at[:, at], sems.at[1, i]),
        )
        for copy in pair:
            copy.start()
        copies.append(pair)
    shrink_copy = pltpu.make_async_copy(shrink_hbm, shrink, shrink_sem)
    shrink_copy.start()
    for i, pair in enumerate(copies):
        for copy in pair:
            copy.wait()
        at = slice(i * size, (i + 1) * size)
        part = dot(tokens[:, at], weight[at, :])
        if i == 0:
            acc_lo[...] = part[:, :lanes]
            acc_hi[...] = part[:, lanes:]
        else:
            acc_lo[...] += part[:, :lanes]
            acc_hi[...] += part[:, lanes:]
    shrink_copy.wait()
    phase = where[0]

    def column(start, size, stride):
        where_rows = pl.ds(start, size, stride=stride)
        return jnp.concatenate([acc_lo[where_rows, :], acc_hi[where_rows, :]], axis=1)

    @pl.when(phase < LEVELS - 1)
    def _():
        for k in range(phases):
            start = plan.sent_start(phase ^ k)
            for j in range(plan.sent):
                outs[k][j * plan.half : (j + 1) * plan.half, :] = column(
                    start + j, plan.half, G
                ).astype(BF16)

    @pl.when(phase == LEVELS - 1)
    def _():
        total = jnp.zeros((plan.half * plan.half // 2, plan.ch), F32)
        for a in range(2):
            for b in range(2):
                tall = jnp.concatenate(
                    [column(a * G + 2 * j + b, plan.half // 2, 2 * G) for j in range(G // 2)],
                    axis=0,
                )
                total += dot(
                    tall.astype(BF16), shrink[(2 * a + b) * plan.ch : (2 * a + b + 1) * plan.ch, :]
                )
        for k in range(phases):
            outs[k][: total.shape[0], :] = total.astype(BF16)
            outs[k][total.shape[0] :, :] = jnp.zeros(
                (outs[k].shape[0] - total.shape[0], plan.ch), BF16
            )


def project(plan, phases, where, tokens, weight, shrink):
    rows, depth = tokens.shape[1:]
    pixels = plan.sent * plan.half
    hbm = pl.BlockSpec(memory_space=pltpu.HBM)
    out = jax.ShapeDtypeStruct((pixels, plan.ch), BF16)
    vmem = pl.BlockSpec(memory_space=pltpu.VMEM)
    return pl.pallas_call(
        functools.partial(project_kernel, plan, phases),
        in_specs=[pl.BlockSpec(memory_space=pltpu.SMEM), hbm, hbm, hbm],
        out_specs=[vmem] * phases,
        scratch_shapes=[pltpu.VMEM((rows, plan.ch // 2), F32)] * 2
        + [
            pltpu.VMEM((rows, depth), BF16),
            pltpu.VMEM((depth, plan.ch), BF16),
            pltpu.VMEM(shrink.shape, BF16),
            pltpu.SemaphoreType.DMA((2, PROJECT_STEPS)),
            pltpu.SemaphoreType.DMA,
        ],
        out_shape=[out] * phases,
        compiler_params=pltpu.CompilerParams(vmem_limit_bytes=PROJECT_VMEM),
        cost_estimate=pl.CostEstimate(
            flops=2 * rows * depth * plan.ch,
            bytes_accessed=2 * depth * (rows + plan.ch),
            transcendentals=0,
        ),
        name="project",
    )(where, tokens, weight, shrink)


def stack_kernel(*refs):
    for i, ref in enumerate(refs[:-1]):
        refs[-1][i] = ref[...]


def stack(values):
    vmem = pl.BlockSpec(memory_space=pltpu.VMEM)
    size = len(values) * values[0].size * values[0].dtype.itemsize
    return pl.pallas_call(
        stack_kernel,
        out_shape=jax.ShapeDtypeStruct((len(values),) + values[0].shape, values[0].dtype),
        in_specs=[vmem] * len(values),
        out_specs=vmem,
        compiler_params=pltpu.CompilerParams(vmem_limit_bytes=STACK_VMEM),
        cost_estimate=pl.CostEstimate(flops=0, bytes_accessed=2 * size, transcendentals=0),
        name="stack",
    )(*values)


def put_shifted(shifted, col, value):
    count, rows, _ = value.shape
    value = jnp.maximum(value, 0.0)
    at = lax.broadcasted_iota(jnp.int32, value.shape, 1)
    above = jnp.where(at == 0, 0.0, pltpu.roll(value, 1, 1))
    below = jnp.where(at == rows - 1, 0.0, pltpu.roll(value, rows - 1, 1))
    for p, moved in enumerate((above, value, below)):
        shifted[p, pl.ds(col + 1, count)] = moved.astype(BF16)


def clear_edges(shifted):
    shape = shifted.shape
    zeros = jnp.zeros((shape[0], 1) + shape[2:], BF16)
    shifted[:, 0:1] = zeros
    shifted[:, shape[1] - 1 : shape[1]] = zeros


def conv_block(shifted, weight, col, count, rows):
    channels = shifted.shape[3]
    start, size = rows
    patches = [
        shifted[p, pl.ds(col + q, count), pl.ds(start, size), :].reshape(count * size, channels)
        for p in range(3)
        for q in range(3)
    ]
    return dot(jnp.concatenate(patches, axis=1), weight[...]).reshape(count, size, -1)


def loop(count, body):
    lax.fori_loop(0, count, lambda i, c: (body(i), c)[1], 0)


def steps(count, body):
    for i in range(count):
        body(i)


def refine(source, wait, weights, first, second, chunk, out_col, out_count, out_chunk, emit):
    cols, rows = first.shape[1] - 2, first.shape[2]
    clear_edges(first)
    clear_edges(second)
    steps(cols // chunk, lambda i: put_shifted(first, i * chunk, source(i * chunk, chunk)))

    wait(0)

    def inner(i):
        put_shifted(second, i * chunk, conv_block(first, weights.at[0], i * chunk, chunk, (0, rows)))

    steps(cols // chunk, inner)

    wait(1)

    def outer(i):
        col = out_col + i * out_chunk
        branch = conv_block(second, weights.at[1], col, out_chunk, (0, rows))
        emit(i * out_chunk, source(col, out_chunk) + branch)

    steps(out_count // out_chunk, outer)


def start_filters(filters, level, weights, sems):
    if len(filters) == 1:
        for m in range(2):
            pltpu.make_async_copy(filters[0].at[level, m], weights.at[m], sems.at[m]).start()


def wait_filters(filters, weights, sems, m):
    if len(filters) == 1:
        pltpu.make_async_copy(filters[0].at[0, m], weights.at[m], sems.at[m]).wait()


def lay_filters(plan, where, filters, level, weights):
    if len(filters) == 1:
        return
    phase, side, chip = where[0], where[1], where[2]
    own, swapped = filters[:2]
    rows = own.shape[2]
    part = rows // 2
    slot = plan.slot_of(level)
    for ref, core in ((own, side), (swapped, 1 - side)):
        at = pl.ds(pl.multiple_of((2 * chip + core) * rows, 16), rows)
        for m in range(2):
            weights[m, at, :] = ref[level, m]
    if len(filters) == 6:
        for refs, core in ((filters[2:4], side), (filters[4:6], 1 - side)):
            held = (phase >> core) % 2
            for ref, m in zip(refs, (held, 1 - held)):
                for i, away in enumerate(CHIP_ORDER):
                    start = (2 * (chip ^ away) + core) * rows
                    weights[m, pl.ds(pl.multiple_of(start, 16), rows), :] = ref[i, slot]
        return
    for refs, core in ((filters[2:6], side), (filters[6:10], 1 - side)):
        for ref, moved in zip(refs, (0, 1 + core, 2 - core, 3)):
            quarter = phase ^ moved
            for i, away in enumerate(CHIP_ORDER):
                start = (2 * (chip ^ away) + core) * rows + (quarter % 2) * part
                at = pl.ds(pl.multiple_of(start, 16), part)
                weights[quarter // 2, at, :] = ref[i, slot]


def filter_specs(filters):
    space = pl.ANY if len(filters) == 1 else pltpu.VMEM
    return [pl.BlockSpec(memory_space=space)] * len(filters)


def load_patches(plan, patch, mine, other, k, side):
    for ref, at in ((mine, side), (other, 1 - side)):
        patch[:, pl.ds(pl.multiple_of(at * plan.half, plan.half), plan.half), :] = (
            ref[k].astype(F32).reshape(plan.sent, plan.half, plan.ch)
        )


def rounded(value):
    return value.astype(BF16).astype(F32)


COARSE_SCRATCH = 14


def coarse_kernel(plan, where, mine, other, expand_two, *refs):
    count = len(refs) - COARSE_SCRATCH
    filters = refs[:count]
    (
        summed1,
        patch0,
        weight3,
        weight2,
        sems,
        patch,
        map3,
        joined3,
        map2,
        joined2,
        first3,
        second3,
        first2,
        second2,
    ) = refs[count:]
    ch = plan.ch
    phase, side = where[0], where[1]
    for level, weights in ((3, weight3), (2, weight2)):
        start_filters(filters, level, weights, sems.at[level])
        lay_filters(plan, where, filters, level, weights)

    row1 = pl.multiple_of(side * (G - plan.rows1), 8)
    load_patches(plan, patch, mine, other, phase, side)
    off = plan.start0(phase) - plan.sent_start(phase)
    tall = patch[pl.ds(off, plan.cols0), pl.ds(row1, plan.rows1), :]
    patch0[...] = tall.reshape(patch0.shape).astype(BF16)

    size3 = G // 2
    quarter = plan.half // 2
    k3 = phase ^ 3
    for ref, at in ((mine, side), (other, 1 - side)):
        map3[:, pl.ds(pl.multiple_of(at * quarter, quarter), quarter), :] = (
            ref[k3, : size3 * quarter, :].astype(F32).reshape(size3, quarter, ch)
        )

    def keep3(col, value):
        joined3[pl.ds(col, value.shape[0])] = rounded(value)

    refine(
        lambda col, n: map3[pl.ds(col, n)],
        lambda m: wait_filters(filters, weight3, sems.at[3], m),
        weight3,
        first3,
        second3,
        size3,
        0,
        size3,
        size3,
        keep3,
    )

    load_patches(plan, patch, mine, other, phase ^ 2, side)
    from3 = plan.sent_start(phase) // 2
    tall = joined3[pl.ds(from3, plan.sent // 2)]
    for b in range(2):
        for a in range(2):
            put(map2, tall, slice(None), b, pl.ds(a, size3, stride=2), slice(None))
    for j in range(plan.sent):
        at = (j // 2, j % 2)
        put(map2, take(map2, *at) + patch[j], *at)

    def source2(col, n):
        return take(map2, pl.ds(col // 2, n // 2)).reshape(n, G, ch)

    def keep2(col, value):
        joined2[pl.ds(col, value.shape[0])] = rounded(value)

    refine(
        source2,
        lambda m: wait_filters(filters, weight2, sems.at[2], m),
        weight2,
        first2,
        second2,
        plan.sent,
        0,
        plan.sent,
        plan.sent,
        keep2,
    )

    load_patches(plan, patch, mine, other, phase ^ 1, side)
    off1 = plan.start1(phase) - plan.sent_start(phase)
    tall = patch[pl.ds(off1, plan.cols1), pl.ds(row1, plan.rows1), :]
    lhs = tall.reshape(plan.cols1 * plan.rows1, ch).astype(BF16)
    below = joined2[pl.ds(off1, plan.cols1), pl.ds(row1, plan.rows1), :]
    for a in range(2):
        for b in range(2):
            n = 2 * a + b
            grown = dot(lhs, expand_two[:, n * ch : (n + 1) * ch])
            put(
                summed1,
                grown.reshape(plan.cols1, plan.rows1, ch) + below,
                slice(None),
                b,
                pl.ds(a, plan.rows1, stride=2),
                slice(None),
            )


def shifted_maps(cols, rows, ch):
    return [pltpu.VMEM((3, cols + 2, rows, ch), BF16)] * 2


def coarse(plan, where, mine, other, expand_two, filters):
    ch = plan.ch
    vmem = pl.BlockSpec(memory_space=pltpu.VMEM)
    weights = pltpu.VMEM((2, 9 * ch, ch), BF16)
    size3 = G // 2
    slabs = ch // LANES
    return pl.pallas_call(
        functools.partial(coarse_kernel, plan),
        out_shape=[
            jax.ShapeDtypeStruct((slabs, plan.cols1, 2, 2 * plan.rows1, LANES), F32),
            jax.ShapeDtypeStruct((plan.cols0 * plan.rows1, ch), BF16),
        ],
        in_specs=[pl.BlockSpec(memory_space=pltpu.SMEM), vmem, vmem, vmem]
        + filter_specs(filters),
        out_specs=[vmem, vmem],
        scratch_shapes=[
            weights,
            weights,
            pltpu.SemaphoreType.DMA((LEVELS, 2)),
            pltpu.VMEM((plan.sent, G, ch), F32),
            pltpu.VMEM((size3, size3, ch), F32),
            pltpu.VMEM((size3, size3, ch), F32),
            pltpu.VMEM((slabs, plan.sent // 2, 2, G, LANES), F32),
            pltpu.VMEM((plan.sent, G, ch), F32),
        ]
        + shifted_maps(size3, size3, ch)
        + shifted_maps(plan.sent, G, ch),
        compiler_params=pltpu.CompilerParams(vmem_limit_bytes=COARSE_VMEM),
        cost_estimate=pl.CostEstimate(
            flops=2_000_000_000, bytes_accessed=8_000_000, transcendentals=0
        ),
        name="coarse",
    )(where, mine, other, expand_two, *filters)


MIDDLE_SCRATCH = 6


def middle_kernel(plan, where, summed1, patch0, expand_four, *refs):
    count = len(refs) - MIDDLE_SCRATCH
    filters = refs[:count]
    summed0, weight1, sems, joined1, first1, second1 = refs[count:]
    ch = plan.ch
    phase = where[0]
    start_filters(filters, 1, weight1, sems)
    lay_filters(plan, where, filters, 1, weight1)

    off0 = 2 * (plan.start0(phase) - plan.start1(phase))

    def source1(col, n):
        return take(summed1, pl.ds(col // 2, n // 2)).reshape(n, 2 * plan.rows1, ch)

    def keep1(col, value):
        value = rounded(value)
        put(
            joined1,
            value.reshape(value.shape[0] // 2, 2, 2 * plan.rows1, ch),
            pl.ds(col // 2, value.shape[0] // 2),
        )

    refine(
        source1,
        lambda m: wait_filters(filters, weight1, sems, m),
        weight1,
        first1,
        second1,
        plan.cols1,
        off0,
        2 * plan.cols0,
        plan.cols0,
        keep1,
    )

    for a in range(4):
        for b in range(4):
            n = 4 * a + b
            grown = dot(patch0[...], expand_four[:, n * ch : (n + 1) * ch])
            below = take(
                joined1, slice(None), b // 2, pl.ds(a // 2, plan.rows1, stride=2), slice(None)
            )
            put(
                summed0,
                grown.reshape(plan.cols0, plan.rows1, ch) + below,
                slice(None),
                b,
                pl.ds(a, plan.rows1, stride=4),
                slice(None),
            )


def middle(plan, where, summed1, patch0, expand_four, filters):
    ch = plan.ch
    vmem = pl.BlockSpec(memory_space=pltpu.VMEM)
    slabs = ch // LANES
    return pl.pallas_call(
        functools.partial(middle_kernel, plan),
        out_shape=jax.ShapeDtypeStruct((slabs, plan.cols0, 4, 4 * plan.rows1, LANES), F32),
        in_specs=[pl.BlockSpec(memory_space=pltpu.SMEM)] + [vmem] * 3 + filter_specs(filters),
        out_specs=vmem,
        scratch_shapes=[
            pltpu.VMEM((2, 9 * ch, ch), BF16),
            pltpu.SemaphoreType.DMA((2,)),
            pltpu.VMEM((slabs, plan.cols0, 2, 2 * plan.rows1, LANES), F32),
        ]
        + shifted_maps(2 * plan.cols1, 2 * plan.rows1, ch),
        compiler_params=pltpu.CompilerParams(vmem_limit_bytes=MIDDLE_VMEM),
        cost_estimate=pl.CostEstimate(
            flops=3_000_000_000, bytes_accessed=6_000_000, transcendentals=0
        ),
        name="middle",
    )(where, summed1, patch0, expand_four, *filters)


FINE_SCRATCH = 6


def fine_kernel(plan, dp_count, outputs, where, map0, head, vector, tile_slot, *refs):
    count = len(refs) - FINE_SCRATCH - outputs
    filters, portions = refs[:count], refs[count : count + outputs]
    weight0, sems, first, second, by_col, by_row = refs[count + outputs :]
    ch = plan.ch
    phase, side = where[0], where[1]
    start_filters(filters, 0, weight0, sems)
    lay_filters(plan, where, filters, 0, weight0)
    cols, rows, own_rows = plan.conv_cols, plan.conv_rows, 4 * plan.half
    own0 = 4 * (phase * plan.block - plan.start0(phase))
    conv0 = jnp.clip(own0 - 2, 0, 4 * plan.cols0 - cols)
    own = own0 - conv0
    row = pl.multiple_of(side * 16, 16)
    pairs = map0.reshape(ch // LANES, 2 * plan.cols0, 2, 4 * plan.rows1, LANES)
    chunk = cols // 2

    def source0(col, n, start, size):
        at = (pl.ds((conv0 + col) // 2, n // 2), slice(None), pl.ds(start, size), slice(None))
        return take(pairs, *at).reshape(n, size, ch)

    clear_edges(first)
    clear_edges(second)
    loop(9, lambda i: put_shifted(first, i * 4, source0(i * 4, 4, row, rows)))
    wait_filters(filters, weight0, sems, 0)

    def inner(i):
        put_shifted(
            second, i * chunk, conv_block(first, weight0.at[0], i * chunk, chunk, (0, rows))
        )

    loop(cols // chunk, inner)
    wait_filters(filters, weight0, sems, 1)
    half_cols = 2 * plan.block
    hidden_size = head.shape[1]
    scale = jnp.broadcast_to(vector[...], (hidden_size, hidden_size)).T[:, :1]

    def outer(i):
        col = own + i * half_cols
        branch = conv_block(second, weight0.at[1], col, half_cols, (row, own_rows))
        summed = source0(col, half_cols, pl.multiple_of(2 * row, 16), own_rows)
        joined = (summed + branch).astype(BF16)
        hidden = lax.dot_general(
            head[...],
            joined.reshape(half_cols * own_rows, ch),
            (((0,), (1,)), ((), ())),
            preferred_element_type=F32,
        )
        depth = (jnp.maximum(hidden, 0.0) * scale).sum(axis=0, keepdims=True)
        for j in range(half_cols):
            by_col[pl.ds(i * half_cols + j, 1), :own_rows] = depth[
                :, j * own_rows : (j + 1) * own_rows
            ]

    loop(2, outer)

    by_row[...] = by_col[...].T
    tile_rows = own_rows // TILES_DEV
    tiles = jnp.concatenate(
        [
            by_row[pl.ds(i, TILES_DEV, stride=tile_rows), :][:, : 2 * half_cols]
            for i in range(tile_rows)
        ],
        axis=1,
    )

    chip = where[2]
    targets = tile_slot[2 * chip + side, pl.ds(phase, 1), :]
    slot = lax.broadcasted_iota(jnp.int32, (SLOT_DEV, TILES_DEV), 0)

    def tile_sums(d):
        chosen = (slot + (phase * dp_count + d) * SLOT_DEV == targets).astype(F32)
        total = chosen[:, 0:1] * tiles[0:1]
        for j in range(1, TILES_DEV):
            total += chosen[:, j : j + 1] * tiles[j : j + 1]
        return total

    if outputs == 1:
        for d in range(dp_count):
            portions[0][d] = tile_sums(d)
    else:
        for i in range(dp_count // 2):
            for ref, core in zip(portions, (side, 1 - side)):
                ref[i] = tile_sums(2 * (chip ^ i) + core)


def fine(plan, dp_count, outputs, where, summed0, head, vector, tile_slot, filters):
    ch = plan.ch
    vmem = pl.BlockSpec(memory_space=pltpu.VMEM)
    pixels = 16 * plan.block * plan.half // TILES_DEV
    return pl.pallas_call(
        functools.partial(fine_kernel, plan, dp_count, outputs),
        out_shape=[jax.ShapeDtypeStruct((dp_count // outputs, SLOT_DEV, pixels), F32)] * outputs,
        in_specs=[pl.BlockSpec(memory_space=pltpu.SMEM)] + [vmem] * 4 + filter_specs(filters),
        out_specs=[vmem] * outputs,
        scratch_shapes=[pltpu.VMEM((2, 9 * ch, ch), BF16), pltpu.SemaphoreType.DMA((2,))]
        + shifted_maps(plan.conv_cols, plan.conv_rows, ch)
        + [pltpu.VMEM((LANES, LANES), F32)] * 2,
        compiler_params=pltpu.CompilerParams(vmem_limit_bytes=FINE_VMEM),
        cost_estimate=pl.CostEstimate(
            flops=6_000_000_000, bytes_accessed=8_000_000, transcendentals=0
        ),
        name="fine",
    )(where, summed0, head, vector[None, :], tile_slot, *filters)


def gather_filters(filters, phase_id, held, phases, dp_count):
    axes = ("phase", "dp")
    chips = dp_count // 2

    def move(value, to):
        route = []
        for p in range(phases):
            for z in range(chips):
                for c in range(2):
                    q, y, d = to(p, z, c)
                    route.append((p * dp_count + 2 * z + c, q * dp_count + 2 * y + d))
        return lax.ppermute(value, axes, route)

    def across(value, bit):
        return move(value, lambda p, z, c: (p, z ^ bit, c))

    def first(value):
        return move(value, lambda p, z, c: (p ^ (1 + c), z, c))

    def second(value):
        return move(value, lambda p, z, c: (p ^ (2 - c), z, c))

    def swap(value):
        return move(value, lambda p, z, c: (p, z, c ^ 1))

    levels, convs, rows, channels = filters.shape
    part = convs * rows // phases
    quarters = filters.reshape(levels, phases, part, channels)
    swapped = swap(filters)
    gathered = []
    for n, group in enumerate(GROUPS):
        if n == 0:
            source, chosen = quarters, phase_id
        else:
            source, chosen = filters, held
        own = lax.dynamic_slice(
            source, (group[0], chosen, 0, 0), (len(group), 1) + source.shape[2:]
        )[:, 0]
        far = across(own, 2)
        near = across(own, 1)
        column = stack([far, near, across(far, 1)])
        one = first(column)
        pieces = [column, one]
        if n == 0:
            pieces += [second(column), second(one)]
        gathered.append(pieces + [swap(v) for v in pieces])
    return [filters, swapped], gathered


def merge_kernel(kept, given, *outs):
    for i, out in enumerate(outs):
        out[...] = kept[i] + given[i]


def gather_tiles(kept, given, dp_count):
    def move(value, bits):
        return lax.ppermute(value, "dp", [(d, d ^ bits) for d in range(dp_count)])

    vmem = pl.BlockSpec(memory_space=pltpu.VMEM)
    chips = dp_count // 2
    sums = pl.pallas_call(
        merge_kernel,
        out_shape=[jax.ShapeDtypeStruct(kept.shape[1:], F32)] * chips,
        in_specs=[vmem] * 2,
        out_specs=[vmem] * chips,
        compiler_params=pltpu.CompilerParams(vmem_limit_bytes=STACK_VMEM),
        cost_estimate=pl.CostEstimate(
            flops=kept.size, bytes_accessed=12 * kept.size, transcendentals=0
        ),
        name="merge",
    )(kept, move(given, 1))
    total = sums[0]
    for i in CHIP_ORDER:
        total += move(sums[i], 2 * i)
    return total


def by_permutes(phases, dp_count):
    return phases == 4 and dp_count == 8


def per_device(
    phases,
    dp_count,
    tap_tokens,
    project_weight,
    expand_four,
    expand_two,
    shrink_weight,
    refine_filters,
    head_matrix,
    head_vector,
    tile_slot,
):
    plan = Plan(phases, project_weight.shape[2])
    phase_id = lax.axis_index("phase")
    dp_id = lax.axis_index("dp")
    held = (phase_id >> (dp_id & 1)) & 1
    where = jnp.stack([phase_id, dp_id & 1, dp_id >> 1]).astype(jnp.int32)
    if by_permutes(phases, dp_count):
        base, gathered = gather_filters(refine_filters, phase_id, held, phases, dp_count)
        upper, medium, finer = (base + pieces for pieces in gathered)
    else:
        upper = medium = finer = [lax.all_gather(refine_filters, "dp", axis=2, tiled=True)]
    sent = project(plan, phases, where, tap_tokens, project_weight, shrink_weight)
    arrived = [sent[0]]
    for k in range(1, phases):
        arrived.append(lax.ppermute(sent[k], "phase", [(s, s ^ k) for s in range(phases)]))
    mine = stack(arrived)
    other = lax.ppermute(mine, "dp", [(d, d ^ 1) for d in range(dp_count)])
    summed1, patch0 = coarse(plan, where, mine, other, expand_two, upper)
    summed0 = middle(plan, where, summed1, patch0, expand_four, medium)
    outputs = 2 if by_permutes(phases, dp_count) else 1
    portions = fine(
        plan, dp_count, outputs, where, summed0, head_matrix, head_vector, tile_slot, finer
    )
    if outputs == 2:
        return gather_tiles(*portions, dp_count)
    return lax.all_to_all(portions[0], "dp", split_axis=0, concat_axis=0, tiled=True).sum(axis=0)


def solution(mesh):
    in_specs = (
        P("phase", "dp", None),
        P("phase", None, None),
        P(),
        P(),
        P(),
        P(None, None, "dp", None),
        P(),
        P(),
        P(),
    )
    out_specs = P(("phase", "dp"), None)
    phases, dp_count = mesh.shape["phase"], mesh.shape["dp"]

    def body(*args):
        return per_device(phases, dp_count, *args)

    return jax.shard_map(
        body, mesh=mesh, in_specs=in_specs, out_specs=out_specs, check_vma=False
    )
```
